32 devices in a mesh: rows: 8 (over z, x), chan: 4 (over y, core).
Axes of the slice: x: 2, y: 2, z: 4, core: 2. Of those that a mesh axis runs over, the one named last changes fastest.
Arguments:
- tokens: bfloat16 [8192, 1024], P(('rows', 'chan')), may hold values from -6 to 6
- cotangent: bfloat16 [8192, 1024], P(('rows', 'chan')), may hold values from -6 to 6
- segments: int32 [8, 1024], P('rows'), may hold values from 0 to 3, never falling along the last dimension, each value on 1 to 512 neighbouring positions
- w_query: bfloat16 [1024, 1024], P(None, 'chan'), may hold values from -0.25 to 0.25
- w_key: bfloat16 [1024, 1024], P(None, 'chan'), may hold values from -0.1875 to 0.1875
- w_value: bfloat16 [1024, 1024], P(None, 'chan'), may hold values from -0.1875 to 0.1875
- w_out: bfloat16 [1024, 1024], P(None, 'chan'), may hold values from -0.75 to 0.75
- w_up: bfloat16 [1024, 4096], P(None, 'chan'), may hold values from -0.1875 to 0.1875
- up_bias: float32 [4096], P('chan'), may hold values from -3 to 3
- w_down: bfloat16 [1024, 4096], P(None, 'chan'), may hold values from -0.09375 to 0.09375
- down_bias: float32 [1024], replicated, may hold values from -3 to 3
- norm1_gain: float32 [1024], replicated, may hold values from 0.5 to 1.5
- norm1_bias: float32 [1024], replicated, may hold values from -2 to 2
- norm2_gain: float32 [1024], replicated, may hold values from 0.5 to 1.5
- norm2_bias: float32 [1024], replicated, may hold values from -2 to 2
- decay_rates: float32 [1024, 16], P('chan'), may hold values from 0.00048828125 to 0.03125
- input_mix: float32 [1024, 16], P('chan'), may hold values from -4 to 4
- key_mix: float32 [1024, 16], P('chan'), may hold values from -1.5 to 1.5
- value_mix: float32 [1024, 16], P('chan'), may hold values from -1.5 to 1.5
- key_skip: float32 [1024], P('chan'), may hold values from -3 to 3
- value_skip: float32 [1024], P('chan'), may hold values from -3 to 3
Outputs:
- output: bfloat16 [8192, 1024], P(('rows', 'chan'))
- grad_tokens: bfloat16 [8192, 1024], P(('rows', 'chan'))
- grad_w_query: float32 [1024, 1024], P('rows', 'chan')
- grad_w_key: float32 [1024, 1024], P('rows', 'chan')
- grad_w_value: float32 [1024, 1024], P('rows', 'chan')
- grad_w_out: float32 [1024, 1024], P('rows', 'chan')
- grad_w_up: float32 [1024, 4096], P('rows', 'chan')
- grad_up_bias: float32 [4096], replicated
- grad_w_down: float32 [1024, 4096], P('rows', 'chan')
- grad_down_bias: float32 [1024], replicated
- grad_norm1_gain: float32 [1024], replicated
- grad_norm1_bias: float32 [1024], replicated
- grad_norm2_gain: float32 [1024], replicated
- grad_norm2_bias: float32 [1024], replicated
- grad_decay_rates: float32 [1024, 16], replicated
- grad_input_mix: float32 [1024, 16], replicated
- grad_key_mix: float32 [1024, 16], replicated
- grad_value_mix: float32 [1024, 16], replicated
- grad_key_skip: float32 [1024], replicated
- grad_value_skip: float32 [1024], replicated
The draws below stay inside these ranges and needn't reach their ends.
Inputs may be any that keep to these rules, and one draw needn't show every extreme that they name: `segments`: along a row segment ids never fall; each segment spans 1 to 512 tokens, one exactly that many.
All inputs are finite; a program needn't handle non-finite values.
Results may differ from the reference program's by a relative error of at most 0.014.
The reference program's roundings to bfloat16 on the way count: a program that leaves them out, or rounds other values in their place, can miss the bound.
Values may be sent and summed in bfloat16 or wider, within the bound.
A program may use at most 128 MiB of HBM per device.

```python
import math
import jax
import jax.numpy as jnp
import numpy as np
from jax import lax

D = 1024
HEADS = 8
FF = 4096
NS = 16
CTX = 128
BLK = 512
SQ = 256
LEN = 1024
SEQS = 8
TOKENS = 8192


def block_scale(own_key, extent, cuts, low, top_value):
    level = 1.0
    for position, parts in cuts:
        heights = jax.random.uniform(jax.random.fold_in(jax.random.fold_in(own_key, 6), position), (parts,), jnp.float32, low / len(cuts), top_value / len(cuts))
        level = level * jnp.repeat(jnp.exp(heights), extent[position] // parts).reshape((-1,) + (1,) * (len(extent) - 1 - position))
    return level


def split_up(number_of, total, limit, skew):
    weights = [(1 << 20) // math.isqrt(grade ** skew) + 1 for grade in range(2, number_of + 1)]
    rest, holding = total - limit - (number_of - 1), [1] * (number_of - 1)
    while rest > 0:
        free = [i for i in range(number_of - 1) if holding[i] < limit]
        whole, left = sum([weights[i] for i in free]), rest
        for i in free:
            addition = min(limit - holding[i], max(1, left * weights[i] // whole), rest)
            holding[i] = holding[i] + addition
            rest = rest - addition
    return np.array([limit] + holding)


def uneven(key, amount, total, most, skew):
    if amount == 2:
        one = jax.random.randint(key, (), max(1, total - most), min(most, total - 1) + 1)
        return jnp.stack([one, total - one])
    tallies = jnp.asarray(split_up(amount, total, most, skew), jnp.int32)
    twos = (amount - 1) // 2
    donor, receiver = tallies[1:1 + 2 * twos:2], tallies[2:2 + 2 * twos:2]
    margin = jnp.minimum(donor - 1, most - receiver)
    shifted = jax.random.randint(jax.random.fold_in(key, 1), (twos,), 0, 1 << 20) % (margin + 1)
    tallies = tallies.at[1:1 + 2 * twos:2].set(donor - shifted).at[2:2 + 2 * twos:2].set(receiver + shifted)
    return tallies[jax.random.permutation(jax.random.fold_in(key, 2), amount)]


def normal_values(own_key, dims, scale, most, pieces=(), held_as=jnp.bfloat16):
    level = block_scale(own_key, dims, pieces, -0.22, 0.18) if pieces else 1.0
    values = jax.random.normal(own_key, dims, jnp.float32) * scale * level
    return jnp.minimum(jnp.maximum(values, -most), most).astype(held_as)


def setup_inputs(seed: int = 0) -> dict:
    keys = jax.random.split(jax.random.key(seed), 22)
    tokens = normal_values(keys[0], (TOKENS, D), 1.0, 6.0, ((0, 32),))
    cotangent = normal_values(keys[1], (TOKENS, D), 1.0, 6.0, ((0, 32),))
    segments = jax.vmap(lambda own: jnp.searchsorted(jnp.cumsum(uneven(own, max(4, LEN // 1024), LEN, LEN // 2, 0)), jnp.arange(LEN), side="right"))(jax.random.split(keys[2], SEQS)).reshape((SEQS, LEN)).astype(jnp.int32)
    w_query = normal_values(keys[3], (D, D), (D // 2) ** -0.5, 0.25, ((1, 4),))
    w_key = normal_values(keys[4], (D, D), D ** -0.5, 0.1875, ((1, 4),))
    w_value = normal_values(keys[5], (D, D), D ** -0.5, 0.1875, ((1, 4),))
    w_out = normal_values(keys[6], (D, D), (D // 16) ** -0.5, 0.75, ((1, 4),))
    w_up = normal_values(keys[7], (D, FF), D ** -0.5, 0.1875, ((1, 4),))
    up_bias = normal_values(keys[8], (FF,), 0.5, 3.0, ((0, 4),), jnp.float32)
    w_down = normal_values(keys[9], (D, FF), FF ** -0.5, 0.09375, ((1, 4),))
    down_bias = normal_values(keys[10], (D,), 0.5, 3.0, (), jnp.float32)
    norm1_gain = jnp.clip(1.0 + 0.1 * jax.random.normal(keys[11], (D,), jnp.float32), 0.5, 1.5)
    norm1_bias = normal_values(keys[12], (D,), 0.3, 2.0, (), jnp.float32)
    norm2_gain = jnp.clip(1.0 + 0.1 * jax.random.normal(keys[13], (D,), jnp.float32), 0.5, 1.5)
    norm2_bias = normal_values(keys[14], (D,), 0.3, 2.0, (), jnp.float32)
    decay_rates = jnp.clip(jnp.exp(math.log(0.03125) - 4.158883 * jax.random.uniform(keys[15], (D, NS), jnp.float32) ** block_scale(keys[15], (D, NS), ((0, 4),), -0.2, 0.2)), 0.00048828125, 0.03125)
    input_mix = normal_values(keys[16], (D, NS), 1.0, 4.0, ((0, 4),), jnp.float32)
    key_mix = normal_values(keys[17], (D, NS), NS ** -0.5, 1.5, ((0, 4),), jnp.float32)
    value_mix = normal_values(keys[18], (D, NS), NS ** -0.5, 1.5, ((0, 4),), jnp.float32)
    key_skip = normal_values(keys[19], (D,), 0.5, 3.0, ((0, 4),), jnp.float32)
    value_skip = normal_values(keys[20], (D,), 0.5, 3.0, ((0, 4),), jnp.float32)
    return dict(tokens=tokens, cotangent=cotangent, segments=segments, w_query=w_query, w_key=w_key, w_value=w_value, w_out=w_out, w_up=w_up, up_bias=up_bias, w_down=w_down, down_bias=down_bias, norm1_gain=norm1_gain, norm1_bias=norm1_bias, norm2_gain=norm2_gain, norm2_bias=norm2_bias, decay_rates=decay_rates, input_mix=input_mix, key_mix=key_mix, value_mix=value_mix, key_skip=key_skip, value_skip=value_skip)


@jax.custom_vjp
def low(v):
    return lax.optimization_barrier(v.astype(jnp.bfloat16)).astype(jnp.float32)

@jax.custom_vjp
def low_back(v):
    return v

def low_keep(v):
    return (low(v), None)

def low_pass(kept, grad):
    return (grad,)

def back_keep(v):
    return (v, None)

def back_low(kept, grad):
    return (low(grad),)
low.defvjp(low_keep, low_pass)
low_back.defvjp(back_keep, back_low)

def matmul(left_side, right_side):
    return jnp.dot(left_side, right_side, precision=lax.Precision.HIGHEST)

def matmul_t(left_side, right_side):
    return lax.dot_general(left_side, right_side, (((1,), (1,)), ((), ())), precision=lax.Precision.HIGHEST)

def layer_norm(values, gain, bias):
    centered = values - lax.optimization_barrier(jnp.mean(values, axis=-1, keepdims=True))
    variance = lax.optimization_barrier(jnp.mean(centered * centered, axis=-1, keepdims=True))
    return centered * lax.rsqrt(variance + 1e-05) * gain + bias

def segment_starts(segment_rows):
    row_count, length_all = segment_rows.shape
    previous = jnp.concatenate([segment_rows[:, :1], segment_rows[:, :-1]], axis=1)
    row_first = (jnp.arange(length_all, dtype=jnp.int32) == 0)[None, :]
    return jnp.where(row_first | (segment_rows != previous), 1, 0).astype(jnp.int32).reshape(row_count * length_all)

def ssm_block(previous, block_in, mixers):
    decay_rates, input_mix, key_mix, value_mix, key_skip, value_skip = mixers
    inputs, starts = block_in
    positions = jnp.arange(inputs.shape[0], dtype=jnp.int32)
    last_start = lax.cummax(jnp.where(starts > 0, positions, -1), axis=0)
    offsets = positions.astype(jnp.float32)[:, None, None]
    growth = jnp.exp(offsets * decay_rates)
    input_scale = jnp.sqrt(-jnp.expm1(-2.0 * decay_rates)) * input_mix
    summands = growth * input_scale * inputs[:, :, None]
    running = jnp.cumsum(summands, axis=0)
    before = jnp.take(running, jnp.maximum(last_start - 1, 0).astype(jnp.int32), axis=0)
    before = jnp.where((last_start >= 1)[:, None, None], before, 0.0)
    carried = jnp.where((last_start < 0)[:, None, None], jnp.exp(-(offsets + 1.0) * decay_rates) * previous[None], 0.0)
    states = jnp.exp(-offsets * decay_rates) * (running - before) + carried
    ctx_keys = lax.optimization_barrier(jnp.sum(states * key_mix, axis=2)) + key_skip * inputs
    ctx_values = lax.optimization_barrier(jnp.sum(states * value_mix, axis=2)) + value_skip * inputs
    return (states[-1], (ctx_keys, ctx_values))

def ssm_scan(inputs, starts, mixers):
    token_count, channels = inputs.shape
    state_count = mixers[0].shape[1]
    block_count = token_count // SQ

    def step_fn(previous, block_in):
        return ssm_block(previous, block_in, mixers)
    initial = jnp.zeros((channels, state_count), jnp.float32)
    final_state, (ctx_keys, ctx_values) = lax.scan(jax.checkpoint(step_fn), initial, (inputs.reshape(block_count, SQ, channels), starts.reshape(block_count, SQ)))
    return (ctx_keys.reshape(token_count, channels), ctx_values.reshape(token_count, channels))

def block_mask(query_segment, context_segment):
    positions = jnp.arange(query_segment.shape[0], dtype=jnp.int32)
    own_part = (positions[None, :] <= positions[:, None]) & (query_segment[None, :] == query_segment[:, None])
    ctx_part = context_segment[None, :] == query_segment[:, None]
    return jnp.concatenate([own_part, ctx_part], axis=1)

def split_blocks(values, head_count):
    token_count, columns = values.shape
    return values.reshape(token_count // BLK, BLK, head_count, columns // head_count)

def context_of(blocked):
    padding = jnp.zeros((1, CTX) + blocked.shape[2:], blocked.dtype)
    return jnp.concatenate([padding, blocked[:-1, BLK - CTX:]], axis=0)

def context_segments(flat_segments):
    seg_blocks = flat_segments.reshape(-1, BLK)
    block_count = seg_blocks.shape[0]
    earlier = jnp.concatenate([jnp.full((1, CTX), -1, jnp.int32), seg_blocks[:-1, BLK - CTX:]], axis=0)
    row_first = (jnp.arange(block_count, dtype=jnp.int32) % (LEN // BLK) == 0)[:, None]
    return (seg_blocks, jnp.where(row_first, -1, earlier).astype(jnp.int32))

def block_forward(block_items):
    queries, key_own, key_ctx, value_own, value_ctx, query_segment, context_segment = block_items
    key_all = jnp.concatenate([key_own, key_ctx], axis=0)
    value_all = jnp.concatenate([value_own, value_ctx], axis=0)
    scores = low_back(jnp.einsum('qhd,khd->hqk', queries, key_all, precision=lax.Precision.HIGHEST) * queries.shape[2] ** (-0.5))
    masked = jnp.where(block_mask(query_segment, context_segment)[None], scores, -1e+30)
    attn_probs = low(jnp.exp(masked - jax.nn.logsumexp(masked, axis=2, keepdims=True)))
    return jnp.einsum('hqk,khd->qhd', attn_probs, value_all, precision=lax.Precision.HIGHEST)

def attend_row(queries, keys_own, values_own, ctx_key, ctx_value, flat_segments):
    head_count = queries.shape[1] // (D // HEADS)
    query_segment, context_segment = context_segments(flat_segments)
    block_out = lax.map(jax.checkpoint(block_forward), (split_blocks(queries, head_count), split_blocks(keys_own, head_count), context_of(split_blocks(ctx_key, head_count)), split_blocks(values_own, head_count), context_of(split_blocks(ctx_value, head_count)), query_segment, context_segment))
    return block_out.reshape(queries.shape)

def forward(residual, params, starts, flat_segments):
    w_query, w_key, w_value, w_out, w_up, up_bias, w_down, down_bias, norm1_gain, norm1_bias, norm2_gain, norm2_bias, decay_rates, input_mix, key_mix, value_mix, key_skip, value_skip = params
    first_hidden = low(layer_norm(residual, norm1_gain, norm1_bias))
    queries = low_back(low(matmul(first_hidden, w_query)))
    keyed = low_back(low(matmul(first_hidden, w_key)))
    valued = low_back(low(matmul(first_hidden, w_value)))
    ctx_key, ctx_value = ssm_scan(low_back(first_hidden), starts, (decay_rates, input_mix, key_mix, value_mix, key_skip, value_skip))
    attention = attend_row(queries, keyed, valued, low(ctx_key), low(ctx_value), flat_segments)
    attention = low_back(low(attention))
    second_residual = residual + low_back(matmul(attention, w_out))
    second_hidden = low(layer_norm(second_residual, norm2_gain, norm2_bias))
    preact = low_back(matmul(second_hidden, w_up) + up_bias)
    activated = low(jax.nn.gelu(preact))
    return second_residual + matmul_t(activated, w_down) + down_bias

def reference(tokens, cotangent, segments, w_query, w_key, w_value, w_out, w_up, up_bias, w_down, down_bias, norm1_gain, norm1_bias, norm2_gain, norm2_bias, decay_rates, input_mix, key_mix, value_mix, key_skip, value_skip):
    params = tuple((item.astype(jnp.float32) for item in (w_query, w_key, w_value, w_out, w_up, up_bias, w_down, down_bias, norm1_gain, norm1_bias, norm2_gain, norm2_bias, decay_rates, input_mix, key_mix, value_mix, key_skip, value_skip)))
    residual_rows = tokens.astype(jnp.float32).reshape(SEQS, LEN, D)
    cot_rows = cotangent.astype(jnp.float32).reshape(SEQS, LEN, D)

    def row_step(totals, row_items):
        residual, cot_row, segment_row = row_items
        starts = segment_starts(segment_row[None, :])

        def run_row(values, weights):
            return forward(values, weights, starts, segment_row)
        out_row, pullback = jax.vjp(run_row, residual, params)
        grad_residual, grad_params = pullback(cot_row)
        totals = jax.tree.map(jnp.add, totals, grad_params)
        return (totals, (out_row.astype(jnp.bfloat16), grad_residual.astype(jnp.bfloat16)))
    zero_fill = jax.tree.map(jnp.zeros_like, params)
    grads, (out_rows, grad_rows) = lax.scan(row_step, zero_fill, (residual_rows, cot_rows, segments))
    return (out_rows.reshape(TOKENS, D), grad_rows.reshape(TOKENS, D), grads[0], grads[1], grads[2], grads[3], grads[4], grads[5], grads[6], grads[7], grads[8], grads[9], grads[10], grads[11], grads[12], grads[13], grads[14], grads[15], grads[16], grads[17])
```

```python
import functools

import jax
import jax.numpy as jnp
from jax import lax
from jax.experimental import pallas as pl
from jax.experimental.pallas import tpu as pltpu
from jax.sharding import PartitionSpec as P

HEAD = 128
CTX = 128
BLK = 512
EPS = 1e-05
NEG = -1e30
F32 = jnp.float32
BF16 = jnp.bfloat16
NN = (((1,), (0,)), ((), ()))
NT = (((1,), (1,)), ((), ()))
TN = (((0,), (0,)), ((), ()))


def dot(left, right, dims=NN):
    return lax.dot_general(left, right, dims, preferred_element_type=F32)


def ssm_local(x_ref, mask_col, par_ref, first, count, g, e, keep_ref=None):
    a = par_ref[0]
    row = lax.broadcasted_iota(jnp.int32, (8, 1), 0)

    def step(i, carry):
        g, e = carry
        base = pl.multiple_of(first + i * 8, 8)
        x8 = x_ref[pl.ds(base, 8), :].astype(F32)
        x8 = jnp.where(mask_col(row + base), x8, 0.0)
        for t in range(8):
            e = a * e + g
            g = a * g + x8[t : t + 1, :]
            if keep_ref is not None:
                keep_ref[i * 8 + t] = g
        return (g, e)

    return lax.fori_loop(0, count // 8, step, (g, e))


def ssm_prefix(x_ref, mask_col, par_ref):
    a128, d128 = par_ref[6], par_ref[7]
    zero = jnp.zeros(par_ref.shape[1:], F32)
    parts = (BLK - CTX) // 128
    a = par_ref[0]
    row = lax.broadcasted_iota(jnp.int32, (8, 1), 0)

    def step(i, carry):
        out = []
        for j in range(parts):
            g, e = carry[j]
            base = pl.multiple_of(j * 128 + i * 8, 8)
            x8 = x_ref[pl.ds(base, 8), :].astype(F32)
            x8 = jnp.where(mask_col(row + base), x8, 0.0)
            for t in range(8):
                e = a * e + g
                g = a * g + x8[t : t + 1, :]
            out.append((g, e))
        return tuple(out)

    ends = lax.fori_loop(0, 16, step, tuple((zero, zero) for _ in range(parts)))
    g, e = ends[0]
    for j in range(1, parts):
        e = ends[j][1] + a128 * e + d128 * g
        g = ends[j][0] + a128 * g
    return g, e


def segment_mask(seg_ref):
    segs = seg_ref[...]
    here = segs[:, BLK : BLK + 1]
    first = jnp.sum(jnp.where(segs < here, 1, 0), axis=1, keepdims=True)
    return lambda index: index >= first


def ssm_fwd_kernel(x_ref, seg_ref, par_ref, skip_ref, ck_ref, cv_ref, g_ref):
    mask_col = segment_mask(seg_ref)
    g, e = ssm_prefix(x_ref, mask_col, par_ref)
    a, kb, vb = par_ref[0], par_ref[4], par_ref[5]
    first = BLK - CTX
    row = lax.broadcasted_iota(jnp.int32, (8, 1), 0)

    def step(i, g):
        base = pl.multiple_of(first + i * 8, 8)
        raw = x_ref[pl.ds(base, 8), :].astype(F32)
        x8 = jnp.where(mask_col(row + base), raw, 0.0)
        ks, vs = [], []
        for t in range(8):
            g = a * g + x8[t : t + 1, :]
            ks.append(jnp.sum(g * kb, axis=0, keepdims=True))
            vs.append(jnp.sum(g * vb, axis=0, keepdims=True))
        at = pl.ds(pl.multiple_of(i * 8, 8), 8)
        g_ref[at, :] = jnp.concatenate(ks, axis=0) + skip_ref[0:1, :] * raw
        ck_ref[at, :] = jnp.concatenate(vs, axis=0) + skip_ref[1:2, :] * raw
        return g

    lax.fori_loop(0, CTX // 8, step, g)
    cv_ref[...] = ck_ref[...]
    ck_ref[...] = g_ref[...]


def ssm_bwd_kernel(x_ref, seg_ref, par_ref, skip_ref, gk_ref, gv_ref, gx_ref, gp_ref, gs_ref, keep_ref):
    mask_col = segment_mask(seg_ref)
    g0, e0 = ssm_prefix(x_ref, mask_col, par_ref)
    a, b, km, vm = par_ref[0], par_ref[1], par_ref[2], par_ref[3]
    first = BLK - CTX
    zero = jnp.zeros(par_ref.shape[1:], F32)
    keep_ref[0] = g0
    row = lax.broadcasted_iota(jnp.int32, (8, 1), 0)

    def ahead(i, g):
        base = pl.multiple_of(first + i * 8, 8)
        x8 = jnp.where(mask_col(row + base), x_ref[pl.ds(base, 8), :].astype(F32), 0.0)
        for t in range(8):
            g = a * g + x8[t : t + 1, :]
            keep_ref[i * 8 + t + 1] = g
        return g

    lax.fori_loop(0, CTX // 8, ahead, g0)

    def back(j, carry):
        lam, sk, sv, sx, sg = carry
        i = CTX // 8 - 1 - j
        base = pl.multiple_of(first + i * 8, 8)
        at = pl.ds(pl.multiple_of(i * 8, 8), 8)
        raw = x_ref[pl.ds(base, 8), :].astype(F32)
        inside = mask_col(row + base)
        x8 = jnp.where(inside, raw, 0.0)
        k8 = gk_ref[at, :]
        v8 = gv_ref[at, :]
        outs = [None] * 8
        for t in reversed(range(8)):
            kt, vt, xt = k8[t : t + 1, :], v8[t : t + 1, :], x8[t : t + 1, :]
            lam = a * lam + km * kt + vm * vt
            now = keep_ref[i * 8 + t + 1]
            sk = sk + now * kt
            sv = sv + now * vt
            sx = sx + lam * xt
            sg = sg + lam * keep_ref[i * 8 + t]
            outs[t] = jnp.sum(lam * b, axis=0, keepdims=True)
        gx = jnp.where(inside, jnp.concatenate(outs, axis=0), 0.0)
        gx_ref[pl.ds(base, 8), :] = gx + skip_ref[0:1, :] * k8 + skip_ref[1:2, :] * v8
        return (lam, sk, sv, sx, sg)

    lam, sk, sv, sx, sg = lax.fori_loop(0, CTX // 8, back, (zero,) * 5)
    sx = sx + lam * (a * g0)
    sg = sg + lam * (a * e0)
    gp_ref[0] = sk * b
    gp_ref[1] = sv * b
    gp_ref[2] = sx
    gp_ref[3] = sg

    def tail(j, w):
        i = first // 8 - 1 - j
        base = pl.multiple_of(i * 8, 8)
        outs = [None] * 8
        for t in reversed(range(8)):
            w = a * w
            outs[t] = jnp.sum(w, axis=0, keepdims=True)
        gx_ref[pl.ds(base, 8), :] = jnp.where(
            mask_col(row + base), jnp.concatenate(outs, axis=0), 0.0
        )
        return w

    lax.fori_loop(0, first // 8, tail, lam * b)
    raw = x_ref[first:BLK, :].astype(F32)
    gs_ref[0:1, :] = jnp.sum(gk_ref[...] * raw, axis=0, keepdims=True)
    gs_ref[1:2, :] = jnp.sum(gv_ref[...] * raw, axis=0, keepdims=True)
    gx_ref[BLK:, :] = jnp.zeros((gx_ref.shape[0] - BLK, gx_ref.shape[1]), F32)


def call(kernel, outs, scratch=(), **extra):
    return pl.pallas_call(
        kernel,
        out_shape=outs,
        scratch_shapes=scratch,
        compiler_params=pltpu.CompilerParams(vmem_limit_bytes=56 << 20),
        **extra,
    )


TILE = 256


def tile_masks(seg_ref, block, tile):
    width = (tile + 1) * TILE
    segs = seg_ref[...]
    index = lax.broadcasted_iota(jnp.int32, (TILE, 1), 0) + (block * BLK + tile * TILE)
    own_id = jnp.zeros((TILE, 1), jnp.int32)
    for value in (1, 2, 3):
        below = jnp.sum(jnp.where(segs < value, 1, 0), axis=1, keepdims=True)
        own_id = own_id + jnp.where(index >= below, 1, 0)
    keys = segs[:, block * BLK : block * BLK + width]
    column = lax.broadcasted_iota(jnp.int32, (TILE, width), 1) + block * BLK
    own = (own_id == keys) & (column <= index)
    if block == 0:
        return own, None
    return own, own_id == segs[:, block * BLK - CTX : block * BLK]


def tile_scores(q, k, kc, own, ctx, scale):
    s = jnp.where(own, dot(q, k, NT) * scale, NEG)
    if ctx is None:
        return s, None
    return s, jnp.where(ctx, dot(q, kc, NT) * scale, NEG)


def attn_fwd_kernel(blocks, q_ref, k_ref, v_ref, ck_ref, cv_ref, seg_ref, o_ref, lse_ref):
    scale = HEAD**-0.5
    for block in range(blocks):
        for tile in range(BLK // TILE):
            own, ctx = tile_masks(seg_ref, block, tile)
            start, base = block * BLK + tile * TILE, block * BLK
            rows, keys = pl.ds(start, TILE), pl.ds(base, (tile + 1) * TILE)
            for head in range(q_ref.shape[1] // HEAD):
                cols = pl.ds(head * HEAD, HEAD)
                s, sc = tile_scores(
                    q_ref[rows, cols], k_ref[keys, cols], ck_ref[:, cols], own, ctx, scale
                )
                top = jnp.max(s, axis=1, keepdims=True)
                if sc is not None:
                    top = jnp.maximum(top, jnp.max(sc, axis=1, keepdims=True))
                total = jnp.sum(jnp.exp(s - top), axis=1, keepdims=True)
                if sc is not None:
                    total = total + jnp.sum(jnp.exp(sc - top), axis=1, keepdims=True)
                lse = top + jnp.log(total)
                lse_ref[head, rows, :] = lse
                out = dot(jnp.exp(s - lse).astype(BF16), v_ref[keys, cols])
                if sc is not None:
                    out = out + dot(jnp.exp(sc - lse).astype(BF16), cv_ref[:, cols])
                o_ref[rows, cols] = out.astype(BF16)


def attn_bwd_kernel(
    blocks, q_ref, k_ref, v_ref, ck_ref, cv_ref, seg_ref, lse_ref, do_ref,
    gq_ref, gk_ref, gv_ref, gck_ref, gcv_ref, ak_ref, av_ref,
):
    scale = HEAD**-0.5
    for block in range(blocks):
        base = block * BLK
        for tile in range(BLK // TILE):
            own, ctx = tile_masks(seg_ref, block, tile)
            width = (tile + 1) * TILE
            rows, keys = pl.ds(base + tile * TILE, TILE), pl.ds(base, width)
            for head in range(q_ref.shape[1] // HEAD):
                cols = pl.ds(head * HEAD, HEAD)
                q, k, v, do = q_ref[rows, cols], k_ref[keys, cols], v_ref[keys, cols], do_ref[rows, cols]
                kc, vc = ck_ref[:, cols], cv_ref[:, cols]
                s, sc = tile_scores(q, k, kc, own, ctx, scale)
                lse = lse_ref[head, rows, :]
                p = jnp.exp(s - lse)
                dp = dot(do, v, NT)
                weighted = jnp.sum(p * dp, axis=1, keepdims=True)
                if sc is not None:
                    pc = jnp.exp(sc - lse)
                    dpc = dot(do, vc, NT)
                    weighted = weighted + jnp.sum(pc * dpc, axis=1, keepdims=True)
                ds = (p * (dp - weighted)).astype(BF16)
                gq = dot(ds, k)
                gk = dot(ds, q, TN)
                gv = dot(p.astype(BF16), do, TN)
                if tile > 0:
                    half = tile * TILE
                    ak_ref[0:half, cols] = ak_ref[0:half, cols] + gk[0:half, :]
                    av_ref[0:half, cols] = av_ref[0:half, cols] + gv[0:half, :]
                    ak_ref[half:width, cols] = gk[half:width, :]
                    av_ref[half:width, cols] = gv[half:width, :]
                else:
                    ak_ref[0:width, cols] = gk
                    av_ref[0:width, cols] = gv
                if sc is not None:
                    dsc = (pc * (dpc - weighted)).astype(BF16)
                    gq = gq + dot(dsc, kc)
                    gkc = dot(dsc, q, TN) * scale
                    gvc = dot(pc.astype(BF16), do, TN)
                    if tile > 0:
                        gkc = gkc + gck_ref[:, cols]
                        gvc = gvc + gcv_ref[:, cols]
                    gck_ref[:, cols] = gkc
                    gcv_ref[:, cols] = gvc
                gq_ref[rows, cols] = (gq * scale).astype(BF16)
        gk_ref[base : base + BLK, :] = (ak_ref[...] * scale).astype(BF16)
        gv_ref[base : base + BLK, :] = av_ref[...].astype(BF16)


def normalize(values):
    centered = values - jnp.mean(values, axis=-1, keepdims=True)
    inverse = lax.rsqrt(jnp.mean(centered * centered, axis=-1, keepdims=True) + EPS)
    return centered * inverse, inverse


def norm_back(grad, hat, inverse, gain):
    u = grad * gain
    return inverse * (
        u - jnp.mean(u, axis=-1, keepdims=True) - hat * jnp.mean(u * hat, axis=-1, keepdims=True)
    )


def shards(
    tokens, cotangent, segments, w_query, w_key, w_value, w_out, w_up, up_bias, w_down, down_bias,
    norm1_gain, norm1_bias, norm2_gain, norm2_bias, decay_rates, input_mix, key_mix, value_mix,
    key_skip, value_skip,
):
    here = lax.axis_index("chan")
    own_tokens, width = tokens.shape
    length = segments.shape[1]
    own_cols = w_query.shape[1]
    shape = jax.ShapeDtypeStruct
    gather = functools.partial(lax.all_gather, axis_name="chan", axis=0, tiled=True)

    def scatter(partial):
        return lax.psum_scatter(partial.astype(BF16), "chan", scatter_dimension=0, tiled=True).astype(F32)

    def scatter_rows(partial):
        return lax.psum_scatter(partial.astype(BF16), "rows", scatter_dimension=0, tiled=True).astype(F32)

    row_tokens = gather(tokens)
    row_cot = gather(cotangent)
    full_out = lax.all_gather(w_out, "chan", axis=1, tiled=True)
    hat1, inv1 = normalize(row_tokens.astype(F32))
    hidden1 = (hat1 * norm1_gain + norm1_bias).astype(BF16)
    q, k, v = (dot(hidden1, w).astype(BF16) for w in (w_query, w_key, w_value))
    x = lax.dynamic_slice_in_dim(hidden1, here * own_cols, own_cols, 1)
    a = jnp.exp(-decay_rates)
    s = jnp.sqrt(-jnp.expm1(-2.0 * decay_rates))
    b = s * input_mix
    par = jnp.stack(
        [a, b, key_mix, value_mix, key_mix * b, value_mix * b, jnp.exp(-128.0 * decay_rates),
         128.0 * jnp.exp(-127.0 * decay_rates)]
    ).transpose(0, 2, 1)
    skip = jnp.stack([key_skip, value_skip])
    states = par.shape[1]
    ctx_k, ctx_v = call(
        ssm_fwd_kernel,
        [shape((CTX, own_cols), F32)] * 2,
        [pltpu.VMEM((CTX, own_cols), F32)],
    )(x, segments, par, skip)
    ctx_k, ctx_v = ctx_k.astype(BF16), ctx_v.astype(BF16)
    heads = own_cols // HEAD
    blocks = length // BLK
    attn, lse = call(
        functools.partial(attn_fwd_kernel, blocks),
        [shape((length, own_cols), BF16), shape((heads, length, 1), F32)],
    )(q, k, v, ctx_k, ctx_v, segments)
    row_attn = lax.all_gather(attn, "chan", axis=1, tiled=True)
    resid2 = row_tokens.astype(F32) + dot(row_attn, full_out)
    hat2, inv2 = normalize(resid2)
    hidden2 = (hat2 * norm2_gain + norm2_bias).astype(BF16)
    preact = dot(hidden2, w_up) + up_bias
    activated, gelu_back = jax.vjp(jax.nn.gelu, preact)
    act = activated.astype(BF16)
    grad_pre = gelu_back(dot(row_cot, w_down))[0].astype(BF16)
    grad_hidden2 = scatter(dot(grad_pre, w_up, NT))

    def own(values):
        return lax.dynamic_slice_in_dim(values, here * own_tokens, own_tokens, 0)

    own_hat2, own_inv2 = own(hat2), own(inv2)
    grad_resid2 = cotangent.astype(F32) + norm_back(grad_hidden2, own_hat2, own_inv2, norm2_gain)
    row_branch = gather(grad_resid2.astype(BF16))
    ffn = scatter(dot(act, w_down, NT))
    output = (own(resid2) + ffn + down_bias).astype(BF16)
    grad_up = scatter_rows(dot(hidden2, grad_pre, TN))
    grad_down = scatter_rows(dot(row_cot, act, TN))
    out_rows = lax.dynamic_slice_in_dim(full_out, here * own_cols, own_cols, 0)
    grad_attn = dot(row_branch, out_rows, NT).astype(BF16)
    grad_q, grad_k, grad_v, grad_ck, grad_cv = call(
        functools.partial(attn_bwd_kernel, blocks),
        [shape((length, own_cols), BF16)] * 3 + [shape((CTX, own_cols), F32)] * 2,
        [pltpu.VMEM((BLK, own_cols), F32)] * 2,
    )(q, k, v, ctx_k, ctx_v, segments, lse, grad_attn)
    grad_x, grad_par, grad_skip = call(
        ssm_bwd_kernel,
        [shape((length, own_cols), F32), shape((4, states, own_cols), F32), shape((2, own_cols), F32)],
        [pltpu.VMEM((CTX + 1, states, own_cols), F32)],
    )(x, segments, par, skip, grad_ck, grad_cv)
    partial1 = dot(grad_q, w_query, NT) + dot(grad_k, w_key, NT) + dot(grad_v, w_value, NT)
    place = lax.dynamic_update_slice_in_dim(
        jnp.zeros((length, width), F32), grad_x.astype(BF16).astype(F32), here * own_cols, 1
    )
    grad_hidden1 = scatter(partial1 + place)
    own_hat1, own_inv1 = own(hat1), own(inv1)
    grad_tokens = (grad_resid2 + norm_back(grad_hidden1, own_hat1, own_inv1, norm1_gain)).astype(BF16)
    branch_cols = lax.dynamic_slice_in_dim(row_branch, here * own_cols, own_cols, 1)
    grad_out = scatter_rows(dot(row_attn, branch_cols, TN))
    grad_qkv = scatter_rows(
        jnp.concatenate([dot(hidden1, g, TN) for g in (grad_q, grad_k, grad_v)], axis=1)
    )
    sk, sv, sx, sg = (grad_par[i].T for i in range(4))
    grad_in = s * sx
    grad_dec = (a * a / s) * input_mix * sx - a * b * sg
    grad_up_bias = jnp.sum(grad_pre.astype(F32), axis=0)
    mine = jnp.concatenate(
        [t.reshape(-1) for t in (grad_dec, grad_in, sk, sv, grad_skip[0], grad_skip[1], grad_up_bias)]
    )
    mine = lax.all_gather(lax.psum(mine, "rows"), "chan", axis=0)
    size = own_cols * states
    pieces = [mine[:, i * size : (i + 1) * size].reshape(width, states) for i in range(4)]
    rest = mine[:, 4 * size :]
    skips = [rest[:, i * own_cols : (i + 1) * own_cols].reshape(width) for i in range(2)]
    up_bias_grad = rest[:, 2 * own_cols :].reshape(-1)
    shared = lax.psum(
        jnp.stack(
            [
                jnp.sum(grad_hidden1 * own_hat1, axis=0),
                jnp.sum(grad_hidden1, axis=0),
                jnp.sum(grad_hidden2 * own_hat2, axis=0),
                jnp.sum(grad_hidden2, axis=0),
                jnp.sum(cotangent.astype(F32), axis=0),
            ]
        ),
        ("rows", "chan"),
    )
    return (
        output, grad_tokens,
        grad_qkv[:, :own_cols], grad_qkv[:, own_cols : 2 * own_cols], grad_qkv[:, 2 * own_cols :],
        grad_out, grad_up, up_bias_grad, grad_down,
        shared[4], shared[0], shared[1], shared[2], shared[3],
        pieces[0], pieces[1], pieces[2], pieces[3], skips[0], skips[1],
    )


def solution(mesh):
    both, row, col = P(("rows", "chan"), None), P("rows", None), P(None, "chan")
    state = P("chan", None)
    in_specs = (
        both, both, row, col, col, col, col, col, P("chan"), col,
        P(), P(), P(), P(), P(), state, state, state, state, P("chan"), P("chan"),
    )
    grid = P("rows", "chan")
    out_specs = (both, both, grid, grid, grid, grid, grid, P(), grid) + (P(),) * 11
    return jax.shard_map(shards, mesh=mesh, in_specs=in_specs, out_specs=out_specs, check_vma=False)
```

```python
import functools
import math

import jax
import jax.numpy as jnp
from jax import lax
from jax.experimental import pallas as pl
from jax.experimental.pallas import tpu as pltpu
from jax.sharding import PartitionSpec as P

HEAD = 128
CTX = 128
BLK = 512
TILE = 256
EPS = 1e-05
NEG = -1e30
F32 = jnp.float32
BF16 = jnp.bfloat16
NN = (((1,), (0,)), ((), ()))
NT = (((1,), (1,)), ((), ()))
TN = (((0,), (0,)), ((), ()))
ROOT = math.sqrt(2.0 / math.pi)
MESH = pl.DeviceIdType.MESH


def dot(left, right, dims=NN):
    return lax.dot_general(left, right, dims, preferred_element_type=F32)


def at(start, size):
    if isinstance(start, int):
        return pl.ds(start, size)
    return pl.ds(pl.multiple_of(start, math.gcd(size, 1024)), size)


def ssm_params(rate_ref, in_ref, key_ref, value_ref):
    rate = rate_ref[...].T
    a = jnp.exp(-rate)
    s = jnp.sqrt(1.0 - a * a)
    return dict(rate=rate, a=a, s=s, mix=in_ref[...].T, km=key_ref[...].T, vm=value_ref[...].T)


def ssm_forward(x_ref, seg_ref, par, skip_k, skip_v, ck_ref, cv_ref, wide_k, wide_v, keep_ref):
    a, rate = par["a"], par["rate"]
    b = par["s"] * par["mix"]
    kb, vb = par["km"] * b, par["vm"] * b
    a128, d128 = jnp.exp(-128.0 * rate), 128.0 * jnp.exp(-127.0 * rate)
    first = BLK - CTX
    parts = first // 128
    mask = segment_mask(seg_ref)
    row = lax.broadcasted_iota(jnp.int32, (8, 1), 0)
    zero = jnp.zeros(a.shape, F32)

    def step(i, carry):
        out = []
        for j in range(parts):
            g, e = carry[j]
            base = pl.multiple_of(j * 128 + i * 8, 8)
            x8 = jnp.where(mask(row + base), x_ref[pl.ds(base, 8), :], 0.0)
            for t in range(8):
                e = a * e + g
                g = a * g + x8[t : t + 1, :]
            out.append((g, e))
        return tuple(out)

    ends = lax.fori_loop(0, 16, step, tuple((zero, zero) for _ in range(parts)))
    g, e = ends[0]
    for j in range(1, parts):
        e = ends[j][1] + a128 * e + d128 * g
        g = ends[j][0] + a128 * g
    keep_ref[0] = g

    def ahead(i, g):
        base = pl.multiple_of(first + i * 8, 8)
        raw = x_ref[pl.ds(base, 8), :]
        x8 = jnp.where(mask(row + base), raw, 0.0)
        ks, vs = [], []
        for t in range(8):
            g = a * g + x8[t : t + 1, :]
            keep_ref[i * 8 + t + 1] = g
            ks.append(jnp.sum(g * kb, axis=0, keepdims=True))
            vs.append(jnp.sum(g * vb, axis=0, keepdims=True))
        rows = pl.ds(pl.multiple_of(i * 8, 8), 8)
        wide_k[rows, :] = jnp.concatenate(ks, axis=0) + skip_k * raw
        wide_v[rows, :] = jnp.concatenate(vs, axis=0) + skip_v * raw
        return g

    lax.fori_loop(0, CTX // 8, ahead, g)
    ck_ref[...] = wide_k[...].astype(BF16)
    cv_ref[...] = wide_v[...].astype(BF16)
    return e


def segment_mask(seg_ref):
    segs = seg_ref[...]
    first = jnp.sum(jnp.where(segs < segs[:, BLK : BLK + 1], 1, 0), axis=1, keepdims=True)
    return lambda index: index >= first


def ssm_backward(x_ref, seg_ref, par, skip_k, skip_v, gk_ref, gv_ref, keep_ref, e0, gx_ref, small_ref):
    a, s, km, vm = par["a"], par["s"], par["km"], par["vm"]
    b = s * par["mix"]
    first = BLK - CTX
    mask = segment_mask(seg_ref)
    row = lax.broadcasted_iota(jnp.int32, (8, 1), 0)
    zero = jnp.zeros(a.shape, F32)

    def back(j, carry):
        lam, sk, sv, sx, sg = carry
        i = CTX // 8 - 1 - j
        base = pl.multiple_of(first + i * 8, 8)
        rows = pl.ds(pl.multiple_of(i * 8, 8), 8)
        inside = mask(row + base)
        x8 = jnp.where(inside, x_ref[pl.ds(base, 8), :], 0.0)
        k8, v8 = gk_ref[rows, :], gv_ref[rows, :]
        outs = [None] * 8
        for t in reversed(range(8)):
            kt, vt = k8[t : t + 1, :], v8[t : t + 1, :]
            lam = a * lam + km * kt + vm * vt
            now = keep_ref[i * 8 + t + 1]
            sk = sk + now * kt
            sv = sv + now * vt
            sx = sx + lam * x8[t : t + 1, :]
            sg = sg + lam * keep_ref[i * 8 + t]
            outs[t] = jnp.sum(lam * b, axis=0, keepdims=True)
        gx = jnp.where(inside, jnp.concatenate(outs, axis=0), 0.0)
        gx_ref[pl.ds(base, 8), :] = gx + skip_k * k8 + skip_v * v8
        return (lam, sk, sv, sx, sg)

    lam, sk, sv, sx, sg = lax.fori_loop(0, CTX // 8, back, (zero,) * 5)
    sx = sx + lam * (a * keep_ref[0])
    sg = sg + lam * (a * e0)
    ns = a.shape[0]
    small_ref[0:ns, :] = (a * a / s) * par["mix"] * sx - a * b * sg
    small_ref[ns : 2 * ns, :] = s * sx
    small_ref[2 * ns : 3 * ns, :] = sk * b
    small_ref[3 * ns : 4 * ns, :] = sv * b

    def tail(j, w):
        base = pl.multiple_of(first - 8 - j * 8, 8)
        outs = [None] * 8
        for t in reversed(range(8)):
            w = a * w
            outs[t] = jnp.sum(w, axis=0, keepdims=True)
        gx_ref[pl.ds(base, 8), :] = jnp.where(mask(row + base), jnp.concatenate(outs, axis=0), 0.0)
        return w

    lax.fori_loop(0, first // 8, tail, lam * b)
    raw = x_ref[first:BLK, :]
    small_ref[4 * ns : 4 * ns + 1, :] = jnp.sum(gk_ref[...] * raw, axis=0, keepdims=True)
    small_ref[4 * ns + 1 : 4 * ns + 2, :] = jnp.sum(gv_ref[...] * raw, axis=0, keepdims=True)


def tile_masks(seg_ref, block, tile):
    width = (tile + 1) * TILE
    segs = seg_ref[...]
    index = lax.broadcasted_iota(jnp.int32, (TILE, 1), 0) + (block * BLK + tile * TILE)
    own_id = jnp.zeros((TILE, 1), jnp.int32)
    for value in (1, 2, 3):
        below = jnp.sum(jnp.where(segs < value, 1, 0), axis=1, keepdims=True)
        own_id = own_id + jnp.where(index >= below, 1, 0)
    keys = segs[:, block * BLK : block * BLK + width]
    column = lax.broadcasted_iota(jnp.int32, (TILE, width), 1) + block * BLK
    own = (own_id == keys) & (column <= index)
    if block == 0:
        return own, None
    return own, own_id == segs[:, block * BLK - CTX : block * BLK]


def attn_forward(block, q_ref, k_ref, v_ref, ck_ref, cv_ref, seg_ref, store, lse_ref):
    scale = HEAD**-0.5
    for tile in range(BLK // TILE):
        own, ctx = tile_masks(seg_ref, block, tile)
        rows = pl.ds(block * BLK + tile * TILE, TILE)
        keys = pl.ds(block * BLK, (tile + 1) * TILE)
        for head in range(q_ref.shape[1] // HEAD):
            cols = pl.ds(head * HEAD, HEAD)
            q = q_ref[rows, cols]
            s = jnp.where(own, dot(q, k_ref[keys, cols], NT) * scale, NEG)
            top = jnp.max(s, axis=1, keepdims=True)
            if ctx is not None:
                sc = jnp.where(ctx, dot(q, ck_ref[:, cols], NT) * scale, NEG)
                top = jnp.maximum(top, jnp.max(sc, axis=1, keepdims=True))
            p = jnp.exp(s - top)
            total = jnp.sum(p, axis=1, keepdims=True)
            if ctx is not None:
                pc = jnp.exp(sc - top)
                total = total + jnp.sum(pc, axis=1, keepdims=True)
            lse_ref[head, rows, :] = top + jnp.log(total)
            inverse = 1.0 / total
            out = dot((p * inverse).astype(BF16), v_ref[keys, cols])
            if ctx is not None:
                out = out + dot((pc * inverse).astype(BF16), cv_ref[:, cols])
            store(rows, head, out.astype(BF16))


def attn_backward(
    block, q_ref, k_ref, v_ref, ck_ref, cv_ref, seg_ref, lse_ref, do_ref,
    gq_ref, gk_ref, gv_ref, gck_ref, gcv_ref, ak_ref, av_ref,
):
    scale = HEAD**-0.5
    base = block * BLK
    for tile in range(BLK // TILE):
        own, ctx = tile_masks(seg_ref, block, tile)
        width = (tile + 1) * TILE
        rows, keys = pl.ds(base + tile * TILE, TILE), pl.ds(base, width)
        for head in range(q_ref.shape[1] // HEAD):
            cols = pl.ds(head * HEAD, HEAD)
            q, k, v = q_ref[rows, cols], k_ref[keys, cols], v_ref[keys, cols]
            do = do_ref[tile * TILE : (tile + 1) * TILE, cols]
            lse = lse_ref[head, rows, :]
            p = jnp.exp(jnp.where(own, dot(q, k, NT) * scale, NEG) - lse)
            dp = dot(do, v, NT)
            weighted = jnp.sum(p * dp, axis=1, keepdims=True)
            if ctx is not None:
                kc, vc = ck_ref[:, cols], cv_ref[:, cols]
                pc = jnp.exp(jnp.where(ctx, dot(q, kc, NT) * scale, NEG) - lse)
                dpc = dot(do, vc, NT)
                weighted = weighted + jnp.sum(pc * dpc, axis=1, keepdims=True)
            ds = (p * (dp - weighted)).astype(BF16)
            gq = dot(ds, k)
            gk = dot(ds, q, TN)
            gv = dot(p.astype(BF16), do, TN)
            half = tile * TILE
            if tile > 0:
                ak_ref[0:half, cols] = ak_ref[0:half, cols] + gk[0:half, :]
                av_ref[0:half, cols] = av_ref[0:half, cols] + gv[0:half, :]
            ak_ref[half:width, cols] = gk[half:width, :]
            av_ref[half:width, cols] = gv[half:width, :]
            if ctx is not None:
                dsc = (pc * (dpc - weighted)).astype(BF16)
                gq = gq + dot(dsc, kc)
                gkc = dot(dsc, q, TN) * scale
                gvc = dot(pc.astype(BF16), do, TN)
                if tile > 0:
                    gkc = gkc + gck_ref[:, cols]
                    gvc = gvc + gcv_ref[:, cols]
                gck_ref[:, cols] = gkc
                gcv_ref[:, cols] = gvc
            gq_ref[rows, cols] = (gq * scale).astype(BF16)
    gk_ref[base : base + BLK, :] = (ak_ref[...] * scale).astype(BF16)
    gv_ref[base : base + BLK, :] = av_ref[...].astype(BF16)


def normalize(values):
    centered = values - jnp.mean(values, axis=-1, keepdims=True)
    inverse = lax.rsqrt(jnp.mean(centered * centered, axis=-1, keepdims=True) + EPS)
    return centered * inverse, inverse


def norm_back(grad, hat, inverse, gain):
    u = grad * gain
    return inverse * (
        u - jnp.mean(u, axis=-1, keepdims=True) - hat * jnp.mean(u * hat, axis=-1, keepdims=True)
    )


class Links:
    def __init__(self, plan, send, recv):
        self.plan, self.send, self.recv, self.used = plan, send, recv, 0
        self.chan, self.rows = lax.axis_index("chan"), lax.axis_index("rows")
        self.mate = self.chan + 1 - 2 * lax.rem(self.chan, 2)
        self.core = lax.rem(self.chan, 2)
        self.y = self.chan // 2
        self.x = lax.rem(self.rows, plan["X"])
        self.z = self.rows // plan["X"]

    def far(self, j):
        count = self.plan["Y"]
        return 2 * lax.rem(self.y + count + j, count) + self.core

    def other(self, chan):
        return chan + 1 - 2 * lax.rem(chan, 2)

    def put(self, source, target, **device):
        i = self.used
        self.used += 1
        copy = pltpu.make_async_remote_copy(
            src_ref=source, dst_ref=target, send_sem=self.send.at[i], recv_sem=self.recv.at[i],
            device_id=device, device_id_type=MESH,
        )
        copy.start()
        return copy

    def load(self, source, target):
        i = self.used
        self.used += 1
        copy = pltpu.make_async_copy(source, target, self.send.at[i])
        copy.start()
        return copy

    def enter(self):
        barrier = pltpu.get_barrier_semaphore()
        plan = self.plan
        partners = [{"chan": self.mate}]
        partners += [{"chan": self.far(j)} for j in range(1, plan["Y"])]
        partners += [{"rows": self.row_of(self.z, self.x + i)} for i in range(1, plan["X"])]
        partners += [{"rows": self.row_of(self.z + i, self.x)} for i in range(1, plan["Z"])]
        for partner in partners:
            pl.semaphore_signal(barrier, inc=1, device_id=partner, device_id_type=MESH)
        return lambda: pl.semaphore_wait(barrier, len(partners))

    def row_of(self, z, x):
        return lax.rem(z, self.plan["Z"]) * self.plan["X"] + lax.rem(x, self.plan["X"])


class Gather:
    def __init__(self, links, view):
        self.links, self.view = links, view
        own = view(links.chan)
        count = range(1, links.plan["Y"])
        self.direct = [links.put(own, own, chan=links.far(j)) for j in count]
        self.near = links.put(own, own, chan=links.mate)
        self.passed = []

    def forward(self):
        links = self.links
        for j, copy in enumerate(self.direct, 1):
            copy.wait_recv()
            shard = self.view(links.far(-j))
            self.passed.append(links.put(shard, shard, chan=links.mate))

    def finish(self):
        self.near.wait()
        for copy in self.passed:
            copy.wait()
        for copy in self.direct:
            copy.wait_send()


class Scatter:
    def __init__(self, links, mixed_out, mixed_in, far_out, far_in, near_out, near_in):
        self.links = links
        self.mixed_out, self.mixed_in, self.far_out, self.far_in = mixed_out, mixed_in, far_out, far_in
        self.near_out, self.near_in = near_out, near_in
        self.mix, self.direct = [], []

    def for_mate(self, j, value):
        self.mixed_out[j - 1] = value.astype(BF16)
        self.mix.append(
            self.links.put(self.mixed_out.at[j - 1], self.mixed_in.at[j - 1], chan=self.links.mate)
        )

    def for_far(self, j, value_ref):
        self.mix[j - 1].wait_recv()
        self.far_out[j - 1] = (value_ref[...] + self.mixed_in[j - 1].astype(F32)).astype(BF16)

    def send_far(self):
        links = self.links
        self.direct = [
            links.put(self.far_out.at[j - 1], self.far_in.at[j - 1], chan=links.far(j))
            for j in range(1, links.plan["Y"])
        ]

    def for_near(self, value):
        self.near_out[...] = value.astype(BF16)
        self.near = self.links.put(self.near_out, self.near_in, chan=self.links.mate)

    def total(self, own):
        self.near.wait()
        own = own + self.near_in[...].astype(F32)
        for j, copy in enumerate(self.direct):
            copy.wait()
            own = own + self.far_in[j].astype(F32)
        for copy in self.mix:
            copy.wait_send()
        return own


class RowScatter:
    def __init__(self, links, stage, x_in, z_in):
        self.links, self.stage, self.x_in, self.z_in = links, stage, x_in, z_in

    def slab(self, z, x):
        size = self.x_in.shape[2]
        return pl.ds(pl.multiple_of(self.links.row_of(z, x) * size, size), size)

    def over_x(self):
        links, plan = self.links, self.links.plan
        self.first = []
        for step in range(1, plan["Z"] + 1):
            for i in range(1, plan["X"]):
                self.first.append(
                    links.put(
                        self.stage.at[self.slab(links.z + step, links.x + i)],
                        self.x_in.at[i - 1, step - 1],
                        rows=links.row_of(links.z, links.x + i),
                    )
                )

    def mixed(self, step):
        links, plan = self.links, self.links.plan
        value = self.stage[self.slab(links.z + step, links.x), :].astype(F32)
        for i in range(1, plan["X"]):
            self.first[(step - 1) * (plan["X"] - 1) + i - 1].wait()
            value = value + self.x_in[i - 1, step - 1].astype(F32)
        return value

    def over_z(self):
        links, plan = self.links, self.links.plan
        self.second = []
        for step in range(1, plan["Z"]):
            slab = self.slab(links.z + step, links.x)
            self.stage[slab, :] = self.mixed(step).astype(BF16)
            self.second.append(
                links.put(
                    self.stage.at[slab], self.z_in.at[step - 1],
                    rows=links.row_of(links.z + step, links.x),
                )
            )
        self.own = self.mixed(plan["Z"])

    def total(self):
        value = self.own
        for i, copy in enumerate(self.second):
            copy.wait()
            value = value + self.z_in[i].astype(F32)
        return value


def names(plan):
    n, length, d, t, c, f = (plan[k] for k in ("n", "L", "D", "T", "C", "F"))
    far = plan["Y"] - 1
    x1, z, rw = plan["X"] - 1, plan["Z"], plan["RW"]
    grid = (length, d)
    out = [("tok", grid, BF16), ("h1", grid, BF16), ("cot", grid, BF16), ("wout", (d, d), BF16)]
    out += [("attn", grid, BF16), ("h2", grid, BF16), ("act", (length, f), BF16), ("gpre", (length, f), BF16)]
    out += [(w, (d, c), BF16) for w in ("wq", "wk", "wv")] + [("wup", (d, f), BF16), ("wdn", (d, f), BF16)]
    out += [(w, (length, c), BF16) for w in ("q", "k", "v")]
    out += [("ck", (CTX, c), BF16), ("cv", (CTX, c), BF16), ("gck", (CTX, c), F32), ("gcv", (CTX, c), F32)]
    out += [("lse", (c // HEAD, length, 1), F32), ("xs", (BLK, c), F32), ("gx", (BLK, c), F32)]
    out += [("keep", (CTX + 1, plan["NS"], c), F32), ("ak", (BLK, c), F32), ("av", (BLK, c), F32)]
    out += [("do", (BLK, c), BF16), ("r2own", (t, d), F32), ("p", (t, d), F32)]
    out += [("acc", (t, d), F32), ("ffn", (t, d), F32)]
    for s in ("a", "b"):
        out += [(s + part, (far, t, d), BF16) for part in ("_mo", "_mi", "_fo", "_fi")]
        out += [(s + part, (t, d), BF16) for part in ("_no", "_ni")]
    out += [("stage", (d, f), BF16)]
    for s in ("up", "dn", "at"):
        out += [(s + "_xi", (x1, z, rw, f), BF16), (s + "_zi", (z - 1, rw, f), BF16)]
    steps = plan["R"].bit_length() - 1
    out += [("small", (plan["SM"], c), F32), ("smallin", (steps, plan["SM"], c), F32), ("smallout", (steps, plan["SM"], c), F32)]
    out += [("smallall", (n, plan["SM"], c), F32)]
    return out


INPUTS = (
    "tokens", "cotangent", "segments", "w_query", "w_key", "w_value", "w_out", "w_up", "up_bias", "w_down",
    "down_bias", "norm1_gain", "norm1_bias", "norm2_gain", "norm2_bias", "decay_rates", "input_mix",
    "key_mix", "value_mix", "key_skip", "value_skip",
)
LARGE = (
    "tokens", "cotangent", "w_query", "w_key", "w_value", "w_out", "w_up", "w_down",
)


class Box:
    def __init__(self, **items):
        self.__dict__.update(items)


def layer_kernel(plan, *refs):
    i = Box(**dict(zip(INPUTS, refs[:21])))
    outs = refs[21 : 21 + plan["outs"]]
    o_out, o_tok, o_q, o_k, o_v, o_o, o_up, o_dn, o_ub, o_vec, o_dec, o_in, o_km, o_vm, o_skip = outs
    scratch = refs[21 + plan["outs"] :]
    s = Box(**dict(zip([x[0] for x in names(plan)], scratch)))
    links = Links(plan, scratch[-2], scratch[-1])
    n, length, d, t, c, f = (plan[k] for k in ("n", "L", "D", "T", "C", "F"))
    far = range(1, plan["Y"])
    here, mate = links.chan, links.mate
    own_rows, own_cols = at(here * t, t), at(here * c, c)
    rows_of = lambda owner: at(owner * t, t)

    ready = links.enter()
    got_tok = links.load(i.tokens, s.tok.at[own_rows])
    got_w = [links.load(a, b) for a, b in ((i.w_query, s.wq), (i.w_key, s.wk), (i.w_value, s.wv))]
    got_cot = links.load(i.cotangent, s.cot.at[own_rows])
    got_out = links.load(i.w_out, s.wout.at[:, own_cols])
    got_up, got_dn = links.load(i.w_up, s.wup), links.load(i.w_down, s.wdn)
    par = ssm_params(i.decay_rates, i.input_mix, i.key_mix, i.value_mix)
    got_tok.wait()
    ready()
    tok_gather = Gather(links, lambda o: s.tok.at[rows_of(o)])

    def project(owner):
        rows = rows_of(owner)
        hat, _ = normalize(s.tok[rows, :].astype(F32))
        s.h1[rows, :] = (hat * i.norm1_gain[...] + i.norm1_bias[...]).astype(BF16)
        for w, target in ((s.wq, s.q), (s.wk, s.k), (s.wv, s.v)):
            target[rows, :] = dot(s.h1[rows, :], w[...]).astype(BF16)

    for got in got_w:
        got.wait()
    project(here)
    tok_gather.near.wait_recv()
    project(mate)
    got_cot.wait()
    got_out.wait()
    tok_gather.forward()
    out_gather = Gather(links, lambda o: s.wout.at[:, at(o * c, c)])
    cot_gather = Gather(links, lambda o: s.cot.at[rows_of(o)])
    for j in far:
        project(links.far(-j))
    for j, copy in zip(far, tok_gather.passed):
        copy.wait_recv()
        project(links.other(links.far(-j)))
    tok_gather.near.wait_send()
    for copy in tok_gather.passed + tok_gather.direct:
        copy.wait_send()

    s.xs[...] = s.h1[0:BLK, own_cols].astype(F32)
    skip_k, skip_v = i.key_skip[...], i.value_skip[...]
    e0 = ssm_forward(s.xs, i.segments, par, skip_k, skip_v, s.ck, s.cv, s.gck, s.gcv, s.keep)

    def store(rows, head, value):
        s.attn[rows, at(here * c + head * HEAD, HEAD)] = value

    attn_gathers = []
    for block in range(length // BLK):
        attn_forward(block, s.q, s.k, s.v, s.ck, s.cv, i.segments, store, s.lse)
        attn_gathers.append(
            Gather(links, lambda o, block=block: s.attn.at[pl.ds(block * BLK, BLK), at(o * c, c)])
        )
    out_gather.forward()
    cot_gather.forward()
    for gather in attn_gathers:
        gather.forward()
    out_gather.finish()
    cot_gather.finish()
    for gather in attn_gathers:
        gather.finish()
    got_up.wait()
    got_dn.wait()

    wide = 256

    def feed(owner, keep):
        rows = rows_of(owner)

        def residual(e, carry):
            cols = at(e * wide, wide)
            s.p[:, cols] = s.tok[rows, cols].astype(F32) + dot(s.attn[rows, :], s.wout[:, cols])
            return carry

        lax.fori_loop(0, d // wide, residual, 0)
        hat, _ = normalize(s.p[...])
        s.h2[rows, :] = (hat * i.norm2_gain[...] + i.norm2_bias[...]).astype(BF16)
        if keep:
            s.r2own[...] = s.p[...]

        def hidden(e, carry):
            cols = at(e * wide, wide)
            v = dot(s.h2[rows, :], s.wup[:, cols]) + i.up_bias[:, cols]
            grad = dot(s.cot[rows, :], s.wdn[:, cols])
            square = v * v
            th = jnp.tanh(ROOT * (v + 0.044715 * (square * v)))
            half = 0.5 * (1.0 + th)
            s.act[rows, cols] = (v * half).astype(BF16)
            slope = half + 0.5 * v * (1.0 - th * th) * (ROOT * (1.0 + 0.134145 * square))
            s.gpre[rows, cols] = (grad * slope).astype(BF16)
            return carry

        lax.fori_loop(0, f // wide, hidden, 0)

    def back_tile(owner, source, weight):
        rows = rows_of(owner)

        def part(e, carry):
            cols = at(e * wide, wide)
            s.p[:, cols] = dot(source[rows, :], weight[cols, :], NT)
            return carry

        lax.fori_loop(0, d // wide, part, 0)

    def weight_grad(left, right, stage, column):
        def part(e, carry):
            cols = at(e * wide, wide)
            stage[cols, column : column + right.shape[1]] = dot(left[:, cols], right[...], TN).astype(BF16)
            return carry

        lax.fori_loop(0, d // wide, part, 0)

    scatter = lambda k: Scatter(links, *(getattr(s, k + x) for x in ("_mo", "_mi", "_fo", "_fi", "_no", "_ni")))
    grad2 = scatter("a")
    for j in far:
        feed(links.other(links.far(j)), False)
        back_tile(links.other(links.far(j)), s.gpre, s.wup)
        grad2.for_mate(j, s.p[...])
    for j in far:
        feed(links.far(j), False)
        back_tile(links.far(j), s.gpre, s.wup)
        grad2.for_far(j, s.p)
    grad2.send_far()
    feed(mate, False)
    back_tile(mate, s.gpre, s.wup)
    grad2.for_near(s.p[...])
    feed(here, True)
    back_tile(here, s.gpre, s.wup)
    s.acc[...] = s.p[...]

    def rows_sum(k, stage):
        return RowScatter(links, stage, *(getattr(s, k + x) for x in ("_xi", "_zi")))

    weight_grad(s.cot, s.act, s.stage, 0)
    down_sum = rows_sum("dn", s.stage)
    down_sum.over_x()
    ffn = scatter("b")
    for j in far:
        back_tile(links.other(links.far(j)), s.act, s.wdn)
        ffn.for_mate(j, s.p[...])
    for j in far:
        back_tile(links.far(j), s.act, s.wdn)
        ffn.for_far(j, s.p)
    back_tile(mate, s.act, s.wdn)
    ffn.for_near(s.p[...])
    back_tile(here, s.act, s.wdn)
    s.ffn[...] = s.p[...]
    weight_grad(s.h2, s.gpre, s.act, 0)
    up_sum = rows_sum("up", s.act)
    up_sum.over_x()

    base = 4 * plan["NS"] + 2
    bias_rows = f // c
    for e in range(bias_rows):
        s.small[base + e : base + e + 1, :] = jnp.sum(
            s.gpre[:, e * c : (e + 1) * c].astype(F32), axis=0, keepdims=True
        )
    base += bias_rows

    def keep_vector(k, value):
        for e in range(n):
            s.small[base + k * n + e : base + k * n + e + 1, :] = value[:, e * c : (e + 1) * c]

    def colsum(value):
        return jnp.sum(value, axis=0, keepdims=True)

    grad_hidden2 = grad2.total(s.acc[...])
    hat2, inv2 = normalize(s.r2own[...])
    own_cot = s.cot[own_rows, :].astype(F32)
    s.acc[...] = own_cot + norm_back(grad_hidden2, hat2, inv2, i.norm2_gain[...])
    s.tok[own_rows, :] = s.acc[...].astype(BF16)
    branch_gather = Gather(links, lambda o: s.tok.at[rows_of(o)])
    keep_vector(0, colsum(own_cot))
    keep_vector(3, colsum(grad_hidden2 * hat2))
    keep_vector(4, colsum(grad_hidden2))
    down_sum.over_z()
    branch_gather.forward()
    branch_gather.finish()
    ffn.send_far()

    for block in reversed(range(length // BLK)):
        s.do[...] = dot(s.tok[block * BLK : (block + 1) * BLK, :], s.wout[own_cols, :], NT).astype(BF16)
        attn_backward(
            block, s.q, s.k, s.v, s.ck, s.cv, i.segments, s.lse, s.do,
            s.q, s.k, s.v, s.gck, s.gcv, s.ak, s.av,
        )
        if block == 1:
            up_sum.over_z()
            ssm_backward(
                s.xs, i.segments, par, skip_k, skip_v, s.gck, s.gcv, s.keep, e0, s.gx, s.small
            )

    def input_tile(owner):
        rows = rows_of(owner)

        def part(e, carry):
            cols = at(e * wide, wide)
            s.p[:, cols] = (
                dot(s.q[rows, :], s.wq[cols, :], NT)
                + dot(s.k[rows, :], s.wk[cols, :], NT)
                + dot(s.v[rows, :], s.wv[cols, :], NT)
            )
            return carry

        lax.fori_loop(0, d // wide, part, 0)

        @pl.when(owner < BLK // t)
        def _():
            s.p[:, own_cols] = s.p[:, own_cols] + s.gx[rows, :].astype(BF16).astype(F32)

    grad1 = scatter("a")
    for j in far:
        input_tile(links.other(links.far(j)))
        grad1.for_mate(j, s.p[...])
    for j in far:
        input_tile(links.far(j))
        grad1.for_far(j, s.p)
    grad1.send_far()
    input_tile(mate)
    grad1.for_near(s.p[...])
    input_tile(here)
    weight_grad(s.h1, s.q, s.h2, 0)
    weight_grad(s.h1, s.k, s.h2, c)
    weight_grad(s.h1, s.v, s.h2, 2 * c)
    s.q[...] = s.tok[:, own_cols]
    weight_grad(s.attn, s.q, s.h2, 3 * c)
    attn_sum = rows_sum("at", s.h2 if f == d else s.h2.at[:, 0:f])
    attn_sum.over_x()
    o_dn[...] = down_sum.total()
    o_up[...] = up_sum.total()
    o_out[...] = (s.r2own[...] + ffn.total(s.ffn[...]) + i.down_bias[...]).astype(BF16)

    got_tok = links.load(i.tokens, s.gpre.at[0:t] if f == d else s.cot.at[0:t])
    got_tok.wait()
    own_tok = (s.gpre if f == d else s.cot)[0:t, :].astype(F32)
    hat1, inv1 = normalize(own_tok)
    grad_hidden1 = grad1.total(s.p[...])
    o_tok[...] = (s.acc[...] + norm_back(grad_hidden1, hat1, inv1, i.norm1_gain[...])).astype(BF16)
    keep_vector(1, colsum(grad_hidden1 * hat1))
    keep_vector(2, colsum(grad_hidden1))

    steps = plan["R"].bit_length() - 1
    for step in range(steps):
        s.smallout[step] = s.small[...]
        bit = 1 << step
        up = lax.rem(links.rows // bit, 2)
        copy = links.put(s.smallout.at[step], s.smallin.at[step], rows=links.rows + bit - 2 * bit * up)
        if step == 0:
            attn_sum.over_z()
        copy.wait()
        s.small[...] = s.small[...] + s.smallin[step]
    s.smallall[here] = s.small[...]
    small_gather = Gather(links, lambda o: s.smallall.at[o])
    total = attn_sum.total()
    for e, target in enumerate((o_q, o_k, o_v, o_o)):
        target[...] = total[:, e * c : (e + 1) * c]
    small_gather.forward()
    small_gather.finish()
    ns = plan["NS"]
    for e in range(n):
        piece = s.smallall[e]
        for k, target in enumerate((o_dec, o_in, o_km, o_vm)):
            target[e * c : (e + 1) * c, :] = piece[k * ns : (k + 1) * ns, :].T
        o_skip[:, e * c : (e + 1) * c] = piece[4 * ns : 4 * ns + 2, :]
        for b in range(bias_rows):
            o_ub[:, e * f + b * c : e * f + (b + 1) * c] = piece[4 * ns + 2 + b : 4 * ns + 3 + b, :]
    vectors = s.smallall[0]
    for e in range(1, n):
        vectors = vectors + s.smallall[e]
    for k in range(5):
        for e in range(n):
            o_vec[k : k + 1, e * c : (e + 1) * c] = vectors[base + k * n + e : base + k * n + e + 1, :]


def shards(*args):
    a = dict(zip(INPUTS, args))
    n, r = lax.axis_size("chan"), lax.axis_size("rows")
    t, d = a["tokens"].shape
    c, f = a["w_query"].shape[1], a["w_up"].shape[1]
    ns = a["decay_rates"].shape[1]
    x = math.isqrt(r // 2)
    small = 4 * ns + 2 + f // c + 5 * n
    plan = dict(
        n=n, R=r, L=a["segments"].shape[1], D=d, T=t, C=c, F=f, NS=ns, Y=n // 2, X=x, Z=r // x,
        RW=d // r, SM=-(-small // 8) * 8, outs=15,
    )
    shape = jax.ShapeDtypeStruct
    rw = d // r
    outs = [shape((t, d), BF16)] * 2 + [shape((rw, c), F32)] * 4 + [shape((rw, f), F32)] * 2
    outs += [shape((1, n * f), F32), shape((5, d), F32)] + [shape((d, ns), F32)] * 4 + [shape((2, d), F32)]
    values = [v if v.ndim == 2 else v.reshape(1, -1) for v in args]
    vmem, any_space = pl.BlockSpec(memory_space=pltpu.VMEM), pl.BlockSpec(memory_space=pl.ANY)
    sems = pltpu.SemaphoreType.DMA((plan_semaphores(plan),))
    got = pl.pallas_call(
        functools.partial(layer_kernel, plan),
        out_shape=outs,
        in_specs=[any_space if k in LARGE else vmem for k in INPUTS],
        out_specs=[vmem] * len(outs),
        scratch_shapes=[pltpu.VMEM(s, k) for _, s, k in names(plan)] + [sems, sems],
        compiler_params=pltpu.CompilerParams(
            collective_id=0, has_side_effects=True, vmem_limit_bytes=60 << 20
        ),
    )(*values)
    out, tok, q, k, v, o, up, dn, ub, vec, dec, mix, km, vm, skip = got
    return (
        out, tok, q, k, v, o, up, ub[0], dn, vec[0], vec[1], vec[2], vec[3], vec[4],
        dec, mix, km, vm, skip[0], skip[1],
    )


def plan_semaphores(plan):
    y, x, z = plan["Y"] - 1, plan["X"] - 1, plan["Z"]
    gathers = 6 + plan["L"] // BLK
    return 12 + gathers * (2 * y + 1) + 3 * (2 * y + 1) + 3 * (x * z + z - 1) + plan["R"].bit_length()


def solution(mesh):
    both, row, col = P(("rows", "chan"), None), P("rows", None), P(None, "chan")
    state = P("chan", None)
    in_specs = (
        both, both, row, col, col, col, col, col, P("chan"), col,
        P(), P(), P(), P(), P(), state, state, state, state, P("chan"), P("chan"),
    )
    grid = P("rows", "chan")
    out_specs = (both, both, grid, grid, grid, grid, grid, P(), grid) + (P(),) * 11
    return jax.shard_map(shards, mesh=mesh, in_specs=in_specs, out_specs=out_specs, check_vma=False)
```

```python
import functools
import math

import jax
import jax.numpy as jnp
from jax import lax
from jax.experimental import pallas as pl
from jax.experimental.pallas import tpu as pltpu
from jax.sharding import PartitionSpec as P

HEAD = 128
CTX = 128
BLK = 512
TILE = 256
EPS = 1e-05
NEG = -1e30
F32 = jnp.float32
BF16 = jnp.bfloat16
NN = (((1,), (0,)), ((), ()))
NT = (((1,), (1,)), ((), ()))
TN = (((0,), (0,)), ((), ()))
ROOT = math.sqrt(2.0 / math.pi)
MESH = pl.DeviceIdType.MESH


def dot(left, right, dims=NN):
    return lax.dot_general(left, right, dims, preferred_element_type=F32)


def at(start, size):
    if isinstance(start, int):
        return pl.ds(start, size)
    return pl.ds(pl.multiple_of(start, math.gcd(size, 1024)), size)


def ssm_params(rate_ref, in_ref, key_ref, value_ref):
    rate = rate_ref[...]
    a = jnp.exp(-rate)
    s = jnp.sqrt(1.0 - a * a)
    return dict(rate=rate, a=a, s=s, mix=in_ref[...], km=key_ref[...], vm=value_ref[...])


def ssm_forward(x_ref, seg_ref, par, skip_k, skip_v, ck_ref, cv_ref, wide_k, wide_v, keep_ref):
    a, rate = par["a"], par["rate"]
    b = par["s"] * par["mix"]
    kb, vb = par["km"] * b, par["vm"] * b
    a128, d128 = jnp.exp(-128.0 * rate), 128.0 * jnp.exp(-127.0 * rate)
    first = BLK - CTX
    parts = first // 128
    mask = segment_mask(seg_ref)
    row = lax.broadcasted_iota(jnp.int32, (8, 1), 0)
    zero = jnp.zeros(a.shape, F32)

    def step(i, carry):
        out = []
        for j in range(parts):
            g, e = carry[j]
            base = pl.multiple_of(j * 128 + i * 8, 8)
            x8 = jnp.where(mask(row + base), x_ref[pl.ds(base, 8), :], 0.0)
            for t in range(8):
                e = a * e + g
                g = a * g + x8[t : t + 1, :]
            out.append((g, e))
        return tuple(out)

    ends = lax.fori_loop(0, 16, step, tuple((zero, zero) for _ in range(parts)))
    g, e = ends[0]
    for j in range(1, parts):
        e = ends[j][1] + a128 * e + d128 * g
        g = ends[j][0] + a128 * g
    keep_ref[0] = g

    def ahead(i, g):
        base = pl.multiple_of(first + i * 8, 8)
        raw = x_ref[pl.ds(base, 8), :]
        x8 = jnp.where(mask(row + base), raw, 0.0)
        ks, vs = [], []
        for t in range(8):
            g = a * g + x8[t : t + 1, :]
            keep_ref[i * 8 + t + 1] = g
            ks.append(jnp.sum(g * kb, axis=0, keepdims=True))
            vs.append(jnp.sum(g * vb, axis=0, keepdims=True))
        rows = pl.ds(pl.multiple_of(i * 8, 8), 8)
        wide_k[rows, :] = jnp.concatenate(ks, axis=0) + skip_k * raw
        wide_v[rows, :] = jnp.concatenate(vs, axis=0) + skip_v * raw
        return g

    lax.fori_loop(0, CTX // 8, ahead, g)
    ck_ref[...] = wide_k[...].astype(BF16)
    cv_ref[...] = wide_v[...].astype(BF16)
    return e


def segment_mask(seg_ref):
    segs = seg_ref[...]
    first = jnp.sum(jnp.where(segs < segs[:, BLK : BLK + 1], 1, 0), axis=1, keepdims=True)
    return lambda index: index >= first


def ssm_backward(x_ref, seg_ref, par, skip_k, skip_v, gk_ref, gv_ref, keep_ref, e0, gx_ref, small_ref):
    a, s, km, vm = par["a"], par["s"], par["km"], par["vm"]
    b = s * par["mix"]
    first = BLK - CTX
    mask = segment_mask(seg_ref)
    row = lax.broadcasted_iota(jnp.int32, (8, 1), 0)
    zero = jnp.zeros(a.shape, F32)

    def back(j, carry):
        lam, sk, sv, sx, sg = carry
        i = CTX // 8 - 1 - j
        base = pl.multiple_of(first + i * 8, 8)
        rows = pl.ds(pl.multiple_of(i * 8, 8), 8)
        inside = mask(row + base)
        x8 = jnp.where(inside, x_ref[pl.ds(base, 8), :], 0.0)
        k8, v8 = gk_ref[rows, :], gv_ref[rows, :]
        outs = [None] * 8
        for t in reversed(range(8)):
            kt, vt = k8[t : t + 1, :], v8[t : t + 1, :]
            lam = a * lam + km * kt + vm * vt
            now = keep_ref[i * 8 + t + 1]
            sk = sk + now * kt
            sv = sv + now * vt
            sx = sx + lam * x8[t : t + 1, :]
            sg = sg + lam * keep_ref[i * 8 + t]
            outs[t] = jnp.sum(lam * b, axis=0, keepdims=True)
        gx = jnp.where(inside, jnp.concatenate(outs, axis=0), 0.0)
        gx_ref[pl.ds(base, 8), :] = gx + skip_k * k8 + skip_v * v8
        return (lam, sk, sv, sx, sg)

    lam, sk, sv, sx, sg = lax.fori_loop(0, CTX // 8, back, (zero,) * 5)
    sx = sx + lam * (a * keep_ref[0])
    sg = sg + lam * (a * e0)
    ns = a.shape[0]
    small_ref[0:ns, :] = (a * a / s) * par["mix"] * sx - a * b * sg
    small_ref[ns : 2 * ns, :] = s * sx
    small_ref[2 * ns : 3 * ns, :] = sk * b
    small_ref[3 * ns : 4 * ns, :] = sv * b

    def tail(j, w):
        base = pl.multiple_of(first - 8 - j * 8, 8)
        outs = [None] * 8
        for t in reversed(range(8)):
            w = a * w
            outs[t] = jnp.sum(w, axis=0, keepdims=True)
        gx_ref[pl.ds(base, 8), :] = jnp.where(mask(row + base), jnp.concatenate(outs, axis=0), 0.0)
        return w

    lax.fori_loop(0, first // 8, tail, lam * b)
    raw = x_ref[first:BLK, :]
    small_ref[4 * ns : 4 * ns + 1, :] = jnp.sum(gk_ref[...] * raw, axis=0, keepdims=True)
    small_ref[4 * ns + 1 : 4 * ns + 2, :] = jnp.sum(gv_ref[...] * raw, axis=0, keepdims=True)


def tile_masks(seg_ref, block, tile):
    width = (tile + 1) * TILE
    segs = seg_ref[...]
    index = lax.broadcasted_iota(jnp.int32, (TILE, 1), 0) + (block * BLK + tile * TILE)
    own_id = jnp.zeros((TILE, 1), jnp.int32)
    for value in (1, 2, 3):
        below = jnp.sum(jnp.where(segs < value, 1, 0), axis=1, keepdims=True)
        own_id = own_id + jnp.where(index >= below, 1, 0)
    keys = segs[:, block * BLK : block * BLK + width]
    column = lax.broadcasted_iota(jnp.int32, (TILE, width), 1) + block * BLK
    own = (own_id == keys) & (column <= index)
    if block == 0:
        return own, None
    return own, own_id == segs[:, block * BLK - CTX : block * BLK]


def attn_forward(block, q_ref, k_ref, v_ref, ck_ref, cv_ref, seg_ref, store, lse_ref):
    scale = HEAD**-0.5
    for tile in range(BLK // TILE):
        own, ctx = tile_masks(seg_ref, block, tile)
        rows = pl.ds(block * BLK + tile * TILE, TILE)
        keys = pl.ds(block * BLK, (tile + 1) * TILE)
        for head in range(q_ref.shape[1] // HEAD):
            cols = pl.ds(head * HEAD, HEAD)
            q = q_ref[rows, cols]
            s = jnp.where(own, dot(q, k_ref[keys, cols], NT) * scale, NEG)
            top = jnp.max(s, axis=1, keepdims=True)
            if ctx is not None:
                sc = jnp.where(ctx, dot(q, ck_ref[:, cols], NT) * scale, NEG)
                top = jnp.maximum(top, jnp.max(sc, axis=1, keepdims=True))
            p = jnp.exp(s - top)
            total = jnp.sum(p, axis=1, keepdims=True)
            if ctx is not None:
                pc = jnp.exp(sc - top)
                total = total + jnp.sum(pc, axis=1, keepdims=True)
            lse_ref[head, rows, :] = top + jnp.log(total)
            inverse = 1.0 / total
            out = dot((p * inverse).astype(BF16), v_ref[keys, cols])
            if ctx is not None:
                out = out + dot((pc * inverse).astype(BF16), cv_ref[:, cols])
            store(rows, head, out.astype(BF16))


def attn_backward(
    block, q_ref, k_ref, v_ref, ck_ref, cv_ref, seg_ref, lse_ref, do_ref,
    gq_ref, gk_ref, gv_ref, gck_ref, gcv_ref, ak_ref, av_ref,
):
    scale = HEAD**-0.5
    base = block * BLK
    for tile in range(BLK // TILE):
        own, ctx = tile_masks(seg_ref, block, tile)
        width = (tile + 1) * TILE
        rows, keys = pl.ds(base + tile * TILE, TILE), pl.ds(base, width)
        for head in range(q_ref.shape[1] // HEAD):
            cols = pl.ds(head * HEAD, HEAD)
            q, k, v = q_ref[rows, cols], k_ref[keys, cols], v_ref[keys, cols]
            do = do_ref[tile * TILE : (tile + 1) * TILE, cols]
            lse = lse_ref[head, rows, :]
            p = jnp.exp(jnp.where(own, dot(q, k, NT) * scale, NEG) - lse)
            dp = dot(do, v, NT)
            weighted = jnp.sum(p * dp, axis=1, keepdims=True)
            if ctx is not None:
                kc, vc = ck_ref[:, cols], cv_ref[:, cols]
                pc = jnp.exp(jnp.where(ctx, dot(q, kc, NT) * scale, NEG) - lse)
                dpc = dot(do, vc, NT)
                weighted = weighted + jnp.sum(pc * dpc, axis=1, keepdims=True)
            ds = (p * (dp - weighted)).astype(BF16)
            gq = dot(ds, k)
            gk = dot(ds, q, TN)
            gv = dot(p.astype(BF16), do, TN)
            half = tile * TILE
            if tile > 0:
                ak_ref[0:half, cols] = ak_ref[0:half, cols] + gk[0:half, :]
                av_ref[0:half, cols] = av_ref[0:half, cols] + gv[0:half, :]
            ak_ref[half:width, cols] = gk[half:width, :]
            av_ref[half:width, cols] = gv[half:width, :]
            if ctx is not None:
                dsc = (pc * (dpc - weighted)).astype(BF16)
                gq = gq + dot(dsc, kc)
                gkc = dot(dsc, q, TN) * scale
                gvc = dot(pc.astype(BF16), do, TN)
                if tile > 0:
                    gkc = gkc + gck_ref[:, cols]
                    gvc = gvc + gcv_ref[:, cols]
                gck_ref[:, cols] = gkc
                gcv_ref[:, cols] = gvc
            gq_ref[rows, cols] = (gq * scale).astype(BF16)
    gk_ref[base : base + BLK, :] = (ak_ref[...] * scale).astype(BF16)
    gv_ref[base : base + BLK, :] = av_ref[...].astype(BF16)


def normalize(values):
    centered = values - jnp.mean(values, axis=-1, keepdims=True)
    inverse = lax.rsqrt(jnp.mean(centered * centered, axis=-1, keepdims=True) + EPS)
    return centered * inverse, inverse


def norm_back(grad, hat, inverse, gain):
    u = grad * gain
    return inverse * (
        u - jnp.mean(u, axis=-1, keepdims=True) - hat * jnp.mean(u * hat, axis=-1, keepdims=True)
    )


class Links:
    def __init__(self, plan, send, recv):
        self.plan, self.send, self.recv, self.used = plan, send, recv, 0
        self.chan, self.rows = lax.axis_index("chan"), lax.axis_index("rows")
        self.core = lax.rem(self.chan, 2)
        self.y = self.chan // 2
        self.mate = self.other(self.chan)
        self.x = lax.rem(self.rows, plan["X"])
        self.z = self.rows // plan["X"]

    def far(self, j):
        count = self.plan["Y"]
        return 2 * lax.rem(self.y + count + j, count) + self.core

    def other(self, chan):
        return chan + 1 - 2 * lax.rem(chan, 2)

    def put(self, source, target, **device):
        i = self.used
        self.used += 1
        copy = pltpu.make_async_remote_copy(
            src_ref=source, dst_ref=target, send_sem=self.send.at[i], recv_sem=self.recv.at[i],
            device_id=device, device_id_type=MESH,
        )
        copy.start()
        return copy

    def load(self, source, target):
        i = self.used
        self.used += 1
        copy = pltpu.make_async_copy(source, target, self.send.at[i])
        copy.start()
        return copy

    def enter(self):
        barrier = pltpu.get_barrier_semaphore()
        plan = self.plan
        partners = [{"chan": self.mate}]
        for j in range(1, plan["Y"]):
            partners += [{"chan": self.far(j)}, {"chan": self.other(self.far(j))}]
        partners += [{"rows": self.row_of(self.z, self.x + i)} for i in range(1, plan["X"])]
        partners += [{"rows": self.row_of(self.z + i, self.x)} for i in range(1, plan["Z"])]
        for partner in partners:
            pl.semaphore_signal(barrier, inc=1, device_id=partner, device_id_type=MESH)
        return lambda: pl.semaphore_wait(barrier, len(partners))

    def row_of(self, z, x):
        return lax.rem(z, self.plan["Z"]) * self.plan["X"] + lax.rem(x, self.plan["X"])


class Gather:
    def __init__(self, links, view):
        self.links, self.view = links, view
        own = view(links.chan)
        count = range(1, links.plan["Y"])
        self.direct = [links.put(own, own, chan=links.far(j)) for j in count]
        self.near = links.put(own, own, chan=links.mate)
        self.passed = []

    def forward(self):
        links = self.links
        for j, copy in enumerate(self.direct, 1):
            copy.wait_recv()
            shard = self.view(links.far(-j))
            self.passed.append(links.put(shard, shard, chan=links.mate))

    def finish(self):
        self.near.wait()
        for copy in self.passed:
            copy.wait()
        for copy in self.direct:
            copy.wait_send()


class SlabGather:
    def __init__(self, links, whole, width):
        self.links, self.whole, self.width = links, whole, width
        plan = links.plan
        self.size = whole.shape[0] // plan["R"]
        own = self.view(links.rows * self.size, self.size, links.chan)
        self.over_y = [links.put(own, own, chan=links.far(j)) for j in range(1, plan["Y"])]
        column = whole.at[:, at(links.chan * width, width)]
        self.near = links.put(column, column, chan=links.mate)

    def view(self, start, size, chan):
        return self.whole.at[at(start, size), at(chan * self.width, self.width)]

    def spread_x(self):
        links, plan = self.links, self.links.plan
        self.over_x = []
        for j, copy in enumerate(self.over_y, 1):
            copy.wait_recv()
            slab = self.view(links.rows * self.size, self.size, links.far(-j))
            for i in range(1, plan["X"]):
                self.over_x.append(links.put(slab, slab, rows=links.row_of(links.z, links.x + i)))

    def spread_z(self):
        links, plan = self.links, self.links.plan
        self.over_z = []
        for copy in self.over_x:
            copy.wait_recv()
        group = plan["X"] * self.size
        for j in range(1, plan["Y"]):
            slab = self.view(links.z * group, group, links.far(-j))
            for i in range(1, plan["Z"]):
                self.over_z.append(links.put(slab, slab, rows=links.row_of(links.z + i, links.x)))

    def forward(self):
        links, plan = self.links, self.links.plan
        for copy in self.over_z:
            copy.wait_recv()
        self.passed = []
        for j in range(1, plan["Y"]):
            column = self.whole.at[:, at(links.far(-j) * self.width, self.width)]
            self.passed.append(links.put(column, column, chan=links.mate))

    def finish(self):
        self.near.wait()
        for copy in self.passed:
            copy.wait()
        for copy in self.over_y + self.over_x + self.over_z:
            copy.wait_send()


class Scatter:
    def __init__(self, links, mixed_out, mixed_in, far_out, far_in, near_out, near_in):
        self.links = links
        self.mixed_out, self.mixed_in, self.far_out, self.far_in = mixed_out, mixed_in, far_out, far_in
        self.near_out, self.near_in = near_out, near_in
        self.mix, self.direct = [], []

    def for_mate(self, j, value):
        self.mixed_out[j - 1] = value.astype(BF16)
        self.mix.append(
            self.links.put(self.mixed_out.at[j - 1], self.mixed_in.at[j - 1], chan=self.links.mate)
        )

    def for_far(self, j, value):
        self.mix[j - 1].wait_recv()
        self.far_out[j - 1] = (value + self.mixed_in[j - 1].astype(F32)).astype(BF16)

    def send_far(self, j):
        links = self.links
        self.direct.append(
            links.put(self.far_out.at[j - 1], self.far_in.at[j - 1], chan=links.far(j))
        )

    def for_near(self, value):
        self.near_out[...] = value.astype(BF16)
        self.near = self.links.put(self.near_out, self.near_in, chan=self.links.mate)

    def total(self, own):
        self.near.wait()
        own = own + self.near_in[...].astype(F32)
        for j, copy in enumerate(self.direct):
            copy.wait()
            own = own + self.far_in[j].astype(F32)
        for copy in self.mix:
            copy.wait_send()
        return own


class RowScatter:
    def __init__(self, links, stage, x_in, z_in):
        self.links, self.stage, self.x_in, self.z_in = links, stage, x_in, z_in
        self.first, self.second = {}, []

    def slab(self, z, x):
        size = self.x_in.shape[2]
        return pl.ds(pl.multiple_of(self.links.row_of(z, x) * size, size), size)

    def compute(self, left, right):
        links, plan = self.links, self.links.plan
        size = plan["X"] * self.x_in.shape[2]
        for step in range(1, plan["Z"] + 1):
            rows = at(lax.rem(links.z + step, plan["Z"]) * size, size)
            self.stage[rows, :] = dot(left[:, rows], right[...], TN).astype(BF16)
            for i in range(1, plan["X"]):
                self.first[step, i] = links.put(
                    self.stage.at[self.slab(links.z + step, links.x + i)],
                    self.x_in.at[i - 1, step - 1],
                    rows=links.row_of(links.z, links.x + i),
                )

    def mixed(self, step):
        links, plan = self.links, self.links.plan
        value = self.stage[self.slab(links.z + step, links.x), :].astype(F32)
        for i in range(1, plan["X"]):
            self.first[step, i].wait()
            value = value + self.x_in[i - 1, step - 1].astype(F32)
        return value

    def over_z(self, *steps):
        links, plan = self.links, self.links.plan
        for step in steps or range(1, plan["Z"]):
            slab = self.slab(links.z + step, links.x)
            self.stage[slab, :] = self.mixed(step).astype(BF16)
            self.second.append(
                links.put(
                    self.stage.at[slab], self.z_in.at[step - 1],
                    rows=links.row_of(links.z + step, links.x),
                )
            )

    def total(self):
        value = self.mixed(self.links.plan["Z"])
        for i, copy in enumerate(self.second):
            copy.wait()
            value = value + self.z_in[i].astype(F32)
        return value


class Doubling:
    def __init__(self, links, block, out, got):
        self.links, self.block, self.out, self.got, self.step = links, block, out, got, 0

    def begin(self):
        step, rows = self.step, self.links.rows
        self.out[step] = self.block[...]
        bit = 1 << step
        partner = rows + bit - 2 * bit * lax.rem(rows // bit, 2)
        self.copy = self.links.put(self.out.at[step], self.got.at[step], rows=partner)

    def end(self):
        self.copy.wait()
        self.block[...] = self.block[...] + self.got[self.step]
        self.step += 1


def names(plan):
    n, length, d, t, c, f = (plan[k] for k in ("n", "L", "D", "T", "C", "F"))
    far = plan["Y"] - 1
    x1, z, rw = plan["X"] - 1, plan["Z"], plan["RW"]
    grid = (length, d)
    out = [("tok", grid, BF16), ("h1", grid, BF16), ("cot", grid, BF16), ("wout", (d, d), BF16)]
    out += [("attn", grid, BF16), ("h2", grid, BF16), ("act", (length, f), BF16), ("gpre", (length, f), BF16)]
    out += [("wqkv", (d, 3 * c), BF16), ("wup", (d, f), BF16), ("wdn", (d, f), BF16)]
    out += [("qkv", (length, 3 * c), BF16), ("tk", (t, d), BF16), ("gb", (length, c), BF16)]
    out += [("ck", (CTX, c), BF16), ("cv", (CTX, c), BF16), ("gck", (CTX, c), F32), ("gcv", (CTX, c), F32)]
    out += [("lse", (c // HEAD, length, 1), F32), ("xs", (BLK, c), F32), ("gx", (BLK, c), F32)]
    out += [("keep", (CTX + 1, plan["NS"], c), F32), ("ak", (BLK, c), F32), ("av", (BLK, c), F32)]
    out += [("do", (BLK, c), BF16), ("r2own", (t, d), F32), ("p", (BLK, d), F32)]
    out += [("acc", (t, d), F32), ("ffn", (t, d), F32)]
    for s in ("a", "b"):
        out += [(s + part, (far, t, d), BF16) for part in ("_mo", "_mi", "_fo", "_fi")]
        out += [(s + part, (t, d), BF16) for part in ("_no", "_ni")]
    out += [("stage", (d, f), BF16), ("ostage", (d, c), BF16)]
    for s, w in (("up", f), ("dn", f), ("qk", 3 * c), ("ou", c)):
        out += [(s + "_xi", (x1, z, rw, w), BF16), (s + "_zi", (z - 1, rw, w), BF16)]
    steps = plan["R"].bit_length() - 1
    block = (plan["SM"], c)
    out += [("small", block, F32), ("smallin", (steps,) + block, F32), ("smallout", (steps,) + block, F32)]
    out += [("fx", (plan["X"], 8, d), F32), ("fz", (z, 8, d), F32), ("fc", (n, 8, d), F32)]
    return out


INPUTS = (
    "tokens", "cotangent", "segments", "w_query", "w_key", "w_value", "w_out", "w_up", "up_bias", "w_down",
    "down_bias", "norm1_gain", "norm1_bias", "norm2_gain", "norm2_bias", "decay_rates", "input_mix",
    "key_mix", "value_mix", "key_skip", "value_skip",
)
LARGE = (
    "tokens", "cotangent", "w_query", "w_key", "w_value", "w_out", "w_up", "w_down",
)
STATES = ("decay_rates", "input_mix", "key_mix", "value_mix")


class Box:
    def __init__(self, **items):
        self.__dict__.update(items)


def colsum(value):
    return jnp.sum(value, axis=0, keepdims=True)


def layer_kernel(plan, *refs):
    i = Box(**dict(zip(INPUTS, refs[:21])))
    o_out, o_tok, o_w4, o_up, o_dn, o_small, o_last = refs[21:28]
    scratch = refs[28:]
    s = Box(**dict(zip([x[0] for x in names(plan)], scratch)))
    links = Links(plan, scratch[-2], scratch[-1])
    n, length, d, t, c, f = (plan[k] for k in ("n", "L", "D", "T", "C", "F"))
    far = range(1, plan["Y"])
    here, mate, core = links.chan, links.mate, links.core
    pair = 2 * t
    own_rows, own_cols = at(here * t, t), at(here * c, c)
    own_part, mate_part = at(core * t, t), at((1 - core) * t, t)
    rows_of = lambda owner: at(owner * t, t)
    chip_rows = lambda owner: at(owner // 2 * pair, pair)
    q_ref, k_ref, v_ref = (s.qkv.at[:, e * c : (e + 1) * c] for e in range(3))

    ready = links.enter()
    got_tok = links.load(i.tokens, s.tok.at[own_rows])
    got_out = links.load(i.w_out, s.wout.at[:, own_cols])
    got_w = [
        links.load(w, s.wqkv.at[:, e * c : (e + 1) * c])
        for e, w in enumerate((i.w_query, i.w_key, i.w_value))
    ]
    got_cot = links.load(i.cotangent, s.cot.at[own_rows])
    got_up, got_dn = links.load(i.w_up, s.wup), links.load(i.w_down, s.wdn)
    got_own = links.load(i.tokens, s.tk)
    par = ssm_params(i.decay_rates, i.input_mix, i.key_mix, i.value_mix)
    got_tok.wait()
    got_out.wait()
    ready()
    out_gather = SlabGather(links, s.wout, c)
    tok_gather = Gather(links, lambda o: s.tok.at[rows_of(o)])
    out_gather.spread_x()

    def project(rows):
        hat, _ = normalize(s.tok[rows, :].astype(F32))
        s.h1[rows, :] = (hat * i.norm1_gain[...] + i.norm1_bias[...]).astype(BF16)
        s.qkv[rows, :] = dot(s.h1[rows, :], s.wqkv[...]).astype(BF16)

    for got in got_w:
        got.wait()
    project(own_rows)
    out_gather.spread_z()
    tok_gather.near.wait_recv()
    project(rows_of(mate))
    got_cot.wait()
    half = t // 2
    cot_views = [lambda o, e=e: s.cot.at[at(o * t + e * half, half)] for e in range(2)]
    tok_gather.forward()
    cot_gathers = [Gather(links, cot_views[0])]
    for j in far:
        project(rows_of(links.far(-j)))
    for j, copy in zip(far, tok_gather.passed):
        copy.wait_recv()
        project(rows_of(links.other(links.far(-j))))
    tok_gather.near.wait_send()
    for copy in tok_gather.passed + tok_gather.direct:
        copy.wait_send()

    def store(rows, head, value):
        s.attn[rows, at(here * c + head * HEAD, HEAD)] = value

    attn_gathers = []

    def attend(block):
        attn_forward(block, q_ref, k_ref, v_ref, s.ck, s.cv, i.segments, store, s.lse)
        attn_gathers.append(
            Gather(links, lambda o: s.attn.at[pl.ds(block * BLK, BLK), at(o * c, c)])
        )

    attend(0)
    s.xs[...] = s.h1[0:BLK, own_cols].astype(F32)
    skip_k, skip_v = i.key_skip[...], i.value_skip[...]
    e0 = ssm_forward(s.xs, i.segments, par, skip_k, skip_v, s.ck, s.cv, s.gck, s.gcv, s.keep)
    cot_gathers[0].forward()
    attend(1)
    cot_gathers.append(Gather(links, cot_views[1]))
    out_gather.forward()
    attn_gathers[0].forward()
    got_up.wait()
    got_dn.wait()
    out_gather.finish()

    wide = 512

    def loop(count, body):
        def step(e, carry):
            body(at(e * wide, wide))
            return carry

        lax.fori_loop(0, count // wide, step, 0)

    def feed(block):
        rows = pl.ds(block * BLK, BLK)

        def residual(cols):
            s.p[:, cols] = s.tok[rows, cols].astype(F32) + dot(s.attn[rows, :], s.wout[:, cols])

        loop(d, residual)
        hat, _ = normalize(s.p[...])
        s.h2[rows, :] = (hat * i.norm2_gain[...] + i.norm2_bias[...]).astype(BF16)

        @pl.when(here * t // BLK == block)
        def _():
            s.r2own[...] = s.p[at(lax.rem(here * t, BLK), t), :]

        def hidden(cols):
            v = dot(s.h2[rows, :], s.wup[:, cols]) + i.up_bias[:, cols]
            square = v * v
            th = jnp.tanh(ROOT * (v + 0.044715 * (square * v)))
            part = 0.5 * (1.0 + th)
            s.act[rows, cols] = (v * part).astype(BF16)
            slope = part + 0.5 * v * (1.0 - th * th) * (ROOT * (1.0 + 0.134145 * square))
            s.gpre[rows, cols] = slope.astype(BF16)

        loop(f, hidden)

    attn_gathers[0].finish()
    feed(0)
    attn_gathers[1].forward()
    cot_gathers[1].forward()
    attn_gathers[1].finish()
    feed(1)
    for gather in cot_gathers:
        gather.finish()

    def rows_sum(k, stage):
        return RowScatter(links, stage, getattr(s, k + "_xi"), getattr(s, k + "_zi"))

    down_sum = rows_sum("dn", s.stage)
    down_sum.compute(s.cot, s.act)

    def slope_grad(owner):
        rows = chip_rows(owner)

        def part(cols):
            grad = dot(s.cot[rows, :], s.wdn[:, cols])
            s.gpre[rows, cols] = (grad * s.gpre[rows, cols].astype(F32)).astype(BF16)

        loop(f, part)

    def back(owner, source, weight):
        rows = chip_rows(owner)

        def part(cols):
            s.p[0:pair, cols] = dot(source[rows, :], weight[cols, :], NT)

        loop(d, part)

    scatter = lambda k: Scatter(links, *(getattr(s, k + x) for x in ("_mo", "_mi", "_fo", "_fi", "_no", "_ni")))
    grad2 = scatter("a")
    for j in far:
        slope_grad(links.far(j))
        back(links.far(j), s.gpre, s.wup)
        grad2.for_mate(j, s.p[mate_part, :])
        if j == plan["Y"] - 1:
            slope_grad(here)
        grad2.for_far(j, s.p[own_part, :])
        grad2.send_far(j)
    back(here, s.gpre, s.wup)
    grad2.for_near(s.p[mate_part, :])
    s.acc[...] = s.p[own_part, :]
    ffn = scatter("b")
    for j in far:
        back(links.far(j), s.act, s.wdn)
        ffn.for_mate(j, s.p[mate_part, :])
        ffn.for_far(j, s.p[own_part, :])
    back(here, s.act, s.wdn)
    ffn.for_near(s.p[mate_part, :])
    s.ffn[...] = s.p[own_part, :]
    up_sum = rows_sum("up", s.act)
    up_sum.compute(s.h2, s.gpre)

    base = 4 * plan["NS"] + 2
    bias_rows = f // c
    for e in range(bias_rows):
        s.small[base + e : base + e + 1, :] = colsum(s.gpre[:, e * c : (e + 1) * c].astype(F32))
    base += bias_rows

    def keep_vector(k, value):
        for e in range(n):
            s.small[base + k * n + e : base + k * n + e + 1, :] = value[:, e * c : (e + 1) * c]

    grad_hidden2 = grad2.total(s.acc[...])
    hat2, inv2 = normalize(s.r2own[...])
    own_cot = s.cot[own_rows, :].astype(F32)
    s.acc[...] = own_cot + norm_back(grad_hidden2, hat2, inv2, i.norm2_gain[...])
    s.tok[own_rows, :] = s.acc[...].astype(BF16)
    branch_gather = Gather(links, lambda o: s.tok.at[rows_of(o)])
    keep_vector(0, colsum(own_cot))
    keep_vector(1, colsum(grad_hidden2 * hat2))
    keep_vector(2, colsum(grad_hidden2))
    down_sum.over_z()
    branch_gather.forward()
    branch_gather.finish()
    for j in far:
        ffn.send_far(j)

    def attend_back(block):
        s.do[...] = dot(s.tok[block * BLK : (block + 1) * BLK, :], s.wout[own_cols, :], NT).astype(BF16)
        attn_backward(
            block, q_ref, k_ref, v_ref, s.ck, s.cv, i.segments, s.lse, s.do,
            q_ref, k_ref, v_ref, s.gck, s.gcv, s.ak, s.av,
        )

    attend_back(1)
    ssm_backward(s.xs, i.segments, par, skip_k, skip_v, s.gck, s.gcv, s.keep, e0, s.gx, s.small)
    steps = plan["R"].bit_length() - 1
    doubling = Doubling(links, s.small, s.smallout, s.smallin)
    doubling.begin()
    attend_back(0)

    def input_back(owner):
        rows = chip_rows(owner)

        def part(cols):
            s.p[0:pair, cols] = dot(s.qkv[rows, :], s.wqkv[cols, :], NT)

        loop(d, part)

        @pl.when(owner // 2 * pair < BLK)
        def _():
            s.p[0:pair, own_cols] = s.p[0:pair, own_cols] + s.gx[rows, :].astype(BF16).astype(F32)

    grad1 = scatter("a")
    qkv_sum = rows_sum("qk", s.h2.at[:, 0 : 3 * c])
    for j in far:
        input_back(links.far(j))
        grad1.for_mate(j, s.p[mate_part, :])
        if j == 1:
            qkv_sum.compute(s.h1, s.qkv)
        grad1.for_far(j, s.p[own_part, :])
        grad1.send_far(j)
    doubling.end()
    doubling.begin()
    input_back(here)
    grad1.for_near(s.p[mate_part, :])
    s.gb[...] = s.tok[:, own_cols]
    out_sum = rows_sum("ou", s.ostage)
    out_sum.compute(s.attn, s.gb)
    up_sum.over_z()
    for step in range(1, steps):
        doubling.end()
        if step < steps - 1:
            doubling.begin()
    o_small[here] = s.small[...]
    small_gather = Gather(links, lambda o: o_small.at[o])
    o_dn[...] = down_sum.total()
    qkv_sum.over_z()
    out_sum.over_z()
    o_up[...] = up_sum.total()
    o_out[...] = (s.r2own[...] + ffn.total(s.ffn[...]) + i.down_bias[...]).astype(BF16)

    got_own.wait()
    hat1, inv1 = normalize(s.tk[...].astype(F32))
    grad_hidden1 = grad1.total(s.p[own_part, :])
    o_tok[...] = (s.acc[...] + norm_back(grad_hidden1, hat1, inv1, i.norm1_gain[...])).astype(BF16)
    s.fx[links.x, 0:1, :] = colsum(grad_hidden1 * hat1)
    s.fx[links.x, 1:2, :] = colsum(grad_hidden1)
    s.fx[links.x, 2:8, :] = jnp.zeros((6, d), F32)

    def spread(slots, own, targets):
        return [links.put(slots.at[own], slots.at[own], **target) for target in targets]

    hops = spread(s.fx, links.x, [{"rows": links.row_of(links.z, links.x + e)} for e in range(1, plan["X"])])
    small_gather.forward()
    for hop in hops:
        hop.wait()
    s.fz[links.z] = sum([s.fx[e] for e in range(1, plan["X"])], s.fx[0])
    hops = spread(s.fz, links.z, [{"rows": links.row_of(links.z + e, links.x)} for e in range(1, plan["Z"])])
    small_gather.finish()
    for hop in hops:
        hop.wait()
    s.fc[here] = sum([s.fz[e] for e in range(1, plan["Z"])], s.fz[0])
    group = [mate] + [links.far(j) for j in far] + [links.other(links.far(j)) for j in far]
    hops = spread(s.fc, here, [{"chan": e} for e in group])
    o_w4[:, 3 * c : 4 * c] = out_sum.total()
    o_w4[:, 0 : 3 * c] = qkv_sum.total()
    for hop in hops:
        hop.wait()
    o_last[...] = sum([s.fc[e] for e in range(1, n)], s.fc[0])


def finish_kernel(plan, *refs):
    out, tok, w4, up, dn, small, last = refs[:7]
    o_out, o_tok, o_q, o_k, o_v, o_o, o_up, o_ub, o_dn, o_db, o_g1, o_b1, o_g2, o_b2 = refs[7:21]
    o_dec, o_in, o_km, o_vm, o_ks, o_vs, sem = refs[21:]
    n, c, f, ns = (plan[k] for k in ("n", "C", "F", "NS"))
    moves = [(out, o_out), (tok, o_tok), (up, o_up), (dn, o_dn)]
    moves += [(w4.at[:, e * c : (e + 1) * c], o) for e, o in enumerate((o_q, o_k, o_v, o_o))]
    copies = [pltpu.make_async_copy(a, b, sem.at[e]) for e, (a, b) in enumerate(moves)]
    for copy in copies:
        copy.start()
    bias_rows = f // c
    base = 4 * ns + 2 + bias_rows
    for e in range(n):
        cols = slice(e * c, (e + 1) * c)
        for k, target in enumerate((o_dec, o_in, o_km, o_vm)):
            target[:, cols] = small[e, k * ns : (k + 1) * ns, :]
        o_ks[:, cols] = small[e, 4 * ns : 4 * ns + 1, :]
        o_vs[:, cols] = small[e, 4 * ns + 1 : 4 * ns + 2, :]
        for b in range(bias_rows):
            o_ub[:, e * f + b * c : e * f + (b + 1) * c] = small[e, 4 * ns + 2 + b : 4 * ns + 3 + b, :]
        for k, target in enumerate((o_db, o_g2, o_b2)):
            row = base + k * n + e
            target[:, cols] = sum([small[g, row : row + 1, :] for g in range(1, n)], small[0, row : row + 1, :])
    o_g1[...] = last[0:1, :]
    o_b1[...] = last[1:2, :]
    for copy in copies:
        copy.wait()


def shards(*args):
    a = dict(zip(INPUTS, args))
    n, r = lax.axis_size("chan"), lax.axis_size("rows")
    t, d = a["tokens"].shape
    c, f = a["w_query"].shape[1], a["w_up"].shape[1]
    ns = a["decay_rates"].shape[1]
    x = math.isqrt(r // 2)
    small = 4 * ns + 2 + f // c + 3 * n
    plan = dict(
        n=n, R=r, L=a["segments"].shape[1], D=d, T=t, C=c, F=f, NS=ns, Y=n // 2, X=x, Z=r // x,
        RW=d // r, SM=-(-small // 8) * 8,
    )
    shape = jax.ShapeDtypeStruct
    rw = d // r
    outs = [shape((t, d), BF16)] * 2 + [shape((rw, 4 * c), F32)] + [shape((rw, f), F32)] * 2
    outs += [shape((n, plan["SM"], c), F32), shape((8, d), F32)]
    for k in STATES:
        a[k] = a[k].T
    values = [v if v.ndim == 2 else v.reshape(1, -1) for v in (a[k] for k in INPUTS)]
    vmem, any_space = pl.BlockSpec(memory_space=pltpu.VMEM), pl.BlockSpec(memory_space=pl.ANY)
    sems = pltpu.SemaphoreType.DMA((plan_semaphores(plan),))
    got = pl.pallas_call(
        functools.partial(layer_kernel, plan),
        out_shape=outs,
        in_specs=[any_space if k in LARGE else vmem for k in INPUTS],
        out_specs=[vmem] * len(outs),
        scratch_shapes=[pltpu.VMEM(s, k) for _, s, k in names(plan)] + [sems, sems],
        compiler_params=pltpu.CompilerParams(
            collective_id=0, has_side_effects=True, vmem_limit_bytes=60 << 20
        ),
    )(*values)
    row, state, line = shape((1, d), F32), shape((ns, d), F32), shape((rw, c), F32)
    token = shape((t, d), BF16)
    wide = shape((rw, f), F32)
    outs = [token, token, line, line, line, line, wide, shape((1, n * f), F32), wide]
    outs += [row] * 5 + [state] * 4 + [row] * 2
    large = (0, 1, 2, 3, 4, 5, 6, 8)
    done = pl.pallas_call(
        functools.partial(finish_kernel, plan),
        out_shape=outs,
        in_specs=[vmem] * 7,
        out_specs=[any_space if e in large else vmem for e in range(len(outs))],
        scratch_shapes=[pltpu.SemaphoreType.DMA((len(large),))],
    )(*got)
    done = list(done)
    for e in range(len(done)):
        if 14 <= e < 18:
            done[e] = done[e].T
        elif e not in large:
            done[e] = done[e].reshape(-1)
    return tuple(done)


def plan_semaphores(plan):
    y, x, z = plan["Y"] - 1, plan["X"] - 1, plan["Z"]
    gathers = 5 + plan["L"] // BLK
    slabs = 1 + y * (2 + x + z)
    hops = x + z + plan["n"]
    rows = 4 * (x * z + z - 1)
    return 12 + gathers * (2 * y + 1) + slabs + 3 * (2 * y + 1) + rows + plan["R"].bit_length() + hops


def solution(mesh):
    both, row, col = P(("rows", "chan"), None), P("rows", None), P(None, "chan")
    state = P("chan", None)
    in_specs = (
        both, both, row, col, col, col, col, col, P("chan"), col,
        P(), P(), P(), P(), P(), state, state, state, state, P("chan"), P("chan"),
    )
    grid = P("rows", "chan")
    out_specs = (both, both, grid, grid, grid, grid, grid, P(), grid) + (P(),) * 11
    return jax.shard_map(shards, mesh=mesh, in_specs=in_specs, out_specs=out_specs, check_vma=False)
```

```python
import functools
import itertools
import math

import jax
import jax.numpy as jnp
from jax import lax
from jax.experimental import pallas as pl
from jax.experimental.pallas import tpu as pltpu
from jax.sharding import PartitionSpec as P

HEAD = 128
CTX = 128
BLK = 512
TILE = 256
EPS = 1e-05
NEG = -1e30
F32 = jnp.float32
BF16 = jnp.bfloat16
NN = (((1,), (0,)), ((), ()))
NT = (((1,), (1,)), ((), ()))
TN = (((0,), (0,)), ((), ()))
ROOT = math.sqrt(2.0 / math.pi)
MESH = pl.DeviceIdType.MESH


def dot(left, right, dims=NN):
    return lax.dot_general(left, right, dims, preferred_element_type=F32)


def at(start, size):
    if isinstance(start, int):
        return pl.ds(start, size)
    return pl.ds(pl.multiple_of(start, math.gcd(size, 1024)), size)


def ssm_params(rate_ref, in_ref, key_ref, value_ref):
    rate = rate_ref[...]
    a = jnp.exp(-rate)
    s = jnp.sqrt(1.0 - a * a)
    return dict(rate=rate, a=a, s=s, mix=in_ref[...], km=key_ref[...], vm=value_ref[...])


def ssm_forward(x_ref, seg_ref, par, skip_k, skip_v, ck_ref, cv_ref, wide_k, wide_v, keep_ref):
    a, rate = par["a"], par["rate"]
    b = par["s"] * par["mix"]
    kb, vb = par["km"] * b, par["vm"] * b
    a128, d128 = jnp.exp(-128.0 * rate), 128.0 * jnp.exp(-127.0 * rate)
    first = BLK - CTX
    parts = first // 128
    mask = segment_mask(seg_ref)
    row = lax.broadcasted_iota(jnp.int32, (8, 1), 0)
    zero = jnp.zeros(a.shape, F32)

    def step(i, carry):
        out = []
        for j in range(parts):
            g, e = carry[j]
            base = pl.multiple_of(j * 128 + i * 8, 8)
            x8 = jnp.where(mask(row + base), x_ref[pl.ds(base, 8), :], 0.0)
            for t in range(8):
                e = a * e + g
                g = a * g + x8[t : t + 1, :]
            out.append((g, e))
        return tuple(out)

    ends = lax.fori_loop(0, 16, step, tuple((zero, zero) for _ in range(parts)))
    g, e = ends[0]
    for j in range(1, parts):
        e = ends[j][1] + a128 * e + d128 * g
        g = ends[j][0] + a128 * g
    keep_ref[0] = g

    def ahead(i, g):
        base = pl.multiple_of(first + i * 8, 8)
        raw = x_ref[pl.ds(base, 8), :]
        x8 = jnp.where(mask(row + base), raw, 0.0)
        ks, vs = [], []
        for t in range(8):
            g = a * g + x8[t : t + 1, :]
            keep_ref[i * 8 + t + 1] = g
            ks.append(jnp.sum(g * kb, axis=0, keepdims=True))
            vs.append(jnp.sum(g * vb, axis=0, keepdims=True))
        rows = pl.ds(pl.multiple_of(i * 8, 8), 8)
        wide_k[rows, :] = jnp.concatenate(ks, axis=0) + skip_k * raw
        wide_v[rows, :] = jnp.concatenate(vs, axis=0) + skip_v * raw
        return g

    lax.fori_loop(0, CTX // 8, ahead, g)
    ck_ref[...] = wide_k[...].astype(BF16)
    cv_ref[...] = wide_v[...].astype(BF16)
    return e


def segment_mask(seg_ref):
    segs = seg_ref[...]
    first = jnp.sum(jnp.where(segs < segs[:, BLK : BLK + 1], 1, 0), axis=1, keepdims=True)
    return lambda index: index >= first


def ssm_backward(x_ref, seg_ref, par, skip_k, skip_v, gk_ref, gv_ref, keep_ref, e0, gx_ref, small_ref):
    a, s, km, vm = par["a"], par["s"], par["km"], par["vm"]
    b = s * par["mix"]
    first = BLK - CTX
    mask = segment_mask(seg_ref)
    row = lax.broadcasted_iota(jnp.int32, (8, 1), 0)
    zero = jnp.zeros(a.shape, F32)

    def back(j, carry):
        lam, sk, sv, sx, sg = carry
        i = CTX // 8 - 1 - j
        base = pl.multiple_of(first + i * 8, 8)
        rows = pl.ds(pl.multiple_of(i * 8, 8), 8)
        inside = mask(row + base)
        x8 = jnp.where(inside, x_ref[pl.ds(base, 8), :], 0.0)
        k8, v8 = gk_ref[rows, :], gv_ref[rows, :]
        outs = [None] * 8
        for t in reversed(range(8)):
            kt, vt = k8[t : t + 1, :], v8[t : t + 1, :]
            lam = a * lam + km * kt + vm * vt
            now = keep_ref[i * 8 + t + 1]
            sk = sk + now * kt
            sv = sv + now * vt
            sx = sx + lam * x8[t : t + 1, :]
            sg = sg + lam * keep_ref[i * 8 + t]
            outs[t] = jnp.sum(lam * b, axis=0, keepdims=True)
        gx = jnp.where(inside, jnp.concatenate(outs, axis=0), 0.0)
        gx_ref[pl.ds(base, 8), :] = gx + skip_k * k8 + skip_v * v8
        return (lam, sk, sv, sx, sg)

    lam, sk, sv, sx, sg = lax.fori_loop(0, CTX // 8, back, (zero,) * 5)
    sx = sx + lam * (a * keep_ref[0])
    sg = sg + lam * (a * e0)
    ns = a.shape[0]
    small_ref[0:ns, :] = (a * a / s) * par["mix"] * sx - a * b * sg
    small_ref[ns : 2 * ns, :] = s * sx
    small_ref[2 * ns : 3 * ns, :] = sk * b
    small_ref[3 * ns : 4 * ns, :] = sv * b

    def tail(j, w):
        base = pl.multiple_of(first - 8 - j * 8, 8)
        outs = [None] * 8
        for t in reversed(range(8)):
            w = a * w
            outs[t] = jnp.sum(w, axis=0, keepdims=True)
        gx_ref[pl.ds(base, 8), :] = jnp.where(mask(row + base), jnp.concatenate(outs, axis=0), 0.0)
        return w

    lax.fori_loop(0, first // 8, tail, lam * b)
    raw = x_ref[first:BLK, :]
    small_ref[4 * ns : 4 * ns + 1, :] = jnp.sum(gk_ref[...] * raw, axis=0, keepdims=True)
    small_ref[4 * ns + 1 : 4 * ns + 2, :] = jnp.sum(gv_ref[...] * raw, axis=0, keepdims=True)


def tile_masks(seg_ref, block, tile):
    width = (tile + 1) * TILE
    segs = seg_ref[...]
    index = lax.broadcasted_iota(jnp.int32, (TILE, 1), 0) + (block * BLK + tile * TILE)
    own_id = jnp.zeros((TILE, 1), jnp.int32)
    for value in (1, 2, 3):
        below = jnp.sum(jnp.where(segs < value, 1, 0), axis=1, keepdims=True)
        own_id = own_id + jnp.where(index >= below, 1, 0)
    keys = segs[:, block * BLK : block * BLK + width]
    column = lax.broadcasted_iota(jnp.int32, (TILE, width), 1) + block * BLK
    own = (own_id == keys) & (column <= index)
    if block == 0:
        return own, None
    return own, own_id == segs[:, block * BLK - CTX : block * BLK]


def attn_forward(block, q_ref, k_ref, v_ref, ck_ref, cv_ref, seg_ref, store, lse_ref):
    scale = HEAD**-0.5
    for tile in range(BLK // TILE):
        own, ctx = tile_masks(seg_ref, block, tile)
        rows = pl.ds(block * BLK + tile * TILE, TILE)
        keys = pl.ds(block * BLK, (tile + 1) * TILE)
        for head in range(q_ref.shape[1] // HEAD):
            cols = pl.ds(head * HEAD, HEAD)
            q = q_ref[rows, cols]
            s = jnp.where(own, dot(q, k_ref[keys, cols], NT) * scale, NEG)
            top = jnp.max(s, axis=1, keepdims=True)
            if ctx is not None:
                sc = jnp.where(ctx, dot(q, ck_ref[:, cols], NT) * scale, NEG)
                top = jnp.maximum(top, jnp.max(sc, axis=1, keepdims=True))
            p = jnp.exp(s - top)
            total = jnp.sum(p, axis=1, keepdims=True)
            if ctx is not None:
                pc = jnp.exp(sc - top)
                total = total + jnp.sum(pc, axis=1, keepdims=True)
            lse_ref[head, rows, :] = top + jnp.log(total)
            inverse = 1.0 / total
            out = dot((p * inverse).astype(BF16), v_ref[keys, cols])
            if ctx is not None:
                out = out + dot((pc * inverse).astype(BF16), cv_ref[:, cols])
            store(rows, head, out.astype(BF16))


def attn_backward(
    block, q_ref, k_ref, v_ref, ck_ref, cv_ref, seg_ref, lse_ref, do_ref,
    gq_ref, gk_ref, gv_ref, gck_ref, gcv_ref, ak_ref, av_ref,
):
    scale = HEAD**-0.5
    base = block * BLK
    for tile in range(BLK // TILE):
        own, ctx = tile_masks(seg_ref, block, tile)
        width = (tile + 1) * TILE
        rows, keys = pl.ds(base + tile * TILE, TILE), pl.ds(base, width)
        for head in range(q_ref.shape[1] // HEAD):
            cols = pl.ds(head * HEAD, HEAD)
            q, k, v = q_ref[rows, cols], k_ref[keys, cols], v_ref[keys, cols]
            do = do_ref[tile * TILE : (tile + 1) * TILE, cols]
            lse = lse_ref[head, rows, :]
            p = jnp.exp(jnp.where(own, dot(q, k, NT) * scale, NEG) - lse)
            dp = dot(do, v, NT)
            weighted = jnp.sum(p * dp, axis=1, keepdims=True)
            if ctx is not None:
                kc, vc = ck_ref[:, cols], cv_ref[:, cols]
                pc = jnp.exp(jnp.where(ctx, dot(q, kc, NT) * scale, NEG) - lse)
                dpc = dot(do, vc, NT)
                weighted = weighted + jnp.sum(pc * dpc, axis=1, keepdims=True)
            ds = (p * (dp - weighted)).astype(BF16)
            gq = dot(ds, k)
            gk = dot(ds, q, TN)
            gv = dot(p.astype(BF16), do, TN)
            half = tile * TILE
            if tile > 0:
                ak_ref[0:half, cols] = ak_ref[0:half, cols] + gk[0:half, :]
                av_ref[0:half, cols] = av_ref[0:half, cols] + gv[0:half, :]
            ak_ref[half:width, cols] = gk[half:width, :]
            av_ref[half:width, cols] = gv[half:width, :]
            if ctx is not None:
                dsc = (pc * (dpc - weighted)).astype(BF16)
                gq = gq + dot(dsc, kc)
                gkc = dot(dsc, q, TN) * scale
                gvc = dot(pc.astype(BF16), do, TN)
                if tile > 0:
                    gkc = gkc + gck_ref[:, cols]
                    gvc = gvc + gcv_ref[:, cols]
                gck_ref[:, cols] = gkc
                gcv_ref[:, cols] = gvc
            gq_ref[rows, cols] = (gq * scale).astype(BF16)
    gk_ref[base : base + BLK, :] = (ak_ref[...] * scale).astype(BF16)
    gv_ref[base : base + BLK, :] = av_ref[...].astype(BF16)


def normalize(values):
    centered = values - jnp.mean(values, axis=-1, keepdims=True)
    inverse = lax.rsqrt(jnp.mean(centered * centered, axis=-1, keepdims=True) + EPS)
    return centered * inverse, inverse


def norm_back(grad, hat, inverse, gain):
    u = grad * gain
    return inverse * (
        u - jnp.mean(u, axis=-1, keepdims=True) - hat * jnp.mean(u * hat, axis=-1, keepdims=True)
    )


class Links:
    def __init__(self, plan, send, recv):
        self.plan, self.send, self.recv, self.used = plan, send, recv, 0
        self.chan, self.rows = lax.axis_index("chan"), lax.axis_index("rows")
        self.core = lax.rem(self.chan, 2)
        self.y = self.chan // 2
        self.mate = self.other(self.chan)
        self.x = lax.rem(self.rows, plan["X"])
        self.z = self.rows // plan["X"]

    def far(self, j):
        count = self.plan["Y"]
        return 2 * lax.rem(self.y + count + j, count) + self.core

    def other(self, chan):
        return chan + 1 - 2 * lax.rem(chan, 2)

    def put(self, source, target, **device):
        i = self.used
        self.used += 1
        copy = pltpu.make_async_remote_copy(
            src_ref=source, dst_ref=target, send_sem=self.send.at[i], recv_sem=self.recv.at[i],
            device_id=device, device_id_type=MESH,
        )
        copy.start()
        return copy

    def load(self, source, target):
        i = self.used
        self.used += 1
        copy = pltpu.make_async_copy(source, target, self.send.at[i])
        copy.start()
        return copy

    def enter(self):
        barrier = pltpu.get_barrier_semaphore()
        plan = self.plan
        partners = [{"chan": self.mate}]
        for j in range(1, plan["Y"]):
            partners += [{"chan": self.far(j)}, {"chan": self.other(self.far(j))}]
        partners += [{"rows": self.row_of(self.z, self.x + i)} for i in range(1, plan["X"])]
        partners += [{"rows": self.row_of(self.z + i, self.x)} for i in range(1, plan["Z"])]
        for partner in partners:
            pl.semaphore_signal(barrier, inc=1, device_id=partner, device_id_type=MESH)
        return lambda: pl.semaphore_wait(barrier, len(partners))

    def row_of(self, z, x):
        return lax.rem(z, self.plan["Z"]) * self.plan["X"] + lax.rem(x, self.plan["X"])


class Gather:
    def __init__(self, links, view):
        self.links, self.view = links, view
        own = view(links.chan)
        count = range(1, links.plan["Y"])
        self.direct = [links.put(own, own, chan=links.far(j)) for j in count]
        self.near = links.put(own, own, chan=links.mate)
        self.passed = []

    def forward(self):
        links = self.links
        for j, copy in enumerate(self.direct, 1):
            copy.wait_recv()
            shard = self.view(links.far(-j))
            self.passed.append(links.put(shard, shard, chan=links.mate))

    def finish(self):
        self.near.wait()
        for copy in self.passed:
            copy.wait()
        for copy in self.direct:
            copy.wait_send()


class SlabGather:
    def __init__(self, links, whole, width):
        self.links, self.whole, self.width = links, whole, width
        plan = links.plan
        self.size = whole.shape[0] // plan["R"]
        own = self.view(links.rows * self.size, self.size, links.chan)
        self.over_y = [links.put(own, own, chan=links.far(j)) for j in range(1, plan["Y"])]
        column = whole.at[:, at(links.chan * width, width)]
        self.near = links.put(column, column, chan=links.mate)

    def view(self, start, size, chan):
        return self.whole.at[at(start, size), at(chan * self.width, self.width)]

    def spread_x(self):
        links, plan = self.links, self.links.plan
        self.over_x = []
        for j, copy in enumerate(self.over_y, 1):
            copy.wait_recv()
            slab = self.view(links.rows * self.size, self.size, links.far(-j))
            for i in range(1, plan["X"]):
                self.over_x.append(links.put(slab, slab, rows=links.row_of(links.z, links.x + i)))

    def spread_z(self):
        links, plan = self.links, self.links.plan
        self.over_z = []
        for copy in self.over_x:
            copy.wait_recv()
        group = plan["X"] * self.size
        for j in range(1, plan["Y"]):
            slab = self.view(links.z * group, group, links.far(-j))
            for i in range(1, plan["Z"]):
                self.over_z.append(links.put(slab, slab, rows=links.row_of(links.z + i, links.x)))

    def forward(self):
        links, plan = self.links, self.links.plan
        for copy in self.over_z:
            copy.wait_recv()
        self.passed = []
        for j in range(1, plan["Y"]):
            column = self.whole.at[:, at(links.far(-j) * self.width, self.width)]
            self.passed.append(links.put(column, column, chan=links.mate))

    def finish(self):
        self.near.wait()
        for copy in self.passed:
            copy.wait()
        for copy in self.over_y + self.over_x + self.over_z:
            copy.wait_send()


class Scatter:
    def __init__(self, links, mixed_out, mixed_in, far_out, far_in, near_out, near_in):
        self.links = links
        self.mixed_out, self.mixed_in, self.far_out, self.far_in = mixed_out, mixed_in, far_out, far_in
        self.near_out, self.near_in = near_out, near_in
        self.mix, self.direct = [], []

    def for_mate(self, j, value):
        self.mixed_out[j - 1] = value.astype(BF16)
        self.mix.append(
            self.links.put(self.mixed_out.at[j - 1], self.mixed_in.at[j - 1], chan=self.links.mate)
        )

    def for_far(self, j, value):
        self.mix[j - 1].wait_recv()
        self.far_out[j - 1] = (value + self.mixed_in[j - 1].astype(F32)).astype(BF16)

    def send_far(self, j):
        links = self.links
        self.direct.append(
            links.put(self.far_out.at[j - 1], self.far_in.at[j - 1], chan=links.far(j))
        )

    def for_near(self, value):
        self.near_out[...] = value.astype(BF16)
        self.send_near()

    def send_near(self):
        self.near = self.links.put(self.near_out, self.near_in, chan=self.links.mate)

    def total(self, own):
        self.near.wait()
        own = own + self.near_in[...].astype(F32)
        for j, copy in enumerate(self.direct):
            copy.wait()
            own = own + self.far_in[j].astype(F32)
        for copy in self.mix:
            copy.wait_send()
        return own


class RowScatter:
    def __init__(self, links, stage, slots, order):
        self.links, self.stage, self.slots, self.order = links, stage, slots, order
        plan = links.plan
        self.size = dict(x=plan["X"], l=2, h=plan["Z"] // 2)
        self.copies, self.slot = {}, {}
        self.todo = []
        for k in range(3):
            for key in self.keys(k):
                self.slot[key] = len(self.slot)
                if k:
                    self.todo.append(key)

    def keys(self, k):
        rest = [range(self.size[axis] - 1, -1, -1) for axis in self.order[k + 1 :]]
        for i in range(self.size[self.order[k]] - 1, 0, -1):
            for offsets in itertools.product(*rest):
                yield (k, i) + offsets

    def place(self, offsets):
        links = self.links
        own = dict(x=links.x, l=lax.rem(links.z, 2), h=links.z // 2)
        to = {axis: lax.rem(own[axis] + offsets.get(axis, 0), self.size[axis]) for axis in own}
        return (to["h"] * 2 + to["l"]) * self.size["x"] + to["x"]

    def slab(self, offsets):
        size = self.slots.shape[1]
        return pl.ds(pl.multiple_of(self.place(offsets) * size, size), size)

    def send(self, key):
        k, i = key[:2]
        offsets = dict(zip(self.order[k:], key[1:]))
        slab = self.slab(offsets)
        if k:
            self.stage[slab, :] = self.value(k, offsets).astype(BF16)
        self.copies[key] = self.links.put(
            self.stage.at[slab], self.slots.at[self.slot[key]], rows=self.place({self.order[k]: i})
        )

    def value(self, k, offsets):
        total = self.stage[self.slab(offsets), :].astype(F32)
        for j in range(k):
            later = tuple(offsets.get(axis, 0) for axis in self.order[j + 1 :])
            for i in range(1, self.size[self.order[j]]):
                key = (j, i) + later
                self.copies[key].wait_recv()
                total = total + self.slots[self.slot[key]].astype(F32)
        return total

    def ready(self, low, high):
        offsets = dict(l=low, h=high)
        for x in range(self.size["x"] - 1, -1, -1):
            offsets["x"] = x
            key = (0,) + tuple(offsets[axis] for axis in self.order)
            if key[1]:
                self.send(key)

    def advance(self, count=1):
        for _ in range(min(count, len(self.todo))):
            self.send(self.todo.pop(0))

    def total(self):
        self.advance(len(self.todo))
        value = self.value(3, {})
        for copy in self.copies.values():
            copy.wait_send()
        return value


def weight_sums(left, right, sums):
    first = sums[0][0]
    rows = first.links.plan["X"] * first.slots.shape[1]
    for low in (1, 0):
        for high in range(first.size["h"] - 1, -1, -1):
            group = at(first.place(dict(l=low, h=high)) // first.size["x"] * rows, rows)
            product = dot(left[:, group], right[...], TN).astype(BF16)
            for one, cols in sums:
                one.stage[group, :] = product[:, cols]
            for one, _ in sums:
                one.ready(low, high)


class Doubling:
    def __init__(self, links, block, out, got):
        self.links, self.block, self.out, self.got, self.step = links, block, out, got, 0

    def begin(self):
        step, rows = self.step, self.links.rows
        self.out[step] = self.block[...]
        bit = 1 << step
        partner = rows + bit - 2 * bit * lax.rem(rows // bit, 2)
        self.copy = self.links.put(self.out.at[step], self.got.at[step], rows=partner)

    def end(self):
        self.copy.wait()
        self.block[...] = self.block[...] + self.got[self.step]
        self.step += 1


def names(plan):
    n, length, d, t, c, f = (plan[k] for k in ("n", "L", "D", "T", "C", "F"))
    far = plan["Y"] - 1
    z, rw = plan["Z"], plan["RW"]
    grid = (length, d)
    out = [("tok", grid, BF16), ("h1", grid, BF16), ("cot", grid, BF16), ("wout", (d, d), BF16)]
    out += [("attn", grid, BF16), ("h2", grid, BF16), ("act", (length, f), BF16), ("gpre", (length, f), BF16)]
    out += [("wqkv", (d, 3 * c), BF16), ("wup", (d, f), BF16), ("wdn", (d, f), BF16)]
    out += [("qkv", (length, 3 * c), BF16), ("gbr", grid, BF16)]
    out += [("ck", (CTX, c), BF16), ("cv", (CTX, c), BF16), ("gck", (CTX, c), F32), ("gcv", (CTX, c), F32)]
    out += [("lse", (c // HEAD, length, 1), F32), ("xs", (BLK, c), F32), ("gx", (BLK, c), F32)]
    out += [("keep", (CTX + 1, plan["NS"], c), F32), ("ak", (BLK, c), F32), ("av", (BLK, c), F32)]
    out += [("do", (BLK, c), BF16), ("r2own", (t, d), F32), ("p", (BLK, d), F32)]
    out += [("acc", (t, d), F32), ("ffn", (t, d), F32)]
    for s in ("a", "b"):
        out += [(s + part, (far, t, d), BF16) for part in ("_mo", "_mi", "_fo", "_fi")]
        out += [(s + part, (t, d), BF16) for part in ("_no", "_ni")]
    out += [("stage", (d, f), BF16), ("ostage", (d, c), BF16)]
    for s, w in (("up", f), ("dn", f), ("qk", 2 * c), ("va", c), ("ou", c)):
        out += [(s + "_slots", (plan["R"] - 1, rw, w), BF16)]
    steps = plan["R"].bit_length() - 1
    block = (plan["SM"], c)
    out += [("small", block, F32), ("smallin", (steps,) + block, F32), ("smallout", (steps,) + block, F32)]
    out += [("fx", (plan["X"], 8, d), F32), ("fz", (z, 8, d), F32), ("fc", (n, 8, d), F32)]
    return out


INPUTS = (
    "tokens", "cotangent", "segments", "w_query", "w_key", "w_value", "w_out", "w_up", "up_bias", "w_down",
    "down_bias", "norm1_gain", "norm1_bias", "norm2_gain", "norm2_bias", "decay_rates", "input_mix",
    "key_mix", "value_mix", "key_skip", "value_skip",
)
LARGE = (
    "tokens", "cotangent", "w_query", "w_key", "w_value", "w_out", "w_up", "w_down",
)
STATES = ("decay_rates", "input_mix", "key_mix", "value_mix")


class Box:
    def __init__(self, **items):
        self.__dict__.update(items)


def colsum(value):
    return jnp.sum(value, axis=0, keepdims=True)


def layer_kernel(plan, *refs):
    i = Box(**dict(zip(INPUTS, refs[:21])))
    o_out, o_tok, o_w4, o_up, o_dn, o_small, o_last = refs[21:28]
    scratch = refs[28:]
    s = Box(**dict(zip([x[0] for x in names(plan)], scratch)))
    links = Links(plan, scratch[-2], scratch[-1])
    n, length, d, t, c, f = (plan[k] for k in ("n", "L", "D", "T", "C", "F"))
    far = range(1, plan["Y"])
    here, mate, core = links.chan, links.mate, links.core
    pair = 2 * t
    own_rows, own_cols = at(here * t, t), at(here * c, c)
    own_part, mate_part = at(core * t, t), at((1 - core) * t, t)
    rows_of = lambda owner: at(owner * t, t)
    chip_rows = lambda owner: at(owner // 2 * pair, pair)
    q_ref, k_ref, v_ref = (s.qkv.at[:, e * c : (e + 1) * c] for e in range(3))

    ready = links.enter()
    got_tok = links.load(i.tokens, s.tok.at[own_rows])
    got_out = links.load(i.w_out, s.wout.at[:, own_cols])
    got_w = [
        links.load(w, s.wqkv.at[:, e * c : (e + 1) * c])
        for e, w in enumerate((i.w_query, i.w_key, i.w_value))
    ]
    got_cot = links.load(i.cotangent, s.cot.at[own_rows])
    got_up, got_dn = links.load(i.w_up, s.wup), links.load(i.w_down, s.wdn)
    par = ssm_params(i.decay_rates, i.input_mix, i.key_mix, i.value_mix)
    got_tok.wait()
    got_out.wait()
    ready()
    out_gather = SlabGather(links, s.wout, c)
    tok_gather = Gather(links, lambda o: s.tok.at[rows_of(o)])
    out_gather.spread_x()

    def project(rows):
        hat, _ = normalize(s.tok[rows, :].astype(F32))
        s.h1[rows, :] = (hat * i.norm1_gain[...] + i.norm1_bias[...]).astype(BF16)
        s.qkv[rows, :] = dot(s.h1[rows, :], s.wqkv[...]).astype(BF16)

    for got in got_w:
        got.wait()
    project(own_rows)
    out_gather.spread_z()
    tok_gather.near.wait_recv()
    project(rows_of(mate))
    got_cot.wait()
    half = t // 2
    cot_views = [lambda o, e=e: s.cot.at[at(o * t + e * half, half)] for e in range(2)]
    tok_gather.forward()
    cot_gathers = [Gather(links, cot_views[0])]
    for j in far:
        project(rows_of(links.far(-j)))
    for j, copy in zip(far, tok_gather.passed):
        copy.wait_recv()
        project(rows_of(links.other(links.far(-j))))
    tok_gather.near.wait_send()
    for copy in tok_gather.passed + tok_gather.direct:
        copy.wait_send()

    def store(rows, head, value):
        s.attn[rows, at(here * c + head * HEAD, HEAD)] = value

    attn_gathers = []

    def attend(block):
        attn_forward(block, q_ref, k_ref, v_ref, s.ck, s.cv, i.segments, store, s.lse)
        attn_gathers.append(
            Gather(links, lambda o: s.attn.at[pl.ds(block * BLK, BLK), at(o * c, c)])
        )

    attend(0)
    s.xs[...] = s.h1[0:BLK, own_cols].astype(F32)
    skip_k, skip_v = i.key_skip[...], i.value_skip[...]
    e0 = ssm_forward(s.xs, i.segments, par, skip_k, skip_v, s.ck, s.cv, s.gck, s.gcv, s.keep)
    cot_gathers[0].forward()
    attend(1)
    cot_gathers.append(Gather(links, cot_views[1]))
    out_gather.forward()
    attn_gathers[0].forward()
    got_up.wait()
    got_dn.wait()
    out_gather.finish()

    wide = 512

    def loop(count, body):
        def step(e, carry):
            body(at(e * wide, wide))
            return carry

        lax.fori_loop(0, count // wide, step, 0)

    def feed(block):
        rows = pl.ds(block * BLK, BLK)

        def residual(cols):
            s.p[:, cols] = s.tok[rows, cols].astype(F32) + dot(s.attn[rows, :], s.wout[:, cols])

        loop(d, residual)
        hat, _ = normalize(s.p[...])
        s.h2[rows, :] = (hat * i.norm2_gain[...] + i.norm2_bias[...]).astype(BF16)

        @pl.when(here * t // BLK == block)
        def _():
            s.r2own[...] = s.p[at(lax.rem(here * t, BLK), t), :]

        def hidden(cols):
            v = dot(s.h2[rows, :], s.wup[:, cols]) + i.up_bias[:, cols]
            square = v * v
            th = jnp.tanh(ROOT * (v + 0.044715 * (square * v)))
            part = 0.5 * (1.0 + th)
            s.act[rows, cols] = (v * part).astype(BF16)
            slope = part + 0.5 * v * (1.0 - th * th) * (ROOT * (1.0 + 0.134145 * square))
            s.gpre[rows, cols] = slope.astype(BF16)

        loop(f, hidden)

    attn_gathers[0].finish()
    feed(0)
    attn_gathers[1].forward()
    cot_gathers[1].forward()
    attn_gathers[1].finish()
    feed(1)
    for gather in cot_gathers:
        gather.finish()

    def rows_sum(k, stage, order):
        return RowScatter(links, stage, getattr(s, k + "_slots"), order)

    every = slice(None)
    down_sum = rows_sum("dn", s.stage, "xlh")
    weight_sums(s.cot, s.act, [(down_sum, every)])

    def slope_grad(owner):
        rows = chip_rows(owner)

        def part(cols):
            grad = dot(s.cot[rows, :], s.wdn[:, cols])
            s.gpre[rows, cols] = (grad * s.gpre[rows, cols].astype(F32)).astype(BF16)

        loop(f, part)

    def back(owner, source, weight):
        rows = chip_rows(owner)

        def part(cols):
            s.p[0:pair, cols] = dot(source[rows, :], weight[cols, :], NT)

        loop(d, part)

    def back_near(sums, source, weight, own):
        def part(cols):
            sums.near_out[:, cols] = dot(source[rows_of(mate), :], weight[cols, :], NT).astype(BF16)
            own[:, cols] = dot(source[own_rows, :], weight[cols, :], NT)

        loop(d, part)
        sums.send_near()

    scatter = lambda k: Scatter(links, *(getattr(s, k + x) for x in ("_mo", "_mi", "_fo", "_fi", "_no", "_ni")))
    grad2 = scatter("a")
    for j in far:
        slope_grad(links.far(j))
        back(links.far(j), s.gpre, s.wup)
        grad2.for_mate(j, s.p[mate_part, :])
        if j == plan["Y"] - 1:
            slope_grad(here)
            back_near(grad2, s.gpre, s.wup, s.acc)
        grad2.for_far(j, s.p[own_part, :])
        grad2.send_far(j)
    ffn = scatter("b")
    for j in far:
        back(links.far(j), s.act, s.wdn)
        ffn.for_mate(j, s.p[mate_part, :])
        if j == plan["Y"] - 1:
            back_near(ffn, s.act, s.wdn, s.ffn)
        ffn.for_far(j, s.p[own_part, :])
    down_sum.advance()
    up_sum = rows_sum("up", s.act, "xlh")
    weight_sums(s.h2, s.gpre, [(up_sum, every)])

    base = 4 * plan["NS"] + 2
    bias_rows = f // c
    for e in range(bias_rows):
        s.small[base + e : base + e + 1, :] = colsum(s.gpre[:, e * c : (e + 1) * c].astype(F32))
    base += bias_rows

    def keep_vector(k, value):
        for e in range(n):
            s.small[base + k * n + e : base + k * n + e + 1, :] = value[:, e * c : (e + 1) * c]

    down_sum.advance()
    grad_hidden2 = grad2.total(s.acc[...])
    hat2, inv2 = normalize(s.r2own[...])
    own_cot = s.cot[own_rows, :].astype(F32)
    s.acc[...] = own_cot + norm_back(grad_hidden2, hat2, inv2, i.norm2_gain[...])
    s.gbr[own_rows, :] = s.acc[...].astype(BF16)
    branch_gather = Gather(links, lambda o: s.gbr.at[rows_of(o)])
    keep_vector(0, colsum(own_cot))
    keep_vector(1, colsum(grad_hidden2 * hat2))
    keep_vector(2, colsum(grad_hidden2))
    down_sum.advance(plan["R"])
    branch_gather.forward()
    branch_gather.finish()
    for j in far:
        ffn.send_far(j)
    out_sum = rows_sum("ou", s.ostage, "lhx")
    weight_sums(s.attn, s.gbr.at[:, own_cols], [(out_sum, every)])
    up_sum.advance()

    def attend_back(block):
        s.do[...] = dot(s.gbr[block * BLK : (block + 1) * BLK, :], s.wout[own_cols, :], NT).astype(BF16)
        attn_backward(
            block, q_ref, k_ref, v_ref, s.ck, s.cv, i.segments, s.lse, s.do,
            q_ref, k_ref, v_ref, s.gck, s.gcv, s.ak, s.av,
        )

    attend_back(1)
    up_sum.advance()
    ssm_backward(s.xs, i.segments, par, skip_k, skip_v, s.gck, s.gcv, s.keep, e0, s.gx, s.small)
    steps = plan["R"].bit_length() - 1
    doubling = Doubling(links, s.small, s.smallout, s.smallin)
    doubling.begin()
    attend_back(0)
    out_sum.advance(2)

    def input_back(owner):
        rows = chip_rows(owner)

        def part(cols):
            s.p[0:pair, cols] = dot(s.qkv[rows, :], s.wqkv[cols, :], NT)

        loop(d, part)

        @pl.when(owner // 2 * pair < BLK)
        def _():
            s.p[0:pair, own_cols] = s.p[0:pair, own_cols] + s.gx[rows, :].astype(BF16).astype(F32)

    def norm1_sums(owner, total):
        hat, _ = normalize(s.tok[chip_rows(owner), :].astype(F32))
        partial = s.p[0:pair, :]
        return [total[0] + colsum(partial * hat), total[1] + colsum(partial)]

    def spread(slots, own, targets):
        return [links.put(slots.at[own], slots.at[own], **target) for target in targets]

    def settle(hops, slots, count):
        for hop in hops:
            hop.wait()
        return sum([slots[e] for e in range(1, count)], slots[0])

    grad1 = scatter("a")
    qk_sum = rows_sum("qk", s.h2.at[:, 0 : 2 * c], "xlh")
    value_sum = rows_sum("va", s.h2.at[:, 2 * c : 3 * c], "lxh")
    norm1 = [jnp.zeros((1, d), F32)] * 2
    for j in far:
        input_back(links.far(j))
        grad1.for_mate(j, s.p[mate_part, :])
        if j == 1:
            weight_sums(s.h1, s.qkv, [(value_sum, slice(2 * c, 3 * c)), (qk_sum, slice(0, 2 * c))])
        grad1.for_far(j, s.p[own_part, :])
        grad1.send_far(j)
        norm1 = norm1_sums(links.far(j), norm1)
    input_back(here)
    grad1.for_near(s.p[mate_part, :])
    norm1 = norm1_sums(here, norm1)
    s.fx[links.x, 0:1, :] = norm1[0]
    s.fx[links.x, 1:2, :] = norm1[1]
    s.fx[links.x, 2:8, :] = jnp.zeros((6, d), F32)
    hops = spread(s.fx, links.x, [{"rows": links.row_of(links.z, links.x + e)} for e in range(1, plan["X"])])
    doubling.end()
    doubling.begin()
    up_sum.advance(plan["R"])
    out_sum.advance(plan["R"])
    s.fz[links.z] = settle(hops, s.fx, plan["X"])
    hops = spread(s.fz, links.z, [{"rows": links.row_of(links.z + e, links.x)} for e in range(1, plan["Z"])])
    o_dn[...] = down_sum.total()
    for step in range(1, steps):
        doubling.end()
        if step < steps - 1:
            doubling.begin()
    o_small[here] = s.small[...]
    small_gather = Gather(links, lambda o: o_small.at[o])
    s.fc[here] = settle(hops, s.fz, plan["Z"])
    group = [mate] + [links.far(j) for j in far] + [links.other(links.far(j)) for j in far]
    hops = spread(s.fc, here, [{"chan": e} for e in group])
    qk_sum.advance()
    value_sum.advance()
    o_out[...] = (s.r2own[...] + ffn.total(s.ffn[...]) + i.down_bias[...]).astype(BF16)
    small_gather.forward()
    qk_sum.advance()
    value_sum.advance()
    o_up[...] = up_sum.total()
    o_last[...] = settle(hops, s.fc, n)
    small_gather.finish()
    qk_sum.advance(plan["R"])
    value_sum.advance(plan["R"])

    hat1, inv1 = normalize(s.tok[own_rows, :].astype(F32))
    grad_hidden1 = grad1.total(s.p[own_part, :])
    o_tok[...] = (s.acc[...] + norm_back(grad_hidden1, hat1, inv1, i.norm1_gain[...])).astype(BF16)
    o_w4[:, 3 * c : 4 * c] = out_sum.total()
    o_w4[:, 0 : 2 * c] = qk_sum.total()
    o_w4[:, 2 * c : 3 * c] = value_sum.total()


def finish_kernel(plan, *refs):
    out, tok, w4, up, dn, small, last = refs[:7]
    o_out, o_tok, o_q, o_k, o_v, o_o, o_up, o_ub, o_dn, o_db, o_g1, o_b1, o_g2, o_b2 = refs[7:21]
    o_dec, o_in, o_km, o_vm, o_ks, o_vs, sem = refs[21:]
    n, c, f, ns = (plan[k] for k in ("n", "C", "F", "NS"))
    moves = [(out, o_out), (tok, o_tok), (up, o_up), (dn, o_dn)]
    moves += [(w4.at[:, e * c : (e + 1) * c], o) for e, o in enumerate((o_q, o_k, o_v, o_o))]
    copies = [pltpu.make_async_copy(a, b, sem.at[e]) for e, (a, b) in enumerate(moves)]
    for copy in copies:
        copy.start()
    bias_rows = f // c
    base = 4 * ns + 2 + bias_rows
    for e in range(n):
        cols = slice(e * c, (e + 1) * c)
        for k, target in enumerate((o_dec, o_in, o_km, o_vm)):
            target[:, cols] = small[e, k * ns : (k + 1) * ns, :]
        o_ks[:, cols] = small[e, 4 * ns : 4 * ns + 1, :]
        o_vs[:, cols] = small[e, 4 * ns + 1 : 4 * ns + 2, :]
        for b in range(bias_rows):
            o_ub[:, e * f + b * c : e * f + (b + 1) * c] = small[e, 4 * ns + 2 + b : 4 * ns + 3 + b, :]
        for k, target in enumerate((o_db, o_g2, o_b2)):
            row = base + k * n + e
            target[:, cols] = sum([small[g, row : row + 1, :] for g in range(1, n)], small[0, row : row + 1, :])
    o_g1[...] = last[0:1, :]
    o_b1[...] = last[1:2, :]
    for copy in copies:
        copy.wait()


def shards(*args):
    a = dict(zip(INPUTS, args))
    n, r = lax.axis_size("chan"), lax.axis_size("rows")
    t, d = a["tokens"].shape
    c, f = a["w_query"].shape[1], a["w_up"].shape[1]
    ns = a["decay_rates"].shape[1]
    x = math.isqrt(r // 2)
    small = 4 * ns + 2 + f // c + 3 * n
    plan = dict(
        n=n, R=r, L=a["segments"].shape[1], D=d, T=t, C=c, F=f, NS=ns, Y=n // 2, X=x, Z=r // x,
        RW=d // r, SM=-(-small // 8) * 8,
    )
    shape = jax.ShapeDtypeStruct
    rw = d // r
    outs = [shape((t, d), BF16)] * 2 + [shape((rw, 4 * c), F32)] + [shape((rw, f), F32)] * 2
    outs += [shape((n, plan["SM"], c), F32), shape((8, d), F32)]
    for k in STATES:
        a[k] = a[k].T
    values = [v if v.ndim == 2 else v.reshape(1, -1) for v in (a[k] for k in INPUTS)]
    vmem, any_space = pl.BlockSpec(memory_space=pltpu.VMEM), pl.BlockSpec(memory_space=pl.ANY)
    sems = pltpu.SemaphoreType.DMA((plan_semaphores(plan),))
    got = pl.pallas_call(
        functools.partial(layer_kernel, plan),
        out_shape=outs,
        in_specs=[any_space if k in LARGE else vmem for k in INPUTS],
        out_specs=[vmem] * len(outs),
        scratch_shapes=[pltpu.VMEM(s, k) for _, s, k in names(plan)] + [sems, sems],
        compiler_params=pltpu.CompilerParams(
            collective_id=0, has_side_effects=True, vmem_limit_bytes=60 << 20
        ),
    )(*values)
    row, state, line = shape((1, d), F32), shape((ns, d), F32), shape((rw, c), F32)
    token = shape((t, d), BF16)
    wide = shape((rw, f), F32)
    outs = [token, token, line, line, line, line, wide, shape((1, n * f), F32), wide]
    outs += [row] * 5 + [state] * 4 + [row] * 2
    large = (0, 1, 2, 3, 4, 5, 6, 8)
    done = pl.pallas_call(
        functools.partial(finish_kernel, plan),
        out_shape=outs,
        in_specs=[vmem] * 7,
        out_specs=[any_space if e in large else vmem for e in range(len(outs))],
        scratch_shapes=[pltpu.SemaphoreType.DMA((len(large),))],
    )(*got)
    done = list(done)
    for e in range(len(done)):
        if 14 <= e < 18:
            done[e] = done[e].T
        elif e not in large:
            done[e] = done[e].reshape(-1)
    return tuple(done)


def plan_semaphores(plan):
    y, x, z = plan["Y"] - 1, plan["X"] - 1, plan["Z"]
    gathers = 5 + plan["L"] // BLK
    slabs = 1 + y * (2 + x + z)
    hops = x + z + plan["n"]
    rows = 5 * (plan["R"] - 1)
    return 12 + gathers * (2 * y + 1) + slabs + 3 * (2 * y + 1) + rows + plan["R"].bit_length() + hops


def solution(mesh):
    both, row, col = P(("rows", "chan"), None), P("rows", None), P(None, "chan")
    state = P("chan", None)
    in_specs = (
        both, both, row, col, col, col, col, col, P("chan"), col,
        P(), P(), P(), P(), P(), state, state, state, state, P("chan"), P("chan"),
    )
    grid = P("rows", "chan")
    out_specs = (both, both, grid, grid, grid, grid, grid, P(), grid) + (P(),) * 11
    return jax.shard_map(shards, mesh=mesh, in_specs=in_specs, out_specs=out_specs, check_vma=False)
```

```python
import functools
import itertools
import math

import jax
import jax.numpy as jnp
from jax import lax
from jax.experimental import pallas as pl
from jax.experimental.pallas import tpu as pltpu
from jax.sharding import PartitionSpec as P

HEAD = 128
CTX = 128
BLK = 512
TILE = 256
EPS = 1e-05
NEG = -1e30
F32 = jnp.float32
BF16 = jnp.bfloat16
NN = (((1,), (0,)), ((), ()))
NT = (((1,), (1,)), ((), ()))
TN = (((0,), (0,)), ((), ()))
ROOT = math.sqrt(2.0 / math.pi)
MESH = pl.DeviceIdType.MESH


def dot(left, right, dims=NN):
    return lax.dot_general(left, right, dims, preferred_element_type=F32)


def at(start, size):
    if isinstance(start, int):
        return pl.ds(start, size)
    return pl.ds(pl.multiple_of(start, math.gcd(size, 1024)), size)


def ssm_params(rate_ref, in_ref, key_ref, value_ref):
    rate = rate_ref[...]
    a = jnp.exp(-rate)
    s = jnp.sqrt(1.0 - a * a)
    return dict(rate=rate, a=a, s=s, mix=in_ref[...], km=key_ref[...], vm=value_ref[...])


def ssm_forward(x_ref, seg_ref, par, skip_k, skip_v, ck_ref, cv_ref, wide_k, wide_v, keep_ref):
    a, rate = par["a"], par["rate"]
    b = par["s"] * par["mix"]
    kb, vb = par["km"] * b, par["vm"] * b
    a128, d128 = jnp.exp(-128.0 * rate), 128.0 * jnp.exp(-127.0 * rate)
    first = BLK - CTX
    parts = first // 128
    mask = segment_mask(seg_ref)
    row = lax.broadcasted_iota(jnp.int32, (8, 1), 0)
    zero = jnp.zeros(a.shape, F32)

    def step(i, carry):
        out = []
        for j in range(parts):
            g, e = carry[j]
            base = pl.multiple_of(j * 128 + i * 8, 8)
            x8 = jnp.where(mask(row + base), x_ref[pl.ds(base, 8), :], 0.0)
            for t in range(8):
                e = a * e + g
                g = a * g + x8[t : t + 1, :]
            out.append((g, e))
        return tuple(out)

    ends = lax.fori_loop(0, 16, step, tuple((zero, zero) for _ in range(parts)))
    g, e = ends[0]
    for j in range(1, parts):
        e = ends[j][1] + a128 * e + d128 * g
        g = ends[j][0] + a128 * g
    keep_ref[0] = g

    def ahead(i, g):
        base = pl.multiple_of(first + i * 8, 8)
        raw = x_ref[pl.ds(base, 8), :]
        x8 = jnp.where(mask(row + base), raw, 0.0)
        ks, vs = [], []
        for t in range(8):
            g = a * g + x8[t : t + 1, :]
            keep_ref[i * 8 + t + 1] = g
            ks.append(jnp.sum(g * kb, axis=0, keepdims=True))
            vs.append(jnp.sum(g * vb, axis=0, keepdims=True))
        rows = pl.ds(pl.multiple_of(i * 8, 8), 8)
        wide_k[rows, :] = jnp.concatenate(ks, axis=0) + skip_k * raw
        wide_v[rows, :] = jnp.concatenate(vs, axis=0) + skip_v * raw
        return g

    lax.fori_loop(0, CTX // 8, ahead, g)
    ck_ref[...] = wide_k[...].astype(BF16)
    cv_ref[...] = wide_v[...].astype(BF16)
    return e


def segment_mask(seg_ref):
    segs = seg_ref[...]
    first = jnp.sum(jnp.where(segs < segs[:, BLK : BLK + 1], 1, 0), axis=1, keepdims=True)
    return lambda index: index >= first


def ssm_backward(x_ref, seg_ref, par, skip_k, skip_v, gk_ref, gv_ref, keep_ref, e0, gx_ref, small_ref):
    a, s, km, vm = par["a"], par["s"], par["km"], par["vm"]
    b = s * par["mix"]
    first = BLK - CTX
    mask = segment_mask(seg_ref)
    row = lax.broadcasted_iota(jnp.int32, (8, 1), 0)
    zero = jnp.zeros(a.shape, F32)

    def back(j, carry):
        lam, sk, sv, sx, sg = carry
        i = CTX // 8 - 1 - j
        base = pl.multiple_of(first + i * 8, 8)
        rows = pl.ds(pl.multiple_of(i * 8, 8), 8)
        inside = mask(row + base)
        x8 = jnp.where(inside, x_ref[pl.ds(base, 8), :], 0.0)
        k8, v8 = gk_ref[rows, :], gv_ref[rows, :]
        outs = [None] * 8
        for t in reversed(range(8)):
            kt, vt = k8[t : t + 1, :], v8[t : t + 1, :]
            lam = a * lam + km * kt + vm * vt
            now = keep_ref[i * 8 + t + 1]
            sk = sk + now * kt
            sv = sv + now * vt
            sx = sx + lam * x8[t : t + 1, :]
            sg = sg + lam * keep_ref[i * 8 + t]
            outs[t] = jnp.sum(lam * b, axis=0, keepdims=True)
        gx = jnp.where(inside, jnp.concatenate(outs, axis=0), 0.0)
        gx_ref[pl.ds(base, 8), :] = gx + skip_k * k8 + skip_v * v8
        return (lam, sk, sv, sx, sg)

    lam, sk, sv, sx, sg = lax.fori_loop(0, CTX // 8, back, (zero,) * 5)
    sx = sx + lam * (a * keep_ref[0])
    sg = sg + lam * (a * e0)
    ns = a.shape[0]
    small_ref[0:ns, :] = (a * a / s) * par["mix"] * sx - a * b * sg
    small_ref[ns : 2 * ns, :] = s * sx
    small_ref[2 * ns : 3 * ns, :] = sk * b
    small_ref[3 * ns : 4 * ns, :] = sv * b

    def tail(j, w):
        base = pl.multiple_of(first - 8 - j * 8, 8)
        outs = [None] * 8
        for t in reversed(range(8)):
            w = a * w
            outs[t] = jnp.sum(w, axis=0, keepdims=True)
        gx_ref[pl.ds(base, 8), :] = jnp.where(mask(row + base), jnp.concatenate(outs, axis=0), 0.0)
        return w

    lax.fori_loop(0, first // 8, tail, lam * b)
    raw = x_ref[first:BLK, :]
    small_ref[4 * ns : 4 * ns + 1, :] = jnp.sum(gk_ref[...] * raw, axis=0, keepdims=True)
    small_ref[4 * ns + 1 : 4 * ns + 2, :] = jnp.sum(gv_ref[...] * raw, axis=0, keepdims=True)


def tile_masks(seg_ref, block, tile):
    width = (tile + 1) * TILE
    segs = seg_ref[...]
    index = lax.broadcasted_iota(jnp.int32, (TILE, 1), 0) + (block * BLK + tile * TILE)
    own_id = jnp.zeros((TILE, 1), jnp.int32)
    for value in (1, 2, 3):
        below = jnp.sum(jnp.where(segs < value, 1, 0), axis=1, keepdims=True)
        own_id = own_id + jnp.where(index >= below, 1, 0)
    keys = segs[:, block * BLK : block * BLK + width]
    column = lax.broadcasted_iota(jnp.int32, (TILE, width), 1) + block * BLK
    own = (own_id == keys) & (column <= index)
    if block == 0:
        return own, None
    return own, own_id == segs[:, block * BLK - CTX : block * BLK]


def attn_forward(block, q_ref, k_ref, v_ref, ck_ref, cv_ref, seg_ref, store, lse_ref):
    scale = HEAD**-0.5
    for tile in range(BLK // TILE):
        own, ctx = tile_masks(seg_ref, block, tile)
        rows = pl.ds(block * BLK + tile * TILE, TILE)
        keys = pl.ds(block * BLK, (tile + 1) * TILE)
        for head in range(q_ref.shape[1] // HEAD):
            cols = pl.ds(head * HEAD, HEAD)
            q = q_ref[rows, cols]
            s = jnp.where(own, dot(q, k_ref[keys, cols], NT) * scale, NEG)
            top = jnp.max(s, axis=1, keepdims=True)
            if ctx is not None:
                sc = jnp.where(ctx, dot(q, ck_ref[:, cols], NT) * scale, NEG)
                top = jnp.maximum(top, jnp.max(sc, axis=1, keepdims=True))
            p = jnp.exp(s - top)
            total = jnp.sum(p, axis=1, keepdims=True)
            if ctx is not None:
                pc = jnp.exp(sc - top)
                total = total + jnp.sum(pc, axis=1, keepdims=True)
            lse_ref[head, rows, :] = top + jnp.log(total)
            inverse = 1.0 / total
            out = dot((p * inverse).astype(BF16), v_ref[keys, cols])
            if ctx is not None:
                out = out + dot((pc * inverse).astype(BF16), cv_ref[:, cols])
            store(rows, head, out.astype(BF16))


def attn_backward(
    block, q_ref, k_ref, v_ref, ck_ref, cv_ref, seg_ref, lse_ref, do_ref,
    gq_ref, gk_ref, gv_ref, gck_ref, gcv_ref, ak_ref, av_ref,
):
    scale = HEAD**-0.5
    base = block * BLK
    for tile in range(BLK // TILE):
        own, ctx = tile_masks(seg_ref, block, tile)
        width = (tile + 1) * TILE
        rows, keys = pl.ds(base + tile * TILE, TILE), pl.ds(base, width)
        for head in range(q_ref.shape[1] // HEAD):
            cols = pl.ds(head * HEAD, HEAD)
            q, k, v = q_ref[rows, cols], k_ref[keys, cols], v_ref[keys, cols]
            do = do_ref[tile * TILE : (tile + 1) * TILE, cols]
            lse = lse_ref[head, rows, :]
            p = jnp.exp(jnp.where(own, dot(q, k, NT) * scale, NEG) - lse)
            dp = dot(do, v, NT)
            weighted = jnp.sum(p * dp, axis=1, keepdims=True)
            if ctx is not None:
                kc, vc = ck_ref[:, cols], cv_ref[:, cols]
                pc = jnp.exp(jnp.where(ctx, dot(q, kc, NT) * scale, NEG) - lse)
                dpc = dot(do, vc, NT)
                weighted = weighted + jnp.sum(pc * dpc, axis=1, keepdims=True)
            ds = (p * (dp - weighted)).astype(BF16)
            gq = dot(ds, k)
            gk = dot(ds, q, TN)
            gv = dot(p.astype(BF16), do, TN)
            half = tile * TILE
            if tile > 0:
                ak_ref[0:half, cols] = ak_ref[0:half, cols] + gk[0:half, :]
                av_ref[0:half, cols] = av_ref[0:half, cols] + gv[0:half, :]
            ak_ref[half:width, cols] = gk[half:width, :]
            av_ref[half:width, cols] = gv[half:width, :]
            if ctx is not None:
                dsc = (pc * (dpc - weighted)).astype(BF16)
                gq = gq + dot(dsc, kc)
                gkc = dot(dsc, q, TN) * scale
                gvc = dot(pc.astype(BF16), do, TN)
                if tile > 0:
                    gkc = gkc + gck_ref[:, cols]
                    gvc = gvc + gcv_ref[:, cols]
                gck_ref[:, cols] = gkc
                gcv_ref[:, cols] = gvc
            gq_ref[rows, cols] = (gq * scale).astype(BF16)
    gk_ref[base : base + BLK, :] = (ak_ref[...] * scale).astype(BF16)
    gv_ref[base : base + BLK, :] = av_ref[...].astype(BF16)


def normalize(values):
    centered = values - jnp.mean(values, axis=-1, keepdims=True)
    inverse = lax.rsqrt(jnp.mean(centered * centered, axis=-1, keepdims=True) + EPS)
    return centered * inverse, inverse


def norm_back(grad, hat, inverse, gain):
    u = grad * gain
    return inverse * (
        u - jnp.mean(u, axis=-1, keepdims=True) - hat * jnp.mean(u * hat, axis=-1, keepdims=True)
    )


class Links:
    def __init__(self, plan, send, recv):
        self.plan, self.send, self.recv, self.used = plan, send, recv, 0
        self.chan, self.rows = lax.axis_index("chan"), lax.axis_index("rows")
        self.core = lax.rem(self.chan, 2)
        self.y = self.chan // 2
        self.mate = self.other(self.chan)
        self.x = lax.rem(self.rows, plan["X"])
        self.z = self.rows // plan["X"]

    def far(self, j):
        count = self.plan["Y"]
        return 2 * lax.rem(self.y + count + j, count) + self.core

    def other(self, chan):
        return chan + 1 - 2 * lax.rem(chan, 2)

    def put(self, source, target, **device):
        i = self.used
        self.used += 1
        copy = pltpu.make_async_remote_copy(
            src_ref=source, dst_ref=target, send_sem=self.send.at[i], recv_sem=self.recv.at[i],
            device_id=device, device_id_type=MESH,
        )
        copy.start()
        return copy

    def load(self, source, target):
        i = self.used
        self.used += 1
        copy = pltpu.make_async_copy(source, target, self.send.at[i])
        copy.start()
        return copy

    def enter(self):
        barrier = pltpu.get_barrier_semaphore()
        plan = self.plan
        partners = [{"chan": self.mate}]
        for j in range(1, plan["Y"]):
            partners += [{"chan": self.far(j)}, {"chan": self.other(self.far(j))}]
        partners += [{"rows": self.row_of(self.z, self.x + i)} for i in range(1, plan["X"])]
        partners += [{"rows": self.row_of(self.z + i, self.x)} for i in range(1, plan["Z"])]
        for partner in partners:
            pl.semaphore_signal(barrier, inc=1, device_id=partner, device_id_type=MESH)
        return lambda: pl.semaphore_wait(barrier, len(partners))

    def row_of(self, z, x):
        return lax.rem(z, self.plan["Z"]) * self.plan["X"] + lax.rem(x, self.plan["X"])


class Gather:
    def __init__(self, links, view):
        self.links, self.view = links, view
        own = view(links.chan)
        count = range(1, links.plan["Y"])
        self.direct = [links.put(own, own, chan=links.far(j)) for j in count]
        self.near = links.put(own, own, chan=links.mate)
        self.passed = []

    def forward(self):
        links = self.links
        for j, copy in enumerate(self.direct, 1):
            copy.wait_recv()
            shard = self.view(links.far(-j))
            self.passed.append(links.put(shard, shard, chan=links.mate))

    def finish(self):
        self.near.wait()
        for copy in self.passed:
            copy.wait()
        for copy in self.direct:
            copy.wait_send()


class SlabGather:
    def __init__(self, links, whole, width):
        self.links, self.whole, self.width = links, whole, width
        plan = links.plan
        self.size = whole.shape[0] // plan["R"]
        own = self.view(links.rows * self.size, self.size, links.chan)
        self.over_y = [links.put(own, own, chan=links.far(j)) for j in range(1, plan["Y"])]
        column = whole.at[:, at(links.chan * width, width)]
        self.near = links.put(column, column, chan=links.mate)

    def view(self, start, size, chan):
        return self.whole.at[at(start, size), at(chan * self.width, self.width)]

    def spread_x(self):
        links, plan = self.links, self.links.plan
        self.over_x = []
        for j, copy in enumerate(self.over_y, 1):
            copy.wait_recv()
            slab = self.view(links.rows * self.size, self.size, links.far(-j))
            for i in range(1, plan["X"]):
                self.over_x.append(links.put(slab, slab, rows=links.row_of(links.z, links.x + i)))

    def spread_z(self):
        links, plan = self.links, self.links.plan
        self.over_z = []
        for copy in self.over_x:
            copy.wait_recv()
        group = plan["X"] * self.size
        for j in range(1, plan["Y"]):
            slab = self.view(links.z * group, group, links.far(-j))
            for i in range(1, plan["Z"]):
                self.over_z.append(links.put(slab, slab, rows=links.row_of(links.z + i, links.x)))

    def forward(self):
        links, plan = self.links, self.links.plan
        for copy in self.over_z:
            copy.wait_recv()
        self.passed = []
        for j in range(1, plan["Y"]):
            column = self.whole.at[:, at(links.far(-j) * self.width, self.width)]
            self.passed.append(links.put(column, column, chan=links.mate))

    def finish(self):
        self.near.wait()
        for copy in self.passed:
            copy.wait()
        for copy in self.over_y + self.over_x + self.over_z:
            copy.wait_send()


class Scatter:
    def __init__(self, links, mixed_out, mixed_in, far_out, far_in, near_out, near_in):
        self.links = links
        self.mixed_out, self.mixed_in, self.far_out, self.far_in = mixed_out, mixed_in, far_out, far_in
        self.near_out, self.near_in = near_out, near_in
        self.mix, self.direct = [], []

    def for_mate(self, j, value):
        self.mixed_out[j - 1] = value.astype(BF16)
        self.mix.append(
            self.links.put(self.mixed_out.at[j - 1], self.mixed_in.at[j - 1], chan=self.links.mate)
        )

    def for_far(self, j, value):
        self.mix[j - 1].wait_recv()
        self.far_out[j - 1] = (value + self.mixed_in[j - 1].astype(F32)).astype(BF16)

    def send_far(self, j, parts=1):
        links = self.links
        size = self.near_out.shape[0] // parts
        rows = [pl.ds(e * size, size) for e in range(parts)]
        self.direct.append(
            [
                links.put(self.far_out.at[j - 1, r], self.far_in.at[j - 1, r], chan=links.far(j))
                for r in rows
            ]
        )

    def for_near(self, value):
        self.near_out[...] = value.astype(BF16)
        self.send_near()

    def send_near(self):
        self.near = self.links.put(self.near_out, self.near_in, chan=self.links.mate)

    def total(self, own, part=0, parts=1):
        size = self.near_out.shape[0] // parts
        rows = pl.ds(part * size, size)
        if part == 0:
            self.near.wait()
            for copy in self.mix:
                copy.wait_send()
        own = own + self.near_in[rows, :].astype(F32)
        for j, copies in enumerate(self.direct):
            copies[part].wait()
            own = own + self.far_in[j, rows, :].astype(F32)
        return own


class RowScatter:
    def __init__(self, links, stage, slots, order):
        self.links, self.stage, self.slots, self.order = links, stage, slots, order
        plan = links.plan
        self.size = dict(x=plan["X"], l=2, h=plan["Z"] // 2)
        self.copies, self.slot = {}, {}
        self.todo = []
        for k in range(3):
            for key in self.keys(k):
                self.slot[key] = len(self.slot)
                if k:
                    self.todo.append(key)

    def keys(self, k):
        rest = [range(self.size[axis] - 1, -1, -1) for axis in self.order[k + 1 :]]
        for i in range(self.size[self.order[k]] - 1, 0, -1):
            for offsets in itertools.product(*rest):
                yield (k, i) + offsets

    def place(self, offsets):
        links = self.links
        own = dict(x=links.x, l=lax.rem(links.z, 2), h=links.z // 2)
        to = {axis: lax.rem(own[axis] + offsets.get(axis, 0), self.size[axis]) for axis in own}
        return (to["h"] * 2 + to["l"]) * self.size["x"] + to["x"]

    def slab(self, offsets):
        size = self.slots.shape[1]
        return pl.ds(pl.multiple_of(self.place(offsets) * size, size), size)

    def send(self, key):
        k, i = key[:2]
        offsets = dict(zip(self.order[k:], key[1:]))
        slab = self.slab(offsets)
        if k:
            self.stage[slab, :] = self.value(k, offsets).astype(BF16)
        self.copies[key] = self.links.put(
            self.stage.at[slab], self.slots.at[self.slot[key]], rows=self.place({self.order[k]: i})
        )

    def value(self, k, offsets):
        total = self.stage[self.slab(offsets), :].astype(F32)
        for j in range(k):
            later = tuple(offsets.get(axis, 0) for axis in self.order[j + 1 :])
            for i in range(1, self.size[self.order[j]]):
                key = (j, i) + later
                self.copies[key].wait_recv()
                total = total + self.slots[self.slot[key]].astype(F32)
        return total

    def ready(self, low, high):
        offsets = dict(l=low, h=high)
        for x in range(self.size["x"] - 1, -1, -1):
            offsets["x"] = x
            key = (0,) + tuple(offsets[axis] for axis in self.order)
            if key[1]:
                self.send(key)

    def advance(self, count=1):
        for _ in range(min(count, len(self.todo))):
            self.send(self.todo.pop(0))

    def total(self):
        self.advance(len(self.todo))
        value = self.value(3, {})
        for copy in self.copies.values():
            copy.wait_send()
        return value


def weight_sums(left, right, sums, hold):
    first, later = sums[0][0], []
    rows = first.links.plan["X"] * first.slots.shape[1]
    for low in (1, 0):
        for high in range(first.size["h"] - 1, -1, -1):
            group = at(first.place(dict(l=low, h=high)) // first.size["x"] * rows, rows)
            product = dot(left[:, group], right[...], TN).astype(BF16)
            for one, cols in sums:
                one.stage[group, :] = product[:, cols]
            for one, _ in sums:
                if low < hold.get(one, 0):
                    later.append(functools.partial(one.ready, low, high))
                else:
                    one.ready(low, high)
    return later


class Doubling:
    def __init__(self, links, block, out, got):
        self.links, self.block, self.out, self.got, self.step = links, block, out, got, 0

    def begin(self):
        step, rows = self.step, self.links.rows
        self.out[step] = self.block[...]
        bit = 1 << step
        partner = rows + bit - 2 * bit * lax.rem(rows // bit, 2)
        self.copy = self.links.put(self.out.at[step], self.got.at[step], rows=partner)

    def end(self):
        self.copy.wait()
        self.block[...] = self.block[...] + self.got[self.step]
        self.step += 1


def names(plan):
    n, length, d, t, c, f = (plan[k] for k in ("n", "L", "D", "T", "C", "F"))
    far = plan["Y"] - 1
    z, rw = plan["Z"], plan["RW"]
    grid = (length, d)
    out = [("tok", grid, BF16), ("h1", grid, BF16), ("cot", grid, BF16), ("wout", (d, d), BF16)]
    out += [("attn", grid, BF16), ("h2", grid, BF16), ("act", (length, f), BF16), ("gpre", (length, f), BF16)]
    out += [("wqkv", (d, 3 * c), BF16), ("wup", (d, f), BF16), ("wdn", (d, f), BF16)]
    out += [("qkv", (length, 3 * c), BF16), ("gbr", grid, BF16)]
    out += [("ck", (CTX, c), BF16), ("cv", (CTX, c), BF16), ("gck", (CTX, c), F32), ("gcv", (CTX, c), F32)]
    out += [("lse", (c // HEAD, length, 1), F32), ("xs", (BLK, c), F32), ("gx", (BLK, c), F32)]
    out += [("keep", (CTX + 1, plan["NS"], c), F32), ("ak", (BLK, c), F32), ("av", (BLK, c), F32)]
    out += [("do", (BLK, c), BF16), ("r2own", (t, d), F32), ("p", (BLK, d), F32)]
    out += [("acc", (t, d), F32), ("ffn", (t, d), F32)]
    for s in ("a", "b"):
        out += [(s + part, (far, t, d), BF16) for part in ("_mo", "_mi", "_fo", "_fi")]
        out += [(s + part, (t, d), BF16) for part in ("_no", "_ni")]
    out += [("stage", (d, f), BF16), ("ostage", (d, c), BF16)]
    for s, w in (("up", f), ("dn", f), ("qk", 2 * c), ("va", c), ("ou", c)):
        out += [(s + "_slots", (plan["R"] - 1, rw, w), BF16)]
    steps = plan["R"].bit_length() - 1
    block = (plan["SM"], c)
    out += [("small", block, F32), ("smallin", (steps,) + block, F32), ("smallout", (steps,) + block, F32)]
    out += [("fx", (plan["X"], 8, d), F32), ("fz", (z, 8, d), F32), ("fc", (n, 8, d), F32)]
    return out


INPUTS = (
    "tokens", "cotangent", "segments", "w_query", "w_key", "w_value", "w_out", "w_up", "up_bias", "w_down",
    "down_bias", "norm1_gain", "norm1_bias", "norm2_gain", "norm2_bias", "decay_rates", "input_mix",
    "key_mix", "value_mix", "key_skip", "value_skip",
)
LARGE = (
    "tokens", "cotangent", "w_query", "w_key", "w_value", "w_out", "w_up", "w_down",
)
STATES = ("decay_rates", "input_mix", "key_mix", "value_mix")


class Box:
    def __init__(self, **items):
        self.__dict__.update(items)


def colsum(value):
    return jnp.sum(value, axis=0, keepdims=True)


def layer_kernel(plan, *refs):
    i = Box(**dict(zip(INPUTS, refs[:21])))
    o_out, o_tok, o_w4, o_up, o_dn, o_small, o_last = refs[21:28]
    scratch = refs[28:]
    s = Box(**dict(zip([x[0] for x in names(plan)], scratch)))
    links = Links(plan, scratch[-2], scratch[-1])
    n, length, d, t, c, f = (plan[k] for k in ("n", "L", "D", "T", "C", "F"))
    far = range(1, plan["Y"])
    here, mate, core = links.chan, links.mate, links.core
    pair = 2 * t
    own_rows, own_cols = at(here * t, t), at(here * c, c)
    own_part, mate_part = at(core * t, t), at((1 - core) * t, t)
    rows_of = lambda owner: at(owner * t, t)
    chip_rows = lambda owner: at(owner // 2 * pair, pair)
    q_ref, k_ref, v_ref = (s.qkv.at[:, e * c : (e + 1) * c] for e in range(3))

    ready = links.enter()
    got_tok = links.load(i.tokens, s.tok.at[own_rows])
    got_out = links.load(i.w_out, s.wout.at[:, own_cols])
    got_w = [
        links.load(w, s.wqkv.at[:, e * c : (e + 1) * c])
        for e, w in enumerate((i.w_query, i.w_key, i.w_value))
    ]
    got_cot = links.load(i.cotangent, s.cot.at[own_rows])
    got_up, got_dn = links.load(i.w_up, s.wup), links.load(i.w_down, s.wdn)
    par = ssm_params(i.decay_rates, i.input_mix, i.key_mix, i.value_mix)
    got_tok.wait()
    got_out.wait()
    ready()
    out_gather = SlabGather(links, s.wout, c)
    tok_gather = Gather(links, lambda o: s.tok.at[rows_of(o)])
    out_gather.spread_x()

    def project(rows):
        hat, _ = normalize(s.tok[rows, :].astype(F32))
        s.h1[rows, :] = (hat * i.norm1_gain[...] + i.norm1_bias[...]).astype(BF16)
        s.qkv[rows, :] = dot(s.h1[rows, :], s.wqkv[...]).astype(BF16)

    for got in got_w:
        got.wait()
    project(own_rows)
    out_gather.spread_z()
    tok_gather.near.wait_recv()
    project(rows_of(mate))
    got_cot.wait()
    half = t // 2
    cot_views = [lambda o, e=e: s.cot.at[at(o * t + e * half, half)] for e in range(2)]
    tok_gather.forward()
    cot_gathers = [Gather(links, cot_views[0])]
    for j in far:
        project(rows_of(links.far(-j)))
    for j, copy in zip(far, tok_gather.passed):
        copy.wait_recv()
        project(rows_of(links.other(links.far(-j))))
    tok_gather.near.wait_send()
    for copy in tok_gather.passed + tok_gather.direct:
        copy.wait_send()

    def store(rows, head, value):
        s.attn[rows, at(here * c + head * HEAD, HEAD)] = value

    attn_gathers = []

    def attend(block):
        attn_forward(block, q_ref, k_ref, v_ref, s.ck, s.cv, i.segments, store, s.lse)
        attn_gathers.append(
            Gather(links, lambda o: s.attn.at[pl.ds(block * BLK, BLK), at(o * c, c)])
        )

    attend(0)
    s.xs[...] = s.h1[0:BLK, own_cols].astype(F32)
    skip_k, skip_v = i.key_skip[...], i.value_skip[...]
    e0 = ssm_forward(s.xs, i.segments, par, skip_k, skip_v, s.ck, s.cv, s.gck, s.gcv, s.keep)
    cot_gathers[0].forward()
    attend(1)
    cot_gathers.append(Gather(links, cot_views[1]))
    out_gather.forward()
    attn_gathers[0].forward()
    got_up.wait()
    got_dn.wait()
    out_gather.finish()

    wide = 512

    def loop(count, body):
        def step(e, carry):
            body(at(e * wide, wide))
            return carry

        lax.fori_loop(0, count // wide, step, 0)

    def feed(block):
        rows = pl.ds(block * BLK, BLK)

        def residual(cols):
            s.p[:, cols] = s.tok[rows, cols].astype(F32) + dot(s.attn[rows, :], s.wout[:, cols])

        loop(d, residual)
        hat, _ = normalize(s.p[...])
        s.h2[rows, :] = (hat * i.norm2_gain[...] + i.norm2_bias[...]).astype(BF16)

        @pl.when(here * t // BLK == block)
        def _():
            s.r2own[...] = s.p[at(lax.rem(here * t, BLK), t), :]

        def hidden(cols):
            v = dot(s.h2[rows, :], s.wup[:, cols]) + i.up_bias[:, cols]
            square = v * v
            part = 0.5 + 0.5 * jnp.tanh(v * (ROOT + (0.044715 * ROOT) * square))
            act = v * part
            s.act[rows, cols] = act.astype(BF16)
            slope = part + act * (1.0 - part) * (2.0 * ROOT + (0.26829 * ROOT) * square)
            s.gpre[rows, cols] = slope.astype(BF16)

        loop(f, hidden)

    attn_gathers[0].finish()
    feed(0)
    attn_gathers[1].forward()
    cot_gathers[1].forward()
    attn_gathers[1].finish()
    feed(1)
    for gather in cot_gathers:
        gather.finish()

    def rows_sum(k, stage, order):
        return RowScatter(links, stage, getattr(s, k + "_slots"), order)

    every = slice(None)
    down_sum = rows_sum("dn", s.stage, "xlh")
    weight_sums(s.cot, s.act, [(down_sum, every)], {})

    def slope_grad(owner):
        rows = chip_rows(owner)

        def part(cols):
            grad = dot(s.cot[rows, :], s.wdn[:, cols])
            s.gpre[rows, cols] = (grad * s.gpre[rows, cols].astype(F32)).astype(BF16)

        loop(f, part)

    def back(owner, source, weight):
        rows = chip_rows(owner)

        def part(cols):
            s.p[0:pair, cols] = dot(source[rows, :], weight[cols, :], NT)

        loop(d, part)

    def back_near(sums, source, weight, own):
        def part(cols):
            sums.near_out[:, cols] = dot(source[rows_of(mate), :], weight[cols, :], NT).astype(BF16)
            own[:, cols] = dot(source[own_rows, :], weight[cols, :], NT)

        loop(d, part)
        sums.send_near()

    scatter = lambda k: Scatter(links, *(getattr(s, k + x) for x in ("_mo", "_mi", "_fo", "_fi", "_no", "_ni")))
    grad2 = scatter("a")
    for j in far:
        slope_grad(links.far(j))
        back(links.far(j), s.gpre, s.wup)
        grad2.for_mate(j, s.p[mate_part, :])
        if j == plan["Y"] - 1:
            slope_grad(here)
            back_near(grad2, s.gpre, s.wup, s.acc)
        grad2.for_far(j, s.p[own_part, :])
        grad2.send_far(j, 2)
    ffn = scatter("b")
    for j in far:
        back(links.far(j), s.act, s.wdn)
        ffn.for_mate(j, s.p[mate_part, :])
        if j == plan["Y"] - 1:
            back_near(ffn, s.act, s.wdn, s.ffn)
        ffn.for_far(j, s.p[own_part, :])
    down_sum.advance()
    up_sum = rows_sum("up", s.act, "xlh")
    weight_sums(s.h2, s.gpre, [(up_sum, every)], {})

    base = 4 * plan["NS"] + 2
    bias_rows = f // c
    for e in range(bias_rows):
        s.small[base + e : base + e + 1, :] = colsum(s.gpre[:, e * c : (e + 1) * c].astype(F32))
    base += bias_rows

    def keep_vector(k, value):
        for e in range(n):
            s.small[base + k * n + e : base + k * n + e + 1, :] = value[:, e * c : (e + 1) * c]

    down_sum.advance()
    branch_gathers, norm2 = [], [jnp.zeros((1, d), F32)] * 3
    for e in range(2):
        rows = pl.ds(e * half, half)
        tile_rows = at(here * t + e * half, half)
        grad_hidden2 = grad2.total(s.acc[rows, :], e, 2)
        hat2, inv2 = normalize(s.r2own[rows, :])
        own_cot = s.cot[tile_rows, :].astype(F32)
        grad_resid2 = own_cot + norm_back(grad_hidden2, hat2, inv2, i.norm2_gain[...])
        s.acc[rows, :] = grad_resid2
        s.gbr[tile_rows, :] = grad_resid2.astype(BF16)
        branch_gathers.append(Gather(links, lambda o, e=e: s.gbr.at[at(o * t + e * half, half)]))
        sums = colsum(own_cot), colsum(grad_hidden2 * hat2), colsum(grad_hidden2)
        norm2 = [a + b for a, b in zip(norm2, sums)]
    for k in range(3):
        keep_vector(k, norm2[k])
    down_sum.advance(plan["R"])
    up_sum.advance()
    for gather in branch_gathers:
        gather.forward()
    for gather in branch_gathers:
        gather.finish()
    for j in far:
        ffn.send_far(j)
    up_sum.advance()
    out_sum = rows_sum("ou", s.ostage, "xlh")
    held = weight_sums(s.attn, s.gbr.at[:, own_cols], [(out_sum, every)], {out_sum: 2})

    def attend_back(block):
        s.do[...] = dot(s.gbr[block * BLK : (block + 1) * BLK, :], s.wout[own_cols, :], NT).astype(BF16)
        attn_backward(
            block, q_ref, k_ref, v_ref, s.ck, s.cv, i.segments, s.lse, s.do,
            q_ref, k_ref, v_ref, s.gck, s.gcv, s.ak, s.av,
        )

    attend_back(1)
    ssm_backward(s.xs, i.segments, par, skip_k, skip_v, s.gck, s.gcv, s.keep, e0, s.gx, s.small)
    doubling = Doubling(links, s.small, s.smallout, s.smallin)
    steps = plan["R"].bit_length() - 1
    doubling.begin()
    for send in held:
        send()
    up_sum.advance(plan["R"])
    attend_back(0)

    def input_back(owner):
        rows = chip_rows(owner)

        def part(cols):
            s.p[0:pair, cols] = dot(s.qkv[rows, :], s.wqkv[cols, :], NT)

        loop(d, part)

        @pl.when(owner // 2 * pair < BLK)
        def _():
            s.p[0:pair, own_cols] = s.p[0:pair, own_cols] + s.gx[rows, :].astype(BF16).astype(F32)

    def norm1_sums(owner, total):
        hat, _ = normalize(s.tok[chip_rows(owner), :].astype(F32))
        partial = s.p[0:pair, :]
        return [total[0] + colsum(partial * hat), total[1] + colsum(partial)]

    def spread(slots, own, targets):
        return [links.put(slots.at[own], slots.at[own], **target) for target in targets]

    def settle(hops, slots, count):
        for hop in hops:
            hop.wait()
        return sum([slots[e] for e in range(1, count)], slots[0])

    grad1 = scatter("a")
    qk_sum = rows_sum("qk", s.h2.at[:, 0 : 2 * c], "xlh")
    value_sum = rows_sum("va", s.h2.at[:, 2 * c : 3 * c], "lxh")
    norm1 = [jnp.zeros((1, d), F32)] * 2
    for j in far:
        input_back(links.far(j))
        grad1.for_mate(j, s.p[mate_part, :])
        if j == 1:
            doubling.end()
            doubling.begin()
            both = [(value_sum, slice(2 * c, 3 * c)), (qk_sum, slice(0, 2 * c))]
            held = weight_sums(s.h1, s.qkv, both, {qk_sum: 1})
        grad1.for_far(j, s.p[own_part, :])
        grad1.send_far(j)
        norm1 = norm1_sums(links.far(j), norm1)
    input_back(here)
    grad1.for_near(s.p[mate_part, :])
    norm1 = norm1_sums(here, norm1)
    s.fx[links.x, 0:1, :] = norm1[0]
    s.fx[links.x, 1:2, :] = norm1[1]
    s.fx[links.x, 2:8, :] = jnp.zeros((6, d), F32)

    group = [mate] + [links.far(j) for j in far] + [links.other(links.far(j)) for j in far]
    group = [{"chan": e} for e in group]
    hops = spread(s.fx, links.x, [{"rows": links.row_of(links.z, links.x + e)} for e in range(1, plan["X"])])
    for step in range(2, steps):
        doubling.end()
        doubling.begin()
    for send in held:
        send()
    out_sum.advance(2)
    o_dn[...] = down_sum.total()
    qk_sum.advance()
    value_sum.advance()
    doubling.end()
    o_small[here] = s.small[...]
    blocks = spread(o_small, here, group)
    s.fz[links.z] = settle(hops, s.fx, plan["X"])
    hops = spread(s.fz, links.z, [{"rows": links.row_of(links.z + e, links.x)} for e in range(1, plan["Z"])])
    qk_sum.advance()
    value_sum.advance()
    out_sum.advance(plan["R"])
    o_up[...] = up_sum.total()
    s.fc[here] = settle(hops, s.fz, plan["Z"])
    hops = spread(s.fc, here, group)
    qk_sum.advance(plan["R"])
    o_w4[:, 3 * c : 4 * c] = out_sum.total()
    o_out[...] = (s.r2own[...] + ffn.total(s.ffn[...]) + i.down_bias[...]).astype(BF16)
    value_sum.advance(plan["R"])

    hat1, inv1 = normalize(s.tok[own_rows, :].astype(F32))
    grad_hidden1 = grad1.total(s.p[own_part, :])
    o_tok[...] = (s.acc[...] + norm_back(grad_hidden1, hat1, inv1, i.norm1_gain[...])).astype(BF16)
    o_last[...] = settle(hops, s.fc, n)
    for copy in blocks:
        copy.wait()
    o_w4[:, 0 : 2 * c] = qk_sum.total()
    o_w4[:, 2 * c : 3 * c] = value_sum.total()


def finish_kernel(plan, *refs):
    out, tok, w4, up, dn, small, last = refs[:7]
    o_out, o_tok, o_q, o_k, o_v, o_o, o_up, o_ub, o_dn, o_db, o_g1, o_b1, o_g2, o_b2 = refs[7:21]
    o_dec, o_in, o_km, o_vm, o_ks, o_vs, sem = refs[21:]
    n, c, f, ns = (plan[k] for k in ("n", "C", "F", "NS"))
    moves = [(out, o_out), (tok, o_tok), (up, o_up), (dn, o_dn)]
    moves += [(w4.at[:, e * c : (e + 1) * c], o) for e, o in enumerate((o_q, o_k, o_v, o_o))]
    copies = [pltpu.make_async_copy(a, b, sem.at[e]) for e, (a, b) in enumerate(moves)]
    for copy in copies:
        copy.start()
    bias_rows = f // c
    base = 4 * ns + 2 + bias_rows
    for e in range(n):
        cols = slice(e * c, (e + 1) * c)
        for k, target in enumerate((o_dec, o_in, o_km, o_vm)):
            target[:, cols] = small[e, k * ns : (k + 1) * ns, :]
        o_ks[:, cols] = small[e, 4 * ns : 4 * ns + 1, :]
        o_vs[:, cols] = small[e, 4 * ns + 1 : 4 * ns + 2, :]
        for b in range(bias_rows):
            o_ub[:, e * f + b * c : e * f + (b + 1) * c] = small[e, 4 * ns + 2 + b : 4 * ns + 3 + b, :]
        for k, target in enumerate((o_db, o_g2, o_b2)):
            row = base + k * n + e
            target[:, cols] = sum([small[g, row : row + 1, :] for g in range(1, n)], small[0, row : row + 1, :])
    o_g1[...] = last[0:1, :]
    o_b1[...] = last[1:2, :]
    for copy in copies:
        copy.wait()


def shards(*args):
    a = dict(zip(INPUTS, args))
    n, r = lax.axis_size("chan"), lax.axis_size("rows")
    t, d = a["tokens"].shape
    c, f = a["w_query"].shape[1], a["w_up"].shape[1]
    ns = a["decay_rates"].shape[1]
    x = math.isqrt(r // 2)
    small = 4 * ns + 2 + f // c + 3 * n
    plan = dict(
        n=n, R=r, L=a["segments"].shape[1], D=d, T=t, C=c, F=f, NS=ns, Y=n // 2, X=x, Z=r // x,
        RW=d // r, SM=-(-small // 8) * 8,
    )
    shape = jax.ShapeDtypeStruct
    rw = d // r
    outs = [shape((t, d), BF16)] * 2 + [shape((rw, 4 * c), F32)] + [shape((rw, f), F32)] * 2
    outs += [shape((n, plan["SM"], c), F32), shape((8, d), F32)]
    for k in STATES:
        a[k] = a[k].T
    values = [v if v.ndim == 2 else v.reshape(1, -1) for v in (a[k] for k in INPUTS)]
    vmem, any_space = pl.BlockSpec(memory_space=pltpu.VMEM), pl.BlockSpec(memory_space=pl.ANY)
    sems = pltpu.SemaphoreType.DMA((plan_semaphores(plan),))
    got = pl.pallas_call(
        functools.partial(layer_kernel, plan),
        out_shape=outs,
        in_specs=[any_space if k in LARGE else vmem for k in INPUTS],
        out_specs=[vmem] * len(outs),
        scratch_shapes=[pltpu.VMEM(s, k) for _, s, k in names(plan)] + [sems, sems],
        compiler_params=pltpu.CompilerParams(
            collective_id=0, has_side_effects=True, vmem_limit_bytes=60 << 20
        ),
    )(*values)
    row, state, line = shape((1, d), F32), shape((ns, d), F32), shape((rw, c), F32)
    token = shape((t, d), BF16)
    wide = shape((rw, f), F32)
    outs = [token, token, line, line, line, line, wide, shape((1, n * f), F32), wide]
    outs += [row] * 5 + [state] * 4 + [row] * 2
    large = (0, 1, 2, 3, 4, 5, 6, 8)
    done = pl.pallas_call(
        functools.partial(finish_kernel, plan),
        out_shape=outs,
        in_specs=[vmem] * 7,
        out_specs=[any_space if e in large else vmem for e in range(len(outs))],
        scratch_shapes=[pltpu.SemaphoreType.DMA((len(large),))],
    )(*got)
    done = list(done)
    for e in range(len(done)):
        if 14 <= e < 18:
            done[e] = done[e].T
        elif e not in large:
            done[e] = done[e].reshape(-1)
    return tuple(done)


def plan_semaphores(plan):
    y, x, z = plan["Y"] - 1, plan["X"] - 1, plan["Z"]
    gathers = 6 + plan["L"] // BLK
    slabs = 1 + y * (2 + x + z)
    hops = x + z + plan["n"]
    rows = 5 * (plan["R"] - 1)
    return 12 + gathers * (2 * y + 1) + slabs + 3 * (2 * y + 1) + y + rows + plan["R"].bit_length() + hops


def solution(mesh):
    both, row, col = P(("rows", "chan"), None), P("rows", None), P(None, "chan")
    state = P("chan", None)
    in_specs = (
        both, both, row, col, col, col, col, col, P("chan"), col,
        P(), P(), P(), P(), P(), state, state, state, state, P("chan"), P("chan"),
    )
    grid = P("rows", "chan")
    out_specs = (both, both, grid, grid, grid, grid, grid, P(), grid) + (P(),) * 11
    return jax.shard_map(shards, mesh=mesh, in_specs=in_specs, out_specs=out_specs, check_vma=False)
```

```python
import functools
import itertools
import math

import jax
import jax.numpy as jnp
from jax import lax
from jax.experimental import pallas as pl
from jax.experimental.pallas import tpu as pltpu
from jax.sharding import PartitionSpec as P

HEAD = 128
CTX = 128
BLK = 512
TILE = 256
EPS = 1e-05
NEG = -1e30
F32 = jnp.float32
BF16 = jnp.bfloat16
NN = (((1,), (0,)), ((), ()))
NT = (((1,), (1,)), ((), ()))
TN = (((0,), (0,)), ((), ()))
ROOT = math.sqrt(2.0 / math.pi)
MESH = pl.DeviceIdType.MESH


def dot(left, right, dims=NN):
    return lax.dot_general(left, right, dims, preferred_element_type=F32)


def at(start, size):
    if isinstance(start, int):
        return pl.ds(start, size)
    return pl.ds(pl.multiple_of(start, math.gcd(size, 1024)), size)


def ssm_params(rate_ref, in_ref, key_ref, value_ref):
    rate = rate_ref[...]
    a = jnp.exp(-rate)
    s = jnp.sqrt(1.0 - a * a)
    return dict(rate=rate, a=a, s=s, mix=in_ref[...], km=key_ref[...], vm=value_ref[...])


def ssm_forward(x_ref, seg_ref, par, skip_k, skip_v, ck_ref, cv_ref, wide_k, wide_v, keep_ref):
    a, rate = par["a"], par["rate"]
    b = par["s"] * par["mix"]
    kb, vb = par["km"] * b, par["vm"] * b
    a128, d128 = jnp.exp(-128.0 * rate), 128.0 * jnp.exp(-127.0 * rate)
    first = BLK - CTX
    parts = first // 128
    mask = segment_mask(seg_ref)
    row = lax.broadcasted_iota(jnp.int32, (8, 1), 0)
    zero = jnp.zeros(a.shape, F32)

    def step(i, carry):
        out = []
        for j in range(parts):
            g, e = carry[j]
            base = pl.multiple_of(j * 128 + i * 8, 8)
            x8 = jnp.where(mask(row + base), x_ref[pl.ds(base, 8), :], 0.0)
            for t in range(8):
                e = a * e + g
                g = a * g + x8[t : t + 1, :]
            out.append((g, e))
        return tuple(out)

    ends = lax.fori_loop(0, 16, step, tuple((zero, zero) for _ in range(parts)))
    g, e = ends[0]
    for j in range(1, parts):
        e = ends[j][1] + a128 * e + d128 * g
        g = ends[j][0] + a128 * g
    keep_ref[0] = g

    def ahead(i, g):
        base = pl.multiple_of(first + i * 8, 8)
        raw = x_ref[pl.ds(base, 8), :]
        x8 = jnp.where(mask(row + base), raw, 0.0)
        ks, vs = [], []
        for t in range(8):
            g = a * g + x8[t : t + 1, :]
            keep_ref[i * 8 + t + 1] = g
            ks.append(jnp.sum(g * kb, axis=0, keepdims=True))
            vs.append(jnp.sum(g * vb, axis=0, keepdims=True))
        rows = pl.ds(pl.multiple_of(i * 8, 8), 8)
        wide_k[rows, :] = jnp.concatenate(ks, axis=0) + skip_k * raw
        wide_v[rows, :] = jnp.concatenate(vs, axis=0) + skip_v * raw
        return g

    lax.fori_loop(0, CTX // 8, ahead, g)
    ck_ref[...] = wide_k[...].astype(BF16)
    cv_ref[...] = wide_v[...].astype(BF16)
    return e


def segment_mask(seg_ref):
    segs = seg_ref[...]
    first = jnp.sum(jnp.where(segs < segs[:, BLK : BLK + 1], 1, 0), axis=1, keepdims=True)
    return lambda index: index >= first


def ssm_backward(x_ref, seg_ref, par, skip_k, skip_v, gk_ref, gv_ref, keep_ref, e0, gx_ref, small_ref):
    a, s, km, vm = par["a"], par["s"], par["km"], par["vm"]
    b = s * par["mix"]
    first = BLK - CTX
    mask = segment_mask(seg_ref)
    row = lax.broadcasted_iota(jnp.int32, (8, 1), 0)
    zero = jnp.zeros(a.shape, F32)

    def back(j, carry):
        lam, sk, sv, sx, sg = carry
        i = CTX // 8 - 1 - j
        base = pl.multiple_of(first + i * 8, 8)
        rows = pl.ds(pl.multiple_of(i * 8, 8), 8)
        inside = mask(row + base)
        x8 = jnp.where(inside, x_ref[pl.ds(base, 8), :], 0.0)
        k8, v8 = gk_ref[rows, :], gv_ref[rows, :]
        outs = [None] * 8
        for t in reversed(range(8)):
            kt, vt = k8[t : t + 1, :], v8[t : t + 1, :]
            lam = a * lam + km * kt + vm * vt
            now = keep_ref[i * 8 + t + 1]
            sk = sk + now * kt
            sv = sv + now * vt
            sx = sx + lam * x8[t : t + 1, :]
            sg = sg + lam * keep_ref[i * 8 + t]
            outs[t] = jnp.sum(lam * b, axis=0, keepdims=True)
        gx = jnp.where(inside, jnp.concatenate(outs, axis=0), 0.0)
        gx_ref[pl.ds(base, 8), :] = gx + skip_k * k8 + skip_v * v8
        return (lam, sk, sv, sx, sg)

    lam, sk, sv, sx, sg = lax.fori_loop(0, CTX // 8, back, (zero,) * 5)
    sx = sx + lam * (a * keep_ref[0])
    sg = sg + lam * (a * e0)
    ns = a.shape[0]
    small_ref[0:ns, :] = (a * a / s) * par["mix"] * sx - a * b * sg
    small_ref[ns : 2 * ns, :] = s * sx
    small_ref[2 * ns : 3 * ns, :] = sk * b
    small_ref[3 * ns : 4 * ns, :] = sv * b

    def tail(j, w):
        base = pl.multiple_of(first - 8 - j * 8, 8)
        outs = [None] * 8
        for t in reversed(range(8)):
            w = a * w
            outs[t] = jnp.sum(w, axis=0, keepdims=True)
        gx_ref[pl.ds(base, 8), :] = jnp.where(mask(row + base), jnp.concatenate(outs, axis=0), 0.0)
        return w

    lax.fori_loop(0, first // 8, tail, lam * b)
    raw = x_ref[first:BLK, :]
    small_ref[4 * ns : 4 * ns + 1, :] = jnp.sum(gk_ref[...] * raw, axis=0, keepdims=True)
    small_ref[4 * ns + 1 : 4 * ns + 2, :] = jnp.sum(gv_ref[...] * raw, axis=0, keepdims=True)


def tile_masks(seg_ref, block, tile):
    width = (tile + 1) * TILE
    segs = seg_ref[...]
    index = lax.broadcasted_iota(jnp.int32, (TILE, 1), 0) + (block * BLK + tile * TILE)
    own_id = jnp.zeros((TILE, 1), jnp.int32)
    for value in (1, 2, 3):
        below = jnp.sum(jnp.where(segs < value, 1, 0), axis=1, keepdims=True)
        own_id = own_id + jnp.where(index >= below, 1, 0)
    keys = segs[:, block * BLK : block * BLK + width]
    column = lax.broadcasted_iota(jnp.int32, (TILE, width), 1) + block * BLK
    own = (own_id == keys) & (column <= index)
    if block == 0:
        return own, None
    return own, own_id == segs[:, block * BLK - CTX : block * BLK]


def attn_forward(block, q_ref, k_ref, v_ref, ck_ref, cv_ref, seg_ref, store, lse_ref):
    scale = HEAD**-0.5
    for tile in range(BLK // TILE):
        own, ctx = tile_masks(seg_ref, block, tile)
        rows = pl.ds(block * BLK + tile * TILE, TILE)
        keys = pl.ds(block * BLK, (tile + 1) * TILE)
        for head in range(q_ref.shape[1] // HEAD):
            cols = pl.ds(head * HEAD, HEAD)
            q = q_ref[rows, cols]
            s = jnp.where(own, dot(q, k_ref[keys, cols], NT) * scale, NEG)
            top = jnp.max(s, axis=1, keepdims=True)
            if ctx is not None:
                sc = jnp.where(ctx, dot(q, ck_ref[:, cols], NT) * scale, NEG)
                top = jnp.maximum(top, jnp.max(sc, axis=1, keepdims=True))
            p = jnp.exp(s - top)
            total = jnp.sum(p, axis=1, keepdims=True)
            if ctx is not None:
                pc = jnp.exp(sc - top)
                total = total + jnp.sum(pc, axis=1, keepdims=True)
            lse_ref[head, rows, :] = top + jnp.log(total)
            inverse = 1.0 / total
            out = dot((p * inverse).astype(BF16), v_ref[keys, cols])
            if ctx is not None:
                out = out + dot((pc * inverse).astype(BF16), cv_ref[:, cols])
            store(rows, head, out.astype(BF16))


def attn_backward(
    block, q_ref, k_ref, v_ref, ck_ref, cv_ref, seg_ref, lse_ref, do_ref,
    gq_ref, gk_ref, gv_ref, gck_ref, gcv_ref, ak_ref, av_ref,
):
    scale = HEAD**-0.5
    base = block * BLK
    for tile in range(BLK // TILE):
        own, ctx = tile_masks(seg_ref, block, tile)
        width = (tile + 1) * TILE
        rows, keys = pl.ds(base + tile * TILE, TILE), pl.ds(base, width)
        for head in range(q_ref.shape[1] // HEAD):
            cols = pl.ds(head * HEAD, HEAD)
            q, k, v = q_ref[rows, cols], k_ref[keys, cols], v_ref[keys, cols]
            do = do_ref[tile * TILE : (tile + 1) * TILE, cols]
            lse = lse_ref[head, rows, :]
            p = jnp.exp(jnp.where(own, dot(q, k, NT) * scale, NEG) - lse)
            dp = dot(do, v, NT)
            weighted = jnp.sum(p * dp, axis=1, keepdims=True)
            if ctx is not None:
                kc, vc = ck_ref[:, cols], cv_ref[:, cols]
                pc = jnp.exp(jnp.where(ctx, dot(q, kc, NT) * scale, NEG) - lse)
                dpc = dot(do, vc, NT)
                weighted = weighted + jnp.sum(pc * dpc, axis=1, keepdims=True)
            ds = (p * (dp - weighted)).astype(BF16)
            gq = dot(ds, k)
            gk = dot(ds, q, TN)
            gv = dot(p.astype(BF16), do, TN)
            half = tile * TILE
            if tile > 0:
                ak_ref[0:half, cols] = ak_ref[0:half, cols] + gk[0:half, :]
                av_ref[0:half, cols] = av_ref[0:half, cols] + gv[0:half, :]
            ak_ref[half:width, cols] = gk[half:width, :]
            av_ref[half:width, cols] = gv[half:width, :]
            if ctx is not None:
                dsc = (pc * (dpc - weighted)).astype(BF16)
                gq = gq + dot(dsc, kc)
                gkc = dot(dsc, q, TN) * scale
                gvc = dot(pc.astype(BF16), do, TN)
                if tile > 0:
                    gkc = gkc + gck_ref[:, cols]
                    gvc = gvc + gcv_ref[:, cols]
                gck_ref[:, cols] = gkc
                gcv_ref[:, cols] = gvc
            gq_ref[rows, cols] = (gq * scale).astype(BF16)
    gk_ref[base : base + BLK, :] = (ak_ref[...] * scale).astype(BF16)
    gv_ref[base : base + BLK, :] = av_ref[...].astype(BF16)


def normalize(values):
    centered = values - jnp.mean(values, axis=-1, keepdims=True)
    inverse = lax.rsqrt(jnp.mean(centered * centered, axis=-1, keepdims=True) + EPS)
    return centered * inverse, inverse


def norm_back(grad, hat, inverse, gain):
    u = grad * gain
    return inverse * (
        u - jnp.mean(u, axis=-1, keepdims=True) - hat * jnp.mean(u * hat, axis=-1, keepdims=True)
    )


class Links:
    def __init__(self, plan, send, recv):
        self.plan, self.send, self.recv, self.used = plan, send, recv, 0
        self.chan, self.rows = lax.axis_index("chan"), lax.axis_index("rows")
        self.core = lax.rem(self.chan, 2)
        self.y = self.chan // 2
        self.mate = self.other(self.chan)
        self.x = lax.rem(self.rows, plan["X"])
        self.z = self.rows // plan["X"]

    def far(self, j):
        count = self.plan["Y"]
        return 2 * lax.rem(self.y + count + j, count) + self.core

    def other(self, chan):
        return chan + 1 - 2 * lax.rem(chan, 2)

    def put(self, source, target, **device):
        i = self.used
        self.used += 1
        copy = pltpu.make_async_remote_copy(
            src_ref=source, dst_ref=target, send_sem=self.send.at[i], recv_sem=self.recv.at[i],
            device_id=device, device_id_type=MESH,
        )
        copy.start()
        return copy

    def load(self, source, target):
        i = self.used
        self.used += 1
        copy = pltpu.make_async_copy(source, target, self.send.at[i])
        copy.start()
        return copy

    def enter(self):
        barrier = pltpu.get_barrier_semaphore()
        plan = self.plan
        partners = [{"chan": self.mate}]
        for j in range(1, plan["Y"]):
            partners += [{"chan": self.far(j)}, {"chan": self.other(self.far(j))}]
        partners += [{"rows": self.row_of(self.z, self.x + i)} for i in range(1, plan["X"])]
        partners += [{"rows": self.row_of(self.z + i, self.x)} for i in range(1, plan["Z"])]
        for partner in partners:
            pl.semaphore_signal(barrier, inc=1, device_id=partner, device_id_type=MESH)
        return lambda: pl.semaphore_wait(barrier, len(partners))

    def row_of(self, z, x):
        return lax.rem(z, self.plan["Z"]) * self.plan["X"] + lax.rem(x, self.plan["X"])


class Gather:
    def __init__(self, links, view):
        self.links, self.view = links, view
        own = view(links.chan)
        count = range(1, links.plan["Y"])
        self.direct = [links.put(own, own, chan=links.far(j)) for j in count]
        self.near = links.put(own, own, chan=links.mate)
        self.passed = []

    def forward(self):
        links = self.links
        for j, copy in enumerate(self.direct, 1):
            copy.wait_recv()
            shard = self.view(links.far(-j))
            self.passed.append(links.put(shard, shard, chan=links.mate))

    def finish(self):
        self.near.wait()
        for copy in self.passed:
            copy.wait()
        for copy in self.direct:
            copy.wait_send()


class SlabGather:
    def __init__(self, links, whole, width):
        self.links, self.whole, self.width = links, whole, width
        plan = links.plan
        self.size = whole.shape[0] // plan["R"]
        own = self.view(links.rows * self.size, self.size, links.chan)
        self.over_y = [links.put(own, own, chan=links.far(j)) for j in range(1, plan["Y"])]
        column = whole.at[:, at(links.chan * width, width)]
        self.near = links.put(column, column, chan=links.mate)

    def view(self, start, size, chan):
        return self.whole.at[at(start, size), at(chan * self.width, self.width)]

    def spread_x(self):
        links, plan = self.links, self.links.plan
        self.over_x = []
        for j, copy in enumerate(self.over_y, 1):
            copy.wait_recv()
            slab = self.view(links.rows * self.size, self.size, links.far(-j))
            for i in range(1, plan["X"]):
                self.over_x.append(links.put(slab, slab, rows=links.row_of(links.z, links.x + i)))

    def spread_z(self):
        links, plan = self.links, self.links.plan
        self.over_z = []
        for copy in self.over_x:
            copy.wait_recv()
        group = plan["X"] * self.size
        for j in range(1, plan["Y"]):
            slab = self.view(links.z * group, group, links.far(-j))
            for i in range(1, plan["Z"]):
                self.over_z.append(links.put(slab, slab, rows=links.row_of(links.z + i, links.x)))

    def forward(self):
        links, plan = self.links, self.links.plan
        for copy in self.over_z:
            copy.wait_recv()
        self.passed = []
        for j in range(1, plan["Y"]):
            column = self.whole.at[:, at(links.far(-j) * self.width, self.width)]
            self.passed.append(links.put(column, column, chan=links.mate))

    def finish(self):
        self.near.wait()
        for copy in self.passed:
            copy.wait()
        for copy in self.over_y + self.over_x + self.over_z:
            copy.wait_send()


class Scatter:
    def __init__(self, links, mixed_out, mixed_in, far_out, far_in, near_out, near_in):
        self.links = links
        self.mixed_out, self.mixed_in, self.far_out, self.far_in = mixed_out, mixed_in, far_out, far_in
        self.near_out, self.near_in = near_out, near_in
        self.mix, self.direct = [], []

    def for_mate(self, j, value):
        self.mixed_out[j - 1] = value.astype(BF16)
        self.mix.append(
            self.links.put(self.mixed_out.at[j - 1], self.mixed_in.at[j - 1], chan=self.links.mate)
        )

    def for_far(self, j, value):
        self.mix[j - 1].wait_recv()
        self.far_out[j - 1] = (value + self.mixed_in[j - 1].astype(F32)).astype(BF16)

    def send_far(self, j, parts=1):
        links = self.links
        size = self.near_out.shape[0] // parts
        rows = [pl.ds(e * size, size) for e in range(parts)]
        self.direct.append(
            [
                links.put(self.far_out.at[j - 1, r], self.far_in.at[j - 1, r], chan=links.far(j))
                for r in rows
            ]
        )

    def for_near(self, value):
        self.near_out[...] = value.astype(BF16)
        self.send_near()

    def send_near(self):
        self.near = self.links.put(self.near_out, self.near_in, chan=self.links.mate)

    def total(self, own, part=0, parts=1):
        size = self.near_out.shape[0] // parts
        rows = pl.ds(part * size, size)
        if part == 0:
            self.near.wait()
            for copy in self.mix:
                copy.wait_send()
        own = own + self.near_in[rows, :].astype(F32)
        for j, copies in enumerate(self.direct):
            copies[part].wait()
            own = own + self.far_in[j, rows, :].astype(F32)
        return own


class RowScatter:
    def __init__(self, links, stage, slots, order):
        self.links, self.stage, self.slots, self.order = links, stage, slots, order
        plan = links.plan
        self.size = dict(x=plan["X"], l=2, h=plan["Z"] // 2)
        self.copies, self.slot = {}, {}
        self.todo = []
        for k in range(3):
            for key in self.keys(k):
                self.slot[key] = len(self.slot)
                if k:
                    self.todo.append(key)

    def keys(self, k):
        rest = [range(self.size[axis] - 1, -1, -1) for axis in self.order[k + 1 :]]
        for i in range(self.size[self.order[k]] - 1, 0, -1):
            for offsets in itertools.product(*rest):
                yield (k, i) + offsets

    def place(self, offsets):
        links = self.links
        own = dict(x=links.x, l=lax.rem(links.z, 2), h=links.z // 2)
        to = {axis: lax.rem(own[axis] + offsets.get(axis, 0), self.size[axis]) for axis in own}
        return (to["h"] * 2 + to["l"]) * self.size["x"] + to["x"]

    def slab(self, offsets):
        size = self.slots.shape[1]
        return pl.ds(pl.multiple_of(self.place(offsets) * size, size), size)

    def send(self, key):
        k, i = key[:2]
        offsets = dict(zip(self.order[k:], key[1:]))
        slab = self.slab(offsets)
        if k:
            self.stage[slab, :] = self.value(k, offsets).astype(BF16)
        self.copies[key] = self.links.put(
            self.stage.at[slab], self.slots.at[self.slot[key]], rows=self.place({self.order[k]: i})
        )

    def value(self, k, offsets):
        total = self.stage[self.slab(offsets), :].astype(F32)
        for j in range(k):
            later = tuple(offsets.get(axis, 0) for axis in self.order[j + 1 :])
            for i in range(1, self.size[self.order[j]]):
                key = (j, i) + later
                self.copies[key].wait_recv()
                total = total + self.slots[self.slot[key]].astype(F32)
        return total

    def ready(self, low, high):
        offsets = dict(l=low, h=high)
        for x in range(self.size["x"] - 1, -1, -1):
            offsets["x"] = x
            key = (0,) + tuple(offsets[axis] for axis in self.order)
            if key[1]:
                self.send(key)

    def advance(self, count=1):
        for _ in range(min(count, len(self.todo))):
            self.send(self.todo.pop(0))

    def total(self):
        self.advance(len(self.todo))
        value = self.value(3, {})
        for copy in self.copies.values():
            copy.wait_send()
        return value


def weight_sums(left, right, sums, hold):
    first, later = sums[0][0], []
    rows = first.links.plan["X"] * first.slots.shape[1]
    for low in (1, 0):
        for high in range(first.size["h"] - 1, -1, -1):
            group = at(first.place(dict(l=low, h=high)) // first.size["x"] * rows, rows)
            product = dot(left[:, group], right[...], TN).astype(BF16)
            for one, cols in sums:
                one.stage[group, :] = product[:, cols]
            for one, _ in sums:
                if low < hold.get(one, 0):
                    later.append(functools.partial(one.ready, low, high))
                else:
                    one.ready(low, high)
    return later


class Doubling:
    def __init__(self, links, block, out, got):
        self.links, self.block, self.out, self.got, self.step = links, block, out, got, 0

    def begin(self):
        step, rows = self.step, self.links.rows
        self.out[step] = self.block[...]
        bit = 1 << (self.out.shape[0] - 1 - step)
        partner = rows + bit - 2 * bit * lax.rem(rows // bit, 2)
        self.copy = self.links.put(self.out.at[step], self.got.at[step], rows=partner)

    def end(self):
        self.copy.wait()
        self.block[...] = self.block[...] + self.got[self.step]
        self.step += 1


def names(plan):
    n, length, d, t, c, f = (plan[k] for k in ("n", "L", "D", "T", "C", "F"))
    far = plan["Y"] - 1
    z, rw = plan["Z"], plan["RW"]
    grid = (length, d)
    out = [("tok", grid, BF16), ("h1", grid, BF16), ("cot", grid, BF16), ("wout", (d, d), BF16)]
    out += [("attn", grid, BF16), ("h2", grid, BF16), ("act", (length, f), BF16), ("gpre", (length, f), BF16)]
    out += [("wqkv", (d, 3 * c), BF16), ("wup", (d, f), BF16), ("wdn", (d, f), BF16)]
    out += [("qkv", (length, 3 * c), BF16), ("gbr", grid, BF16)]
    out += [("ck", (CTX, c), BF16), ("cv", (CTX, c), BF16), ("gck", (CTX, c), F32), ("gcv", (CTX, c), F32)]
    out += [("lse", (c // HEAD, length, 1), F32), ("xs", (BLK, c), F32), ("gx", (BLK, c), F32)]
    out += [("keep", (CTX + 1, plan["NS"], c), F32), ("ak", (BLK, c), F32), ("av", (BLK, c), F32)]
    out += [("do", (BLK, c), BF16), ("r2own", (t, d), F32), ("p", (BLK, d), F32)]
    out += [("acc", (t, d), F32), ("ffn", (t, d), F32)]
    for s in ("a", "b"):
        out += [(s + part, (far, t, d), BF16) for part in ("_mo", "_mi", "_fo", "_fi")]
        out += [(s + part, (t, d), BF16) for part in ("_no", "_ni")]
    out += [("stage", (d, f), BF16), ("ostage", (d, c), BF16)]
    for s, w in (("up", f), ("dn", f), ("qk", 2 * c), ("va", c), ("ou", c)):
        out += [(s + "_slots", (plan["R"] - 1, rw, w), BF16)]
    steps = plan["R"].bit_length() - 1
    block = (plan["SM"], c)
    out += [("small", block, F32), ("smallin", (steps,) + block, F32), ("smallout", (steps,) + block, F32)]
    out += [("fx", (plan["X"], 8, d), F32), ("fz", (z, 8, d), F32), ("fc", (n, 8, d), F32)]
    return out


INPUTS = (
    "tokens", "cotangent", "segments", "w_query", "w_key", "w_value", "w_out", "w_up", "up_bias", "w_down",
    "down_bias", "norm1_gain", "norm1_bias", "norm2_gain", "norm2_bias", "decay_rates", "input_mix",
    "key_mix", "value_mix", "key_skip", "value_skip",
)
LARGE = (
    "tokens", "cotangent", "w_query", "w_key", "w_value", "w_out", "w_up", "w_down",
)
STATES = ("decay_rates", "input_mix", "key_mix", "value_mix")


class Box:
    def __init__(self, **items):
        self.__dict__.update(items)


def colsum(value):
    return jnp.sum(value, axis=0, keepdims=True)


def layer_kernel(plan, *refs):
    i = Box(**dict(zip(INPUTS, refs[:21])))
    o_out, o_tok, o_w4, o_up, o_dn, o_small, o_last = refs[21:28]
    scratch = refs[28:]
    s = Box(**dict(zip([x[0] for x in names(plan)], scratch)))
    links = Links(plan, scratch[-2], scratch[-1])
    n, length, d, t, c, f = (plan[k] for k in ("n", "L", "D", "T", "C", "F"))
    far = range(1, plan["Y"])
    here, mate, core = links.chan, links.mate, links.core
    pair = 2 * t
    own_rows, own_cols = at(here * t, t), at(here * c, c)
    own_part, mate_part = at(core * t, t), at((1 - core) * t, t)
    rows_of = lambda owner: at(owner * t, t)
    chip_rows = lambda owner: at(owner // 2 * pair, pair)
    q_ref, k_ref, v_ref = (s.qkv.at[:, e * c : (e + 1) * c] for e in range(3))

    ready = links.enter()
    got_tok = links.load(i.tokens, s.tok.at[own_rows])
    got_out = links.load(i.w_out, s.wout.at[:, own_cols])
    got_w = [
        links.load(w, s.wqkv.at[:, e * c : (e + 1) * c])
        for e, w in enumerate((i.w_query, i.w_key, i.w_value))
    ]
    got_cot = links.load(i.cotangent, s.cot.at[own_rows])
    got_up, got_dn = links.load(i.w_up, s.wup), links.load(i.w_down, s.wdn)
    par = ssm_params(i.decay_rates, i.input_mix, i.key_mix, i.value_mix)
    got_tok.wait()
    got_out.wait()
    ready()
    out_gather = SlabGather(links, s.wout, c)
    tok_gather = Gather(links, lambda o: s.tok.at[rows_of(o)])
    out_gather.spread_x()

    def project(rows):
        hat, _ = normalize(s.tok[rows, :].astype(F32))
        s.h1[rows, :] = (hat * i.norm1_gain[...] + i.norm1_bias[...]).astype(BF16)
        s.qkv[rows, :] = dot(s.h1[rows, :], s.wqkv[...]).astype(BF16)

    for got in got_w:
        got.wait()
    project(own_rows)
    out_gather.spread_z()
    tok_gather.near.wait_recv()
    project(rows_of(mate))
    got_cot.wait()
    half = t // 2
    cot_views = [lambda o, e=e: s.cot.at[at(o * t + e * half, half)] for e in range(2)]
    tok_gather.forward()
    cot_gathers = [Gather(links, cot_views[0])]
    for j in far:
        project(rows_of(links.far(-j)))
    for j, copy in zip(far, tok_gather.passed):
        copy.wait_recv()
        project(rows_of(links.other(links.far(-j))))
    tok_gather.near.wait_send()
    for copy in tok_gather.passed + tok_gather.direct:
        copy.wait_send()

    def store(rows, head, value):
        s.attn[rows, at(here * c + head * HEAD, HEAD)] = value

    attn_gathers = []

    def attend(block):
        attn_forward(block, q_ref, k_ref, v_ref, s.ck, s.cv, i.segments, store, s.lse)
        attn_gathers.append(
            Gather(links, lambda o: s.attn.at[pl.ds(block * BLK, BLK), at(o * c, c)])
        )

    attend(0)
    s.xs[...] = s.h1[0:BLK, own_cols].astype(F32)
    skip_k, skip_v = i.key_skip[...], i.value_skip[...]
    e0 = ssm_forward(s.xs, i.segments, par, skip_k, skip_v, s.ck, s.cv, s.gck, s.gcv, s.keep)
    cot_gathers[0].forward()
    attend(1)
    cot_gathers.append(Gather(links, cot_views[1]))
    out_gather.forward()
    attn_gathers[0].forward()
    got_up.wait()
    got_dn.wait()
    out_gather.finish()

    wide = 512

    def loop(count, body):
        def step(e, carry):
            body(at(e * wide, wide))
            return carry

        lax.fori_loop(0, count // wide, step, 0)

    def feed(block):
        rows = pl.ds(block * BLK, BLK)

        def residual(cols):
            s.p[:, cols] = s.tok[rows, cols].astype(F32) + dot(s.attn[rows, :], s.wout[:, cols])

        loop(d, residual)
        hat, _ = normalize(s.p[...])
        s.h2[rows, :] = (hat * i.norm2_gain[...] + i.norm2_bias[...]).astype(BF16)

        @pl.when(here * t // BLK == block)
        def _():
            s.r2own[...] = s.p[at(lax.rem(here * t, BLK), t), :]

        def hidden(cols):
            v = dot(s.h2[rows, :], s.wup[:, cols]) + i.up_bias[:, cols]
            square = v * v
            part = 0.5 + 0.5 * jnp.tanh(v * (ROOT + (0.044715 * ROOT) * square))
            act = v * part
            s.act[rows, cols] = act.astype(BF16)
            slope = part + act * (1.0 - part) * (2.0 * ROOT + (0.26829 * ROOT) * square)
            s.gpre[rows, cols] = slope.astype(BF16)

        loop(f, hidden)

    attn_gathers[0].finish()
    feed(0)
    attn_gathers[1].forward()
    cot_gathers[1].forward()
    attn_gathers[1].finish()
    feed(1)
    for gather in cot_gathers:
        gather.finish()

    def rows_sum(k, stage, order):
        return RowScatter(links, stage, getattr(s, k + "_slots"), order)

    every = slice(None)
    down_sum = rows_sum("dn", s.stage, "xlh")
    weight_sums(s.cot, s.act, [(down_sum, every)], {})

    def slope_grad(owner):
        rows = chip_rows(owner)

        def part(cols):
            grad = dot(s.cot[rows, :], s.wdn[:, cols])
            s.gpre[rows, cols] = (grad * s.gpre[rows, cols].astype(F32)).astype(BF16)

        loop(f, part)

    def back(owner, source, weight):
        rows = chip_rows(owner)

        def part(cols):
            s.p[0:pair, cols] = dot(source[rows, :], weight[cols, :], NT)

        loop(d, part)

    def back_near(sums, source, weight, own):
        def part(cols):
            sums.near_out[:, cols] = dot(source[rows_of(mate), :], weight[cols, :], NT).astype(BF16)
            own[:, cols] = dot(source[own_rows, :], weight[cols, :], NT)

        loop(d, part)
        sums.send_near()

    scatter = lambda k: Scatter(links, *(getattr(s, k + x) for x in ("_mo", "_mi", "_fo", "_fi", "_no", "_ni")))
    grad2 = scatter("a")
    for j in far:
        slope_grad(links.far(j))
        back(links.far(j), s.gpre, s.wup)
        grad2.for_mate(j, s.p[mate_part, :])
        if j == plan["Y"] - 1:
            slope_grad(here)
            back_near(grad2, s.gpre, s.wup, s.acc)
        grad2.for_far(j, s.p[own_part, :])
        grad2.send_far(j, 2)
    ffn = scatter("b")
    for j in far:
        back(links.far(j), s.act, s.wdn)
        ffn.for_mate(j, s.p[mate_part, :])
        if j == plan["Y"] - 1:
            back_near(ffn, s.act, s.wdn, s.ffn)
        ffn.for_far(j, s.p[own_part, :])
    down_sum.advance()
    up_sum = rows_sum("up", s.act, "xlh")
    weight_sums(s.h2, s.gpre, [(up_sum, every)], {})

    base = 4 * plan["NS"] + 2
    bias_rows = f // c
    for e in range(bias_rows):
        s.small[base + e : base + e + 1, :] = colsum(s.gpre[:, e * c : (e + 1) * c].astype(F32))
    base += bias_rows

    def keep_vector(k, value):
        for e in range(n):
            s.small[base + k * n + e : base + k * n + e + 1, :] = value[:, e * c : (e + 1) * c]

    down_sum.advance()
    branch_gathers, norm2 = [], [jnp.zeros((1, d), F32)] * 3
    for e in range(2):
        rows = pl.ds(e * half, half)
        tile_rows = at(here * t + e * half, half)
        grad_hidden2 = grad2.total(s.acc[rows, :], e, 2)
        hat2, inv2 = normalize(s.r2own[rows, :])
        own_cot = s.cot[tile_rows, :].astype(F32)
        grad_resid2 = own_cot + norm_back(grad_hidden2, hat2, inv2, i.norm2_gain[...])
        s.acc[rows, :] = grad_resid2
        s.gbr[tile_rows, :] = grad_resid2.astype(BF16)
        branch_gathers.append(Gather(links, lambda o, e=e: s.gbr.at[at(o * t + e * half, half)]))
        sums = colsum(own_cot), colsum(grad_hidden2 * hat2), colsum(grad_hidden2)
        norm2 = [a + b for a, b in zip(norm2, sums)]
    for k in range(3):
        keep_vector(k, norm2[k])
    down_sum.advance(plan["R"])
    up_sum.advance()
    for gather in branch_gathers:
        gather.forward()
    for gather in branch_gathers:
        gather.finish()
    for j in far:
        ffn.send_far(j)
    up_sum.advance()
    out_sum = rows_sum("ou", s.ostage, "xlh")
    held = weight_sums(s.attn, s.gbr.at[:, own_cols], [(out_sum, every)], {out_sum: 2})

    def attend_back(block):
        s.do[...] = dot(s.gbr[block * BLK : (block + 1) * BLK, :], s.wout[own_cols, :], NT).astype(BF16)
        attn_backward(
            block, q_ref, k_ref, v_ref, s.ck, s.cv, i.segments, s.lse, s.do,
            q_ref, k_ref, v_ref, s.gck, s.gcv, s.ak, s.av,
        )

    attend_back(1)
    ssm_backward(s.xs, i.segments, par, skip_k, skip_v, s.gck, s.gcv, s.keep, e0, s.gx, s.small)
    doubling = Doubling(links, s.small, s.smallout, s.smallin)
    steps = plan["R"].bit_length() - 1
    doubling.begin()
    for send in held:
        send()
    up_sum.advance(plan["R"])
    attend_back(0)

    def input_back(owner):
        rows = chip_rows(owner)

        def part(cols):
            s.p[0:pair, cols] = dot(s.qkv[rows, :], s.wqkv[cols, :], NT)

        loop(d, part)

        @pl.when(owner // 2 * pair < BLK)
        def _():
            s.p[0:pair, own_cols] = s.p[0:pair, own_cols] + s.gx[rows, :].astype(BF16).astype(F32)

    def norm1_sums(owner, total):
        hat, _ = normalize(s.tok[chip_rows(owner), :].astype(F32))
        partial = s.p[0:pair, :]
        return [total[0] + colsum(partial * hat), total[1] + colsum(partial)]

    def spread(slots, own, targets):
        return [links.put(slots.at[own], slots.at[own], **target) for target in targets]

    def settle(hops, slots, count):
        for hop in hops:
            hop.wait()
        return sum([slots[e] for e in range(1, count)], slots[0])

    grad1 = scatter("a")
    qk_sum = rows_sum("qk", s.h2.at[:, 0 : 2 * c], "xlh")
    value_sum = rows_sum("va", s.h2.at[:, 2 * c : 3 * c], "lhx")
    norm1 = [jnp.zeros((1, d), F32)] * 2
    for j in far:
        input_back(links.far(j))
        grad1.for_mate(j, s.p[mate_part, :])
        if j == 1:
            doubling.end()
            doubling.begin()
            both = [(value_sum, slice(2 * c, 3 * c)), (qk_sum, slice(0, 2 * c))]
            held = weight_sums(s.h1, s.qkv, both, {qk_sum: 1})
        grad1.for_far(j, s.p[own_part, :])
        grad1.send_far(j)
        norm1 = norm1_sums(links.far(j), norm1)
    input_back(here)
    grad1.for_near(s.p[mate_part, :])
    norm1 = norm1_sums(here, norm1)
    s.fx[links.x, 0:1, :] = norm1[0]
    s.fx[links.x, 1:2, :] = norm1[1]
    s.fx[links.x, 2:8, :] = jnp.zeros((6, d), F32)

    group = [mate] + [links.far(j) for j in far] + [links.other(links.far(j)) for j in far]
    group = [{"chan": e} for e in group]
    hops = spread(s.fx, links.x, [{"rows": links.row_of(links.z, links.x + e)} for e in range(1, plan["X"])])
    for step in range(2, steps):
        doubling.end()
        doubling.begin()
    for send in held:
        send()
    value_sum.advance()
    out_sum.advance(2)
    s.fz[links.z] = settle(hops, s.fx, plan["X"])
    hops = spread(s.fz, links.z, [{"rows": links.row_of(links.z + e, links.x)} for e in range(1, plan["Z"])])
    doubling.end()
    o_small[here] = s.small[...]
    blocks = spread(o_small, here, group)
    qk_sum.advance()
    value_sum.advance()
    s.fc[here] = settle(hops, s.fz, plan["Z"])
    hops = spread(s.fc, here, group)
    qk_sum.advance()
    out_sum.advance(plan["R"])
    o_dn[...] = down_sum.total()
    o_out[...] = (s.r2own[...] + ffn.total(s.ffn[...]) + i.down_bias[...]).astype(BF16)
    o_up[...] = up_sum.total()
    qk_sum.advance(plan["R"])
    value_sum.advance(plan["R"])
    o_w4[:, 3 * c : 4 * c] = out_sum.total()

    hat1, inv1 = normalize(s.tok[own_rows, :].astype(F32))
    grad_hidden1 = grad1.total(s.p[own_part, :])
    o_tok[...] = (s.acc[...] + norm_back(grad_hidden1, hat1, inv1, i.norm1_gain[...])).astype(BF16)
    o_last[...] = settle(hops, s.fc, n)
    for copy in blocks:
        copy.wait()
    o_w4[:, 0 : 2 * c] = qk_sum.total()
    o_w4[:, 2 * c : 3 * c] = value_sum.total()


def finish_kernel(plan, *refs):
    out, tok, w4, up, dn, small, last = refs[:7]
    o_out, o_tok, o_q, o_k, o_v, o_o, o_up, o_ub, o_dn, o_db, o_g1, o_b1, o_g2, o_b2 = refs[7:21]
    o_dec, o_in, o_km, o_vm, o_ks, o_vs, sem = refs[21:]
    n, c, f, ns = (plan[k] for k in ("n", "C", "F", "NS"))
    moves = [(out, o_out), (tok, o_tok), (up, o_up), (dn, o_dn)]
    moves += [(w4.at[:, e * c : (e + 1) * c], o) for e, o in enumerate((o_q, o_k, o_v, o_o))]
    copies = [pltpu.make_async_copy(a, b, sem.at[e]) for e, (a, b) in enumerate(moves)]
    for copy in copies:
        copy.start()
    bias_rows = f // c
    base = 4 * ns + 2 + bias_rows
    for e in range(n):
        cols = slice(e * c, (e + 1) * c)
        for k, target in enumerate((o_dec, o_in, o_km, o_vm)):
            target[:, cols] = small[e, k * ns : (k + 1) * ns, :]
        o_ks[:, cols] = small[e, 4 * ns : 4 * ns + 1, :]
        o_vs[:, cols] = small[e, 4 * ns + 1 : 4 * ns + 2, :]
        for b in range(bias_rows):
            o_ub[:, e * f + b * c : e * f + (b + 1) * c] = small[e, 4 * ns + 2 + b : 4 * ns + 3 + b, :]
        for k, target in enumerate((o_db, o_g2, o_b2)):
            row = base + k * n + e
            target[:, cols] = sum([small[g, row : row + 1, :] for g in range(1, n)], small[0, row : row + 1, :])
    o_g1[...] = last[0:1, :]
    o_b1[...] = last[1:2, :]
    for copy in copies:
        copy.wait()


def shards(*args):
    a = dict(zip(INPUTS, args))
    n, r = lax.axis_size("chan"), lax.axis_size("rows")
    t, d = a["tokens"].shape
    c, f = a["w_query"].shape[1], a["w_up"].shape[1]
    ns = a["decay_rates"].shape[1]
    x = math.isqrt(r // 2)
    small = 4 * ns + 2 + f // c + 3 * n
    plan = dict(
        n=n, R=r, L=a["segments"].shape[1], D=d, T=t, C=c, F=f, NS=ns, Y=n // 2, X=x, Z=r // x,
        RW=d // r, SM=-(-small // 8) * 8,
    )
    shape = jax.ShapeDtypeStruct
    rw = d // r
    outs = [shape((t, d), BF16)] * 2 + [shape((rw, 4 * c), F32)] + [shape((rw, f), F32)] * 2
    outs += [shape((n, plan["SM"], c), F32), shape((8, d), F32)]
    for k in STATES:
        a[k] = a[k].T
    values = [v if v.ndim == 2 else v.reshape(1, -1) for v in (a[k] for k in INPUTS)]
    vmem, any_space = pl.BlockSpec(memory_space=pltpu.VMEM), pl.BlockSpec(memory_space=pl.ANY)
    sems = pltpu.SemaphoreType.DMA((plan_semaphores(plan),))
    got = pl.pallas_call(
        functools.partial(layer_kernel, plan),
        out_shape=outs,
        in_specs=[any_space if k in LARGE else vmem for k in INPUTS],
        out_specs=[vmem] * len(outs),
        scratch_shapes=[pltpu.VMEM(s, k) for _, s, k in names(plan)] + [sems, sems],
        compiler_params=pltpu.CompilerParams(
            collective_id=0, has_side_effects=True, vmem_limit_bytes=60 << 20
        ),
    )(*values)
    row, state, line = shape((1, d), F32), shape((ns, d), F32), shape((rw, c), F32)
    token = shape((t, d), BF16)
    wide = shape((rw, f), F32)
    outs = [token, token, line, line, line, line, wide, shape((1, n * f), F32), wide]
    outs += [row] * 5 + [state] * 4 + [row] * 2
    large = (0, 1, 2, 3, 4, 5, 6, 8)
    done = pl.pallas_call(
        functools.partial(finish_kernel, plan),
        out_shape=outs,
        in_specs=[vmem] * 7,
        out_specs=[any_space if e in large else vmem for e in range(len(outs))],
        scratch_shapes=[pltpu.SemaphoreType.DMA((len(large),))],
    )(*got)
    done = list(done)
    for e in range(len(done)):
        if 14 <= e < 18:
            done[e] = done[e].T
        elif e not in large:
            done[e] = done[e].reshape(-1)
    return tuple(done)


def plan_semaphores(plan):
    y, x, z = plan["Y"] - 1, plan["X"] - 1, plan["Z"]
    gathers = 6 + plan["L"] // BLK
    slabs = 1 + y * (2 + x + z)
    hops = x + z + plan["n"]
    rows = 5 * (plan["R"] - 1)
    return 12 + gathers * (2 * y + 1) + slabs + 3 * (2 * y + 1) + y + rows + plan["R"].bit_length() + hops


def solution(mesh):
    both, row, col = P(("rows", "chan"), None), P("rows", None), P(None, "chan")
    state = P("chan", None)
    in_specs = (
        both, both, row, col, col, col, col, col, P("chan"), col,
        P(), P(), P(), P(), P(), state, state, state, state, P("chan"), P("chan"),
    )
    grid = P("rows", "chan")
    out_specs = (both, both, grid, grid, grid, grid, grid, P(), grid) + (P(),) * 11
    return jax.shard_map(shards, mesh=mesh, in_specs=in_specs, out_specs=out_specs, check_vma=False)
```
